32 devices in a mesh: energy: 4 (over z), slab: 8 (over y, x, core).
Axes of the slice: x: 2, y: 2, z: 4, core: 2. Of those that a mesh axis runs over, the one named last changes fastest.
Arguments:
- pivots: bfloat16 [4, 8, 2, 1024, 1024], P('energy', 'slab')
- injection: bfloat16 [4, 8, 1024, 128], P('energy', 'slab'), may hold values from -3 to 3
- previous: bfloat16 [4, 8, 1024, 128], P('energy', 'slab'), may hold values from -6 to 6
- coupling: bfloat16 [8, 256, 256], P('slab'), may hold values from -0.375 to 0.375
- strength: float32 [4, 4], replicated, may hold values from 0.1 to 1
- block_start: int32 [4, 4], replicated, may hold values from 0 to 12, as said below
- block_count: int32 [4, 4], replicated, may hold values from 0 to 4, as said below
Outputs:
- panel_out: bfloat16 [4, 8, 1024, 128], P('energy', 'slab')
The draws below stay inside these ranges and needn't reach their ends.
Inputs may be any that keep to these rules, and one draw needn't show every extreme that they name: block_count[e, s] orbital blocks of partner s's panel feed energy e; in every draw some energy takes 4 blocks from every partner, and which one is drawn. block_start[e, s] + block_count[e, s] <= 16.
All inputs are finite; a program needn't handle non-finite values.
Results may differ from the reference program's by a relative error of at most 0.0057.
Values may be sent and summed in bfloat16 or wider, within the bound.
No kernel may reach another device: no remote copies, remote signals or barrier semaphores. Data moves between devices by JAX's collectives and lax.ppermute only.
A program may use at most 128 MiB of HBM per device.

```python
import math
import jax
import jax.numpy as jnp
from jax import lax

NORB = 1024
LAYER = 256
COLS = 64
NBLK = 16
CAP = 4
ENERGIES = 4
SLABS = 8


def link_tables(key):
    base_key = jax.random.fold_in(key, 811)
    key_count, key_start, key_busy = jax.random.split(base_key, 3)
    counts_table = jax.random.randint(key_count, (ENERGIES, ENERGIES), 0, CAP + 1)
    starts_table = jax.random.randint(key_start, (ENERGIES, ENERGIES), 0, NBLK - CAP + 1)
    busiest = jax.random.randint(key_busy, (), 0, ENERGIES)
    row_ids = jnp.arange(ENERGIES)[:, None]
    col_ids = jnp.arange(ENERGIES)[None, :]
    counts_table = jnp.where(row_ids == busiest, CAP, counts_table)
    starts_table = jnp.where((row_ids == busiest) & (col_ids == 0), NBLK - CAP, starts_table)
    return (starts_table.astype(jnp.int32), counts_table.astype(jnp.int32))


def draw_block_start(key, part):
    return link_tables(key)[0]


def draw_block_count(key, part):
    return link_tables(key)[1]


def draw_pivots(key, part):
    full_shape = (ENERGIES, SLABS, 2, NORB, NORB)
    noise_draw = jax.random.normal(key, full_shape, jnp.float32)
    noise_draw = noise_draw * (1.1 / math.sqrt(NORB))
    diag_mask = (lax.broadcasted_iota(jnp.int32, (NORB, NORB), 0) == lax.broadcasted_iota(jnp.int32, (NORB, NORB), 1)).astype(jnp.float32)
    diag_parts = jnp.array([0.5, -0.2], jnp.float32)[:, None, None] * diag_mask[None]
    return (noise_draw + diag_parts).astype(jnp.bfloat16)


def block_scale(own_key, extent, pieces, least, high):
    def one(axis_at, parts):
        steps = jax.random.uniform(jax.random.fold_in(jax.random.fold_in(own_key, 6), axis_at), (parts,), jnp.float32, least / len(pieces), high / len(pieces))
        return jnp.repeat(jnp.exp(steps), extent[axis_at] // parts).reshape((-1,) + (1,) * (len(extent) - axis_at - 1))

    gain = one(*pieces[0])
    for cut in pieces[1:]:
        gain = gain * one(*cut)
    return gain


def centred(rng, extent, spread, most, shards=(), kind=jnp.bfloat16):
    drawn = spread * jax.random.normal(rng, extent, jnp.float32)
    if shards:
        drawn = drawn * block_scale(rng, extent, shards, -0.22, 0.18)
    return jnp.clip(drawn, -most, most).astype(kind)


def setup_inputs(seed: int = 0) -> dict:
    splits = jax.random.split(jax.random.key(seed), 8)
    return {
        "pivots": draw_pivots(jax.random.fold_in(splits[7], 71), 0),
        "injection": centred(splits[1], (ENERGIES, SLABS, NORB, 2 * COLS), 0.5, 3.0, ((0, 4), (1, 8))),
        "previous": centred(splits[2], (ENERGIES, SLABS, NORB, 2 * COLS), 1.0, 6.0, ((0, 4), (1, 8))),
        "coupling": centred(splits[3], (SLABS, LAYER, LAYER), LAYER ** -0.5, 0.375, ((0, 8),)),
        "strength": jnp.clip(jnp.exp(jax.random.uniform(splits[4], (ENERGIES, ENERGIES), jnp.float32, math.log(0.1), math.log(1.0))), 0.1, 1.0),
        "block_start": draw_block_start(jax.random.fold_in(splits[7], 71), 0),
        "block_count": draw_block_count(jax.random.fold_in(splits[7], 71), 0),
    }


highest = lax.Precision.HIGHEST


def panel_product(matrix, panel_in):
    half_cols = panel_in.shape[1] // 2
    real_part = jnp.dot(matrix[0], panel_in, preferred_element_type=jnp.float32)
    imag_part = jnp.dot(matrix[1], panel_in, preferred_element_type=jnp.float32)
    return jnp.concatenate([real_part[:, :half_cols] - imag_part[:, half_cols:], real_part[:, half_cols:] + imag_part[:, :half_cols]], axis=1)


def map_apply(mapping, vector):
    half_cols = vector.shape[1] // 2
    real_part = jnp.dot(mapping[0], vector, precision=highest)
    imag_part = jnp.dot(mapping[1], vector, precision=highest)
    return jnp.concatenate([real_part[:, :half_cols] - imag_part[:, half_cols:], real_part[:, half_cols:] + imag_part[:, :half_cols]], axis=1)


def reference(pivots, injection, previous, coupling, strength, block_start, block_count):
    block_rows = NORB // NBLK
    prev_blocks = previous.astype(jnp.float32).reshape(ENERGIES, SLABS, NBLK, block_rows, 2 * COLS)
    coupling_wide = coupling.astype(jnp.float32)

    def one_energy(energy_args):
        green_all, inject_all, strength_row, start_row, count_row = energy_args
        block_ids = jnp.arange(NBLK, dtype=jnp.int32)[None, :]
        taken = (block_ids >= start_row[:, None]) & (block_ids < (start_row + count_row)[:, None])
        weights = jnp.where(taken, strength_row[:, None], jnp.float32(0.0)).astype(jnp.float32)
        scattered = jnp.einsum('ek,eskrq->skrq', weights, prev_blocks, precision=highest).reshape(SLABS, NORB, 2 * COLS)
        right_side = (inject_all.astype(jnp.float32) + scattered).astype(jnp.bfloat16)

        def forward_step(carry_vec, slab_args):
            green, source_slab, coupling_block = slab_args
            direct = panel_product(green, source_slab)
            forward = direct + panel_product(green[:, :, :LAYER], carry_vec.astype(jnp.bfloat16))
            link_map = jnp.einsum('vw,kvu->kwu', coupling_block.astype(jnp.float32), green[:, NORB - LAYER:, :LAYER].astype(jnp.float32), precision=highest)
            head_vec = jnp.dot(coupling_block.astype(jnp.float32).T, direct[NORB - LAYER:], precision=highest)
            return head_vec + map_apply(link_map, carry_vec), forward

        zero_vec = jnp.zeros((LAYER, 2 * COLS), jnp.float32)
        unused_vec, forwards = lax.scan(forward_step, zero_vec, (green_all, right_side, coupling))

        def backward_step(carry_vec, slab_args):
            green, forward, coupling_block = slab_args
            coupling_f = coupling_block.astype(jnp.float32)
            outgoing = jnp.dot(coupling_f, carry_vec, precision=highest).astype(jnp.bfloat16)
            panel_slab = (forward + panel_product(green[:, :, NORB - LAYER:], outgoing)).astype(jnp.bfloat16)
            back_map = jnp.einsum('kwv,vu->kwu', green[:, :LAYER, NORB - LAYER:].astype(jnp.float32), coupling_f, precision=highest)
            return forward[:LAYER] + map_apply(back_map, carry_vec), panel_slab

        unused_back, panels = lax.scan(backward_step, zero_vec, (green_all, forwards, coupling), reverse=True)
        return panels

    return lax.map(one_energy, (pivots, injection, strength, block_start, block_count))
```

```python
import jax
import jax.numpy as jnp
from jax import lax
from jax.sharding import PartitionSpec as P

NBLK = 16
CAP = 4
bf16 = jnp.bfloat16
f32 = jnp.float32


def swapped(block, axis, mask):
    count = lax.axis_size(axis)
    return lax.ppermute(block, axis, [(i, i ^ mask) for i in range(count)])


def turned(v):
    half = v.shape[1] // 2
    return jnp.concatenate([-v[:, half:], v[:, :half]], axis=1)


def doubled(v):
    return jnp.concatenate([v, turned(v)], axis=0)


def applied(wide, v):
    return jnp.dot(wide, doubled(v), preferred_element_type=f32)


def panel_product(real, imag, v):
    return jnp.dot(real, v, preferred_element_type=f32) + jnp.dot(
        imag, turned(v), preferred_element_type=f32
    )


def body(pivots, injection, previous, coupling, strength, block_start, block_count):
    green = pivots[0, 0]
    norb = green.shape[1]
    layer = coupling.shape[1]
    width = injection.shape[3]
    rows = norb // NBLK
    span = rows * CAP
    coup = coupling[0]
    energies = lax.axis_size("energy")
    slabs = lax.axis_size("slab")
    levels = slabs.bit_length() - 1
    me = lax.axis_index("energy")
    at = lax.axis_index("slab")
    bits = [((at >> k) & 1) == 1 for k in range(levels)]
    low = slice(norb - layer, norb)

    panel = previous[0, 0]
    received = [None] * energies
    for mask in range(energies - 1, 0, -1):
        first = block_start[me ^ mask, me] * rows
        piece = lax.dynamic_slice(panel, (first, 0), (span, width))
        received[mask] = swapped(piece, "energy", mask)
    first = block_start[me, me] * rows
    received[0] = lax.dynamic_slice(panel, (first, 0), (span, width))

    forward_map = jnp.concatenate(
        [
            jnp.dot(coup.T, green[k, low, :layer], preferred_element_type=f32).astype(bf16)
            for k in range(2)
        ],
        axis=1,
    )
    backward_map = jnp.concatenate(
        [
            jnp.dot(green[k, :layer, low], coup, preferred_element_type=f32).astype(bf16)
            for k in range(2)
        ],
        axis=1,
    )

    groups = []
    own = (forward_map, backward_map)
    prefix = [None, None]
    for level in range(levels):
        last = level == levels - 1
        theirs = (None, None)
        if level == 0:
            both = swapped(jnp.concatenate(own, axis=0), "slab", 1)
            theirs = (both[:layer], both[layer:])
        elif not last:
            mine = jnp.where(bits[0], own[1], own[0])
            near = swapped(mine, "slab", 1 << level)
            far = swapped(near, "slab", 1)
            theirs = (jnp.where(bits[0], far, near), jnp.where(bits[0], near, far))
        plan, grown = [], []
        for way in range(2):
            after = bits[level] if way == 0 else ~bits[level]
            later = None if last else jnp.where(after, own[way], theirs[way])
            plan.append((after, prefix[way], later))
            if last:
                continue
            earlier = jnp.where(after, theirs[way], own[way])
            grown.append(applied(later, earlier).astype(bf16) if level + 2 < levels else None)
            if level == 0:
                unit = jnp.concatenate(
                    [jnp.eye(layer, dtype=bf16), jnp.zeros((layer, layer), bf16)], axis=1
                )
                prefix[way] = jnp.where(after, theirs[way], unit)
            else:
                prefix[way] = jnp.where(
                    after, applied(prefix[way], theirs[way]).astype(bf16), prefix[way]
                )
        own = tuple(grown)
        groups.append(plan)

    def scan(vector, way):
        total = vector.astype(bf16)
        reach = None
        for level in range(levels):
            after, before, later = groups[level][way]
            last = level == levels - 1
            if last:
                half = slabs // 2
                if way == 0:
                    route = [(i, i + half) for i in range(half)]
                else:
                    route = [(i + half, i) for i in range(half)]
                other = lax.ppermute(total, "slab", route)
            else:
                other = swapped(total, "slab", 1 << level)
            if level == 0:
                reach = jnp.where(after, other, jnp.zeros_like(other)).astype(f32)
            else:
                reach = reach + jnp.where(after, applied(before, other), 0.0)
            if not last:
                earlier = jnp.where(after, other, total)
                latest = jnp.where(after, total, other)
                total = (applied(later, earlier) + latest.astype(f32)).astype(bf16)
        return reach

    scattered = injection[0, 0].astype(f32)
    slot = lax.broadcasted_iota(jnp.int32, (span, 1), 0) // rows
    for mask in range(energies):
        s = me ^ mask
        weight = jnp.where(slot < block_count[me, s], strength[me, s], 0.0)
        first = block_start[me, s] * rows
        held = lax.dynamic_slice(scattered, (first, 0), (span, width))
        scattered = lax.dynamic_update_slice(
            scattered, held + weight * received[mask].astype(f32), (first, 0)
        )
    source = scattered.astype(bf16)

    direct_low = panel_product(green[0, low], green[1, low], source)
    sent = jnp.dot(coup.T, direct_low.astype(bf16), preferred_element_type=f32)
    incoming = scan(sent, 0).astype(bf16)

    direct_top = panel_product(green[0, :layer], green[1, :layer], source)
    forward_top = direct_top + panel_product(green[0, :layer, :layer], green[1, :layer, :layer], incoming)
    coming_back = scan(forward_top, 1)

    direct_rest = panel_product(green[0, layer:], green[1, layer:], source)
    forward_rest = direct_rest + panel_product(green[0, layer:, :layer], green[1, layer:, :layer], incoming)
    outgoing = jnp.dot(coup, coming_back.astype(bf16), preferred_element_type=f32).astype(bf16)
    out = jnp.concatenate([forward_top, forward_rest], axis=0) + panel_product(
        green[0, :, low], green[1, :, low], outgoing
    )
    return out.astype(bf16)[None, None]


def solution(mesh):
    in_specs = (
        P("energy", "slab", None, None, None),
        P("energy", "slab", None, None),
        P("energy", "slab", None, None),
        P("slab", None, None),
        P(),
        P(),
        P(),
    )
    out_specs = P("energy", "slab", None, None)
    return jax.shard_map(body, mesh=mesh, in_specs=in_specs, out_specs=out_specs, check_vma=False)
```

```python
import math

import jax
import jax.numpy as jnp
from jax import lax
from jax.experimental import pallas as pl
from jax.experimental.pallas import tpu as pltpu
from jax.sharding import PartitionSpec as P


NBLK = 16
CAP = 4
bf16 = jnp.bfloat16
f32 = jnp.float32
VMEM = pltpu.VMEM


def swapped(block, axis, mask):
    count = lax.axis_size(axis)
    return lax.ppermute(block, axis, [(i, i ^ mask) for i in range(count)])


def dot(a, b):
    return jnp.dot(a, b, preferred_element_type=f32)


def turned(v):
    half = v.shape[1] // 2
    if half % 128 == 0:
        return jnp.concatenate([-v[:, half:], v[:, :half]], axis=1)
    lane = lax.broadcasted_iota(jnp.int32, v.shape, 1)
    moved = pltpu.roll(v, half, 1)
    return jnp.where(lane < half, -moved, moved)


def applied(real, imag, v):
    v = v.astype(f32)
    return dot(real, v.astype(bf16)) + dot(imag, turned(v).astype(bf16))


def mapped(wide, v):
    side = wide.shape[1] // 2
    return applied(wide[:, :side], wide[:, side:], v)


def fine(real, v):
    high = v.astype(bf16)
    return dot(real, high) + dot(real, (v - high.astype(f32)).astype(bf16))


def place(k):
    return ((lax.axis_index("slab") >> k) & 1) == 1


def call(kernel, outs, args, flops, spaces=None, scratch=()):
    spaces = spaces or {}
    specs = [pl.BlockSpec(memory_space=spaces.get(i, VMEM)) for i in range(len(args))]
    moved = sum(a.size * a.dtype.itemsize for a in args)
    kept = sum(math.prod(s) * jnp.dtype(t).itemsize for s, t in outs)
    kept += sum(a.size * a.dtype.itemsize for i, a in enumerate(args) if i not in spaces)
    shapes = [jax.ShapeDtypeStruct(s, t) for s, t in outs]
    return pl.pallas_call(
        kernel,
        out_shape=shapes,
        in_specs=specs,
        out_specs=[pl.BlockSpec(memory_space=VMEM)] * len(shapes),
        scratch_shapes=list(scratch),
        compiler_params=pltpu.CompilerParams(vmem_limit_bytes=kept + (4 << 20)),
        cost_estimate=pl.CostEstimate(
            flops=flops, bytes_accessed=moved, transcendentals=0
        ),
    )(*args)


def body(pivots, injection, previous, coupling, strength, block_start, block_count):
    green = pivots[0, 0]
    norb = green.shape[1]
    layer = coupling.shape[1]
    width = injection.shape[3]
    rows = norb // NBLK
    span = rows * CAP
    coup = coupling[0]
    panel = previous[0, 0]
    energies = lax.axis_size("energy")
    slabs = lax.axis_size("slab")
    levels = slabs.bit_length() - 1
    low = norb - layer
    SMEM = pltpu.SMEM

    def pick(start_ref, panel_ref, *outs):
        me = lax.axis_index("energy")
        for k in range(energies - 1):
            first = pl.multiple_of(start_ref[me ^ (k + 1), me] * rows, rows)
            outs[k][...] = panel_ref[pl.ds(first, span)]

    pieces = call(
        pick, [((span, width), bf16)] * (energies - 1), (block_start, panel), 0, {0: SMEM}
    )
    received = [None] * (energies - 1)
    for mask in range(energies - 1, 0, -1):
        received[mask - 1] = swapped(pieces[mask - 1], "energy", mask)

    def own_maps(green_ref, coup_ref, maps_ref, turn_ref):
        c = coup_ref[...]
        ct = c.astype(f32).T.astype(bf16)
        turn_ref[...] = ct
        for k in range(2):
            part = slice(k * layer, (k + 1) * layer)
            maps_ref[:layer, part] = dot(ct, green_ref[k, low:, :layer]).astype(bf16)
            maps_ref[layer:, part] = dot(green_ref[k, :layer, low:], c).astype(bf16)

    maps, coup_t = call(
        own_maps,
        [((2 * layer, 2 * layer), bf16), ((layer, layer), bf16)],
        (green, coup),
        8 * layer**3,
    )
    held = green

    ways = (slice(0, layer), slice(layer, 2 * layer))
    wide = (2 * layer, 2 * layer)
    laters, befores = [], [None]
    own = maps
    for level in range(levels - 1):
        grow = level + 2 < levels

        def group(*refs, level=level, grow=grow):
            refs = list(refs)
            mine = refs.pop(0)
            if level == 0:
                near = refs.pop(0)
                theirs = [near[w] for w in ways]
            else:
                near, far, old = refs.pop(0), refs.pop(0), refs.pop(0)
                first = place(0)
                a, b = near[...], far[...]
                theirs = [jnp.where(first, b, a), jnp.where(first, a, b)]
            later_ref, before_ref = refs.pop(0), refs.pop(0)
            if grow:
                total_ref, send_ref = refs
            grown = []
            for way in range(2):
                after = place(level) if way == 0 else ~place(level)
                other, self = theirs[way], mine[ways[way]]
                later = jnp.where(after, self, other)
                later_ref[ways[way]] = later
                if level == 0:
                    row = lax.broadcasted_iota(jnp.int32, (layer, 2 * layer), 0)
                    col = lax.broadcasted_iota(jnp.int32, (layer, 2 * layer), 1)
                    before = (row == col).astype(f32).astype(bf16)
                    before_ref[ways[way]] = jnp.where(after, other, before)
                else:
                    before = old[ways[way]]
                    before_ref[ways[way]] = jnp.where(
                        after, mapped(before, other).astype(bf16), before
                    )
                if grow:
                    earlier = jnp.where(after, other, self)
                    grown.append(mapped(later, earlier).astype(bf16))
                    total_ref[ways[way]] = grown[way]
            if grow:
                send_ref[...] = jnp.where(place(0), grown[1], grown[0])

        if level == 0:
            args = (own, swapped(own, "slab", 1))
        else:
            near = swapped(send, "slab", 1 << level)
            args = (own, near, swapped(near, "slab", 1), befores[-1])
        outs = [(wide, bf16), (wide, bf16)]
        if grow:
            outs += [(wide, bf16), ((layer, 2 * layer), bf16)]
        res = call(group, outs, args, 32 * layer**3)
        laters.append(res[0])
        befores.append(res[1])
        if grow:
            own, send = res[2], res[3]

    def reach_step(level, way, reach_ref, before_ref, other):
        after = place(level) if way == 0 else ~place(level)
        if level == 0:
            return jnp.where(after, other, jnp.zeros_like(other))
        more = mapped(before_ref[ways[way]], other)
        return reach_ref[...] + jnp.where(after, more, jnp.zeros_like(more))

    def scan(vector, way):
        total, reach, sent = vector, None, vector
        for level in range(levels - 1):
            other = swapped(sent, "slab", 1 << level)

            def step(*refs, level=level):
                refs = list(refs)
                mine, other_ref, later = refs[:3]
                total_ref, sent_ref, reached = refs[-3:]
                after = place(level) if way == 0 else ~place(level)
                theirs = other_ref[...].astype(f32)
                self = mine[...]
                earlier = jnp.where(after, theirs, self)
                latest = jnp.where(after, self, theirs)
                new = mapped(later[ways[way]], earlier) + latest
                total_ref[...] = new
                sent_ref[...] = new.astype(bf16)
                before = refs[3] if level else None
                so_far = refs[4] if level else None
                reached[...] = reach_step(level, way, so_far, before, theirs)

            args = (total, other, laters[level])
            if level:
                args += (befores[level], reach)
            size = (layer, width)
            total, sent, reach = call(
                step, [(size, f32), (size, bf16), (size, f32)], args, 16 * layer * layer * width
            )
        half = slabs // 2
        if way == 0:
            route = [(i, i + half) for i in range(half)]
        else:
            route = [(i + half, i) for i in range(half)]
        return lax.ppermute(sent, "slab", route), reach

    def load(inj_ref, panel_ref, start_ref, count_ref, strength_ref, held_ref, turn_ref, *refs):
        got, (source_ref, spun_ref, low_ref, sent_ref, acc) = refs[:-5], refs[-5:]
        me = lax.axis_index("energy")
        acc[...] = inj_ref[...].astype(f32)
        row = lax.broadcasted_iota(jnp.int32, (span, width), 0)
        for k in range(energies):
            s = me ^ k
            first = pl.multiple_of(start_ref[me, s] * rows, rows)
            taken = panel_ref[pl.ds(first, span)] if k == 0 else got[k - 1][...]
            term = jnp.where(
                row < count_ref[me, s] * rows, taken.astype(f32) * strength_ref[me, s], 0.0
            )
            acc[pl.ds(first, span)] = acc[pl.ds(first, span)] + term
        source = acc[...].astype(bf16)
        spun = turned(source.astype(f32)).astype(bf16)
        source_ref[...] = source
        spun_ref[...] = spun
        direct = dot(held_ref[0, low:], source) + dot(held_ref[1, low:], spun)
        low_ref[...] = direct
        sent_ref[...] = fine(turn_ref[...], direct)

    source, spun, direct_low, sent = call(
        load,
        [((norb, width), bf16)] * 2 + [((layer, width), f32)] * 2,
        (injection[0, 0], panel, block_start, block_count, strength, held, coup_t, *received),
        4 * layer * norb * width,
        {2: SMEM, 3: SMEM, 4: SMEM},
        [pltpu.VMEM((norb, width), f32)],
    )
    arrived, reach = scan(sent, 0)

    def direct_step(held_ref, source_ref, spun_ref, out_ref):
        out_ref[...] = dot(held_ref[0, :low], source_ref[...]) + dot(
            held_ref[1, :low], spun_ref[...]
        )

    (direct,) = call(
        direct_step, [((low, width), f32)], (held, source, spun), 4 * low * norb * width
    )

    def turn_round(other_ref, reach_ref, before_ref, held_ref, direct_ref, inc_ref, top_ref):
        incoming = reach_step(levels - 1, 0, reach_ref, before_ref, other_ref[...]).astype(bf16)
        inc_ref[...] = incoming
        top_ref[...] = direct_ref[:layer] + applied(
            held_ref[0, :layer, :layer], held_ref[1, :layer, :layer], incoming
        )

    incoming, forward_top = call(
        turn_round,
        [((layer, width), bf16), ((layer, width), f32)],
        (arrived, reach, befores[levels - 1], held, direct),
        16 * layer * layer * width,
    )
    arrived, reach = scan(forward_top, 1)

    def forward_step(held_ref, inc_ref, direct_ref, low_ref, out_ref):
        incoming = inc_ref[...]
        spun = turned(incoming.astype(f32)).astype(bf16)
        more = dot(held_ref[0, :, :layer], incoming) + dot(held_ref[1, :, :layer], spun)
        out_ref[:low] = direct_ref[...] + more[:low]
        out_ref[low:] = low_ref[...] + more[low:]

    (forward,) = call(
        forward_step,
        [((norb, width), f32)],
        (held, incoming, direct, direct_low),
        8 * norb * layer * width,
    )

    def finish(other_ref, reach_ref, before_ref, held_ref, coup_ref, forward_ref, out_ref):
        back = reach_step(levels - 1, 1, reach_ref, before_ref, other_ref[...])
        outgoing = fine(coup_ref[...], back).astype(bf16)
        spun = turned(outgoing.astype(f32)).astype(bf16)
        out_ref[...] = (
            forward_ref[...]
            + dot(held_ref[0, :, low:], outgoing)
            + dot(held_ref[1, :, low:], spun)
        ).astype(bf16)

    (out,) = call(
        finish,
        [((norb, width), bf16)],
        (arrived, reach, befores[levels - 1], held, coup, forward),
        8 * norb * layer * width,
    )
    return out[None, None]


def solution(mesh):
    in_specs = (
        P("energy", "slab", None, None, None),
        P("energy", "slab", None, None),
        P("energy", "slab", None, None),
        P("slab", None, None),
        P(),
        P(),
        P(),
    )
    out_specs = P("energy", "slab", None, None)
    return jax.shard_map(body, mesh=mesh, in_specs=in_specs, out_specs=out_specs, check_vma=False)
```

```python
import math

import jax
import jax.numpy as jnp
from jax import lax
from jax.experimental import pallas as pl
from jax.experimental.pallas import tpu as pltpu
from jax.sharding import PartitionSpec as P


NBLK = 16
CAP = 4
VMEM_BYTES = 67043328
bf16 = jnp.bfloat16
f32 = jnp.float32
VMEM = pltpu.VMEM


def swapped(block, axis, mask):
    count = lax.axis_size(axis)
    return lax.ppermute(block, axis, [(i, i ^ mask) for i in range(count)])


def dot(a, b):
    return jnp.dot(a, b, preferred_element_type=f32)


def turned(v):
    half = v.shape[1] // 2
    if half % 128 == 0:
        return jnp.concatenate([-v[:, half:], v[:, :half]], axis=1)
    lane = lax.broadcasted_iota(jnp.int32, v.shape, 1)
    moved = pltpu.roll(v, half, 1)
    return jnp.where(lane < half, -moved, moved)


def applied(real, imag, v):
    v = v.astype(f32)
    return dot(real, v.astype(bf16)) + dot(imag, turned(v).astype(bf16))


def mapped(wide, v):
    side = wide.shape[1] // 2
    return applied(wide[:, :side], wide[:, side:], v)


def fine(real, v):
    high = v.astype(bf16)
    return dot(real, high) + dot(real, (v - high.astype(f32)).astype(bf16))


def place(k):
    return ((lax.axis_index("slab") >> k) & 1) == 1


def call(kernel, outs, args, flops, spaces=None, scratch=(), out_space=VMEM, spare=None):
    spaces = spaces or {}
    specs = [pl.BlockSpec(memory_space=spaces.get(i, VMEM)) for i in range(len(args))]
    moved = sum(a.size * a.dtype.itemsize for a in args)
    kept = sum(math.prod(s) * jnp.dtype(t).itemsize for s, t in outs)
    kept += sum(a.size * a.dtype.itemsize for i, a in enumerate(args) if i not in spaces)
    limit = kept + (4 << 20) if spare is None else VMEM_BYTES - spare
    shapes = [jax.ShapeDtypeStruct(s, t) for s, t in outs]
    return pl.pallas_call(
        kernel,
        out_shape=shapes,
        in_specs=specs,
        out_specs=[pl.BlockSpec(memory_space=out_space)] * len(shapes),
        scratch_shapes=list(scratch),
        compiler_params=pltpu.CompilerParams(vmem_limit_bytes=limit),
        cost_estimate=pl.CostEstimate(
            flops=flops, bytes_accessed=moved, transcendentals=0
        ),
    )(*args)


def body(pivots, injection, previous, coupling, strength, block_start, block_count):
    green = pivots[0, 0]
    norb = green.shape[1]
    layer = coupling.shape[1]
    width = injection.shape[3]
    rows = norb // NBLK
    span = rows * CAP
    far_green = pltpu.with_memory_space_constraint(green, pltpu.HBM)
    coup = coupling[0]
    far_coup = pltpu.with_memory_space_constraint(coup, pltpu.HBM)
    panel = previous[0, 0]
    energies = lax.axis_size("energy")
    slabs = lax.axis_size("slab")
    levels = slabs.bit_length() - 1
    low = norb - layer
    SMEM = pltpu.SMEM

    def own_maps(green_ref, coup_ref, maps_ref, turn_ref, corner, near, sem, sem_c):
        spots = ((pl.ds(low, layer), pl.ds(0, layer)), (pl.ds(0, layer), pl.ds(low, layer)))
        copies = [
            [pltpu.make_async_copy(green_ref.at[k, r, c], corner.at[i, k], sem.at[i, k]) for k in range(2)]
            for i, (r, c) in enumerate(spots)
        ]
        first = pltpu.make_async_copy(coup_ref, near, sem_c)
        first.start()
        for pair in copies:
            for copy in pair:
                copy.start()
        first.wait()
        c = near[...]
        ct = c.astype(f32).T.astype(bf16)
        turn_ref[...] = ct
        for k in range(2):
            copies[0][k].wait()
            maps_ref[:layer, k * layer : (k + 1) * layer] = dot(ct, corner[0, k]).astype(bf16)
        for k in range(2):
            copies[1][k].wait()
            maps_ref[layer:, k * layer : (k + 1) * layer] = dot(corner[1, k], c).astype(bf16)

    maps, coup_t = call(
        own_maps,
        [((2 * layer, 2 * layer), bf16), ((layer, layer), bf16)],
        (far_green, far_coup),
        8 * layer**3,
        {0: pltpu.HBM, 1: pltpu.HBM},
        [
            pltpu.VMEM((2, 2, layer, layer), bf16),
            pltpu.VMEM((layer, layer), bf16),
            pltpu.SemaphoreType.DMA((2, 2)),
            pltpu.SemaphoreType.DMA,
        ],
    )

    def pick(start_ref, panel_ref, *outs):
        me = lax.axis_index("energy")
        for k in range(energies - 1):
            first = pl.multiple_of(start_ref[me ^ (k + 1), me] * rows, rows)
            outs[k][...] = panel_ref[pl.ds(first, span)]

    pieces = call(
        pick, [((span, width), bf16)] * (energies - 1), (block_start, panel), 0, {0: SMEM}
    )
    received = [None] * (energies - 1)
    for mask in range(energies - 1, 0, -1):
        received[mask - 1] = swapped(pieces[mask - 1], "energy", mask)

    held = green

    def fetch(green_ref, hint_ref, held_ref, sem):
        parts = [(k, pl.ds(i * layer, layer)) for k in range(2) for i in range(norb // layer)]
        copies = [
            pltpu.make_async_copy(green_ref.at[k, r], held_ref.at[k, r], sem.at[i])
            for i, (k, r) in enumerate(parts)
        ]
        for copy in copies:
            copy.start()
        for copy in copies:
            copy.wait()

    (held,) = call(
        fetch,
        [(green.shape, bf16)],
        (far_green, coup_t),
        0,
        {0: pltpu.HBM, 1: pl.ANY},
        [pltpu.SemaphoreType.DMA((2 * norb // layer,))],
    )

    ways = (slice(0, layer), slice(layer, 2 * layer))
    wide = (2 * layer, 2 * layer)
    laters, befores = [], [None]
    own = maps
    for level in range(levels - 1):
        grow = level + 2 < levels

        def group(*refs, level=level, grow=grow):
            refs = list(refs)
            mine = refs.pop(0)
            if level == 0:
                near = refs.pop(0)
                theirs = [near[w] for w in ways]
            else:
                near, far, old = refs.pop(0), refs.pop(0), refs.pop(0)
                first = place(0)
                a, b = near[...], far[...]
                theirs = [jnp.where(first, b, a), jnp.where(first, a, b)]
            later_ref, before_ref = refs.pop(0), refs.pop(0)
            if grow:
                total_ref, send_ref = refs
            grown = []
            for way in range(2):
                after = place(level) if way == 0 else ~place(level)
                other, self = theirs[way], mine[ways[way]]
                later = jnp.where(after, self, other)
                later_ref[ways[way]] = later
                if level == 0:
                    row = lax.broadcasted_iota(jnp.int32, (layer, 2 * layer), 0)
                    col = lax.broadcasted_iota(jnp.int32, (layer, 2 * layer), 1)
                    before = (row == col).astype(f32).astype(bf16)
                    before_ref[ways[way]] = jnp.where(after, other, before)
                else:
                    before = old[ways[way]]
                    before_ref[ways[way]] = jnp.where(
                        after, mapped(before, other).astype(bf16), before
                    )
                if grow:
                    earlier = jnp.where(after, other, self)
                    grown.append(mapped(later, earlier).astype(bf16))
                    total_ref[ways[way]] = grown[way]
            if grow:
                send_ref[...] = jnp.where(place(0), grown[1], grown[0])

        if level == 0:
            args = (own, swapped(own, "slab", 1))
        else:
            near = swapped(send, "slab", 1 << level)
            args = (own, near, swapped(near, "slab", 1), befores[-1])
        outs = [(wide, bf16), (wide, bf16)]
        if grow:
            outs += [(wide, bf16), ((layer, 2 * layer), bf16)]
        res = call(group, outs, args, 32 * layer**3)
        laters.append(res[0])
        befores.append(res[1])
        if grow:
            own, send = res[2], res[3]

    def reach_step(level, way, reach_ref, before_ref, other):
        after = place(level) if way == 0 else ~place(level)
        if level == 0:
            return jnp.where(after, other, jnp.zeros_like(other))
        more = mapped(before_ref[ways[way]], other)
        return reach_ref[...] + jnp.where(after, more, jnp.zeros_like(more))

    def scan(vector, way):
        total, reach, sent = vector, None, vector
        for level in range(levels - 1):
            other = swapped(sent, "slab", 1 << level)

            final = level == levels - 2

            def step(*refs, level=level, final=final):
                refs = list(refs)
                mine, other_ref, later = refs[:3]
                sent_ref, reached = refs[-2:]
                after = place(level) if way == 0 else ~place(level)
                theirs = other_ref[...].astype(f32)
                self = mine[...]
                earlier = jnp.where(after, theirs, self)
                latest = jnp.where(after, self, theirs)
                new = mapped(later[ways[way]], earlier) + latest
                sent_ref[...] = new.astype(bf16)
                if not final:
                    refs[-3][...] = new
                before = refs[3] if level else None
                so_far = refs[4] if level else None
                reached[...] = reach_step(level, way, so_far, before, theirs)

            args = (total, other, laters[level])
            if level:
                args += (befores[level], reach)
            size = (layer, width)
            res = call(
                step,
                [(size, f32)] * (not final) + [(size, bf16), (size, f32)],
                args,
                16 * layer * layer * width,
            )
            total, sent, reach = res if not final else [None] + list(res)
        return swapped(sent, "slab", slabs // 2), reach

    me = lax.axis_index("energy")
    row = lax.broadcasted_iota(jnp.int32, (span, width), 0)
    scattered = injection[0, 0].astype(f32)
    own_piece = lax.dynamic_slice(panel, (block_start[me, me] * rows, 0), (span, width))
    for k, piece in enumerate([own_piece] + received):
        s = me ^ k
        first = block_start[me, s] * rows
        term = jnp.where(
            row < block_count[me, s] * rows, piece.astype(f32) * strength[me, s], 0.0
        )
        so_far = lax.dynamic_slice(scattered, (first, 0), (span, width))
        scattered = lax.dynamic_update_slice(scattered, so_far + term, (first, 0))

    def load(sum_ref, held_ref, turn_ref, source_ref, spun_ref, low_ref, sent_ref):
        total = sum_ref[...]
        source = total.astype(bf16)
        spun = turned(source.astype(f32)).astype(bf16)
        source_ref[...] = source
        spun_ref[...] = spun
        direct = dot(held_ref[0, low:], source) + dot(held_ref[1, low:], spun)
        low_ref[...] = direct
        sent_ref[...] = fine(turn_ref[...], direct)

    source, spun, direct_low, sent = call(
        load,
        [((norb, width), bf16)] * 2 + [((layer, width), f32)] * 2,
        (scattered, held, coup_t),
        4 * layer * norb * width,
    )
    arrived, reach = scan(sent, 0)

    def direct_step(held_ref, source_ref, spun_ref, out_ref):
        out_ref[...] = dot(held_ref[0, :low], source_ref[...]) + dot(
            held_ref[1, :low], spun_ref[...]
        )

    (direct,) = call(
        direct_step, [((low, width), f32)], (held, source, spun), 4 * low * norb * width
    )

    def turn_round(other_ref, reach_ref, before_ref, held_ref, direct_ref, inc_ref, top_ref):
        incoming = reach_step(levels - 1, 0, reach_ref, before_ref, other_ref[...]).astype(bf16)
        inc_ref[...] = incoming
        top_ref[...] = direct_ref[:layer] + applied(
            held_ref[0, :layer, :layer], held_ref[1, :layer, :layer], incoming
        )

    incoming, forward_top = call(
        turn_round,
        [((layer, width), bf16), ((layer, width), f32)],
        (arrived, reach, befores[levels - 1], held, direct),
        16 * layer * layer * width,
    )
    arrived, reach = scan(forward_top, 1)

    def forward_step(held_ref, inc_ref, direct_ref, low_ref, out_ref):
        incoming = inc_ref[...]
        spun = turned(incoming.astype(f32)).astype(bf16)
        more = dot(held_ref[0, :, :layer], incoming) + dot(held_ref[1, :, :layer], spun)
        out_ref[:low] = direct_ref[...] + more[:low]
        out_ref[low:] = low_ref[...] + more[low:]

    (forward,) = call(
        forward_step,
        [((norb, width), f32)],
        (held, incoming, direct, direct_low),
        8 * norb * layer * width,
    )

    def finish(
        other_ref, reach_ref, before_ref, held_ref, coup_ref, forward_ref, out_ref, kept, sem
    ):
        back = reach_step(levels - 1, 1, reach_ref, before_ref, other_ref[...])
        outgoing = fine(coup_ref[...], back).astype(bf16)
        spun = turned(outgoing.astype(f32)).astype(bf16)
        copies = []
        for i in range(norb // layer):
            part = pl.ds(i * layer, layer)
            kept[part] = (
                forward_ref[part]
                + dot(held_ref[0, part, low:], outgoing)
                + dot(held_ref[1, part, low:], spun)
            ).astype(bf16)
            copy = pltpu.make_async_copy(kept.at[part], out_ref.at[part], sem.at[i])
            copy.start()
            copies.append(copy)
        for copy in copies:
            copy.wait()

    (out,) = call(
        finish,
        [((norb, width), bf16)],
        (arrived, reach, befores[levels - 1], held, coup, forward),
        8 * norb * layer * width,
        scratch=[pltpu.VMEM((norb, width), bf16), pltpu.SemaphoreType.DMA((norb // layer,))],
        out_space=pltpu.HBM,
    )
    return out[None, None]


def solution(mesh):
    in_specs = (
        P("energy", "slab", None, None, None),
        P("energy", "slab", None, None),
        P("energy", "slab", None, None),
        P("slab", None, None),
        P(),
        P(),
        P(),
    )
    out_specs = P("energy", "slab", None, None)
    return jax.shard_map(body, mesh=mesh, in_specs=in_specs, out_specs=out_specs, check_vma=False)
```

```python
import math

import jax
import jax.numpy as jnp
from jax import lax
from jax.experimental import pallas as pl
from jax.experimental.pallas import tpu as pltpu
from jax.sharding import PartitionSpec as P


NBLK = 16
CAP = 4
VMEM_BYTES = 67043328
bf16 = jnp.bfloat16
f32 = jnp.float32
VMEM = pltpu.VMEM


def swapped(block, axis, mask):
    count = lax.axis_size(axis)
    return lax.ppermute(block, axis, [(i, i ^ mask) for i in range(count)])


def dot(a, b):
    return jnp.dot(a, b, preferred_element_type=f32)


def turned(v):
    half = v.shape[1] // 2
    if half % 128 == 0:
        return jnp.concatenate([-v[:, half:], v[:, :half]], axis=1)
    lane = lax.broadcasted_iota(jnp.int32, v.shape, 1)
    moved = pltpu.roll(v, half, 1)
    return jnp.where(lane < half, -moved, moved)


def applied(real, imag, v):
    v = v.astype(f32)
    return dot(real, v.astype(bf16)) + dot(imag, turned(v).astype(bf16))


def mapped(wide, v):
    side = wide.shape[1] // 2
    return applied(wide[:, :side], wide[:, side:], v)


def fine(real, v):
    high = v.astype(bf16)
    return dot(real, high) + dot(real, (v - high.astype(f32)).astype(bf16))


def place(k):
    return ((lax.axis_index("slab") >> k) & 1) == 1


def call(kernel, outs, args, flops, spaces=None, scratch=(), out_space=VMEM, spare=None):
    spaces = spaces or {}
    specs = [pl.BlockSpec(memory_space=spaces.get(i, VMEM)) for i in range(len(args))]
    moved = sum(a.size * a.dtype.itemsize for a in args)
    kept = sum(math.prod(s) * jnp.dtype(t).itemsize for s, t in outs)
    kept += sum(a.size * a.dtype.itemsize for i, a in enumerate(args) if i not in spaces)
    limit = kept + (4 << 20) if spare is None else VMEM_BYTES - spare
    shapes = [jax.ShapeDtypeStruct(s, t) for s, t in outs]
    return pl.pallas_call(
        kernel,
        out_shape=shapes,
        in_specs=specs,
        out_specs=[pl.BlockSpec(memory_space=out_space)] * len(shapes),
        scratch_shapes=list(scratch),
        compiler_params=pltpu.CompilerParams(vmem_limit_bytes=limit),
        cost_estimate=pl.CostEstimate(
            flops=flops, bytes_accessed=moved, transcendentals=0
        ),
    )(*args)


def body(pivots, injection, previous, coupling, strength, block_start, block_count):
    green = pivots[0, 0]
    norb = green.shape[1]
    layer = coupling.shape[1]
    width = injection.shape[3]
    rows = norb // NBLK
    span = rows * CAP
    far_green = pltpu.with_memory_space_constraint(green, pltpu.HBM)
    coup = coupling[0]
    far_coup = pltpu.with_memory_space_constraint(coup, pltpu.HBM)
    panel = previous[0, 0]
    energies = lax.axis_size("energy")
    slabs = lax.axis_size("slab")
    levels = slabs.bit_length() - 1
    low = norb - layer
    SMEM = pltpu.SMEM

    def own_maps(green_ref, coup_ref, maps_ref, turn_ref, corner, near, sem, sem_c):
        spots = ((pl.ds(low, layer), pl.ds(0, layer)), (pl.ds(0, layer), pl.ds(low, layer)))
        copies = [
            [pltpu.make_async_copy(green_ref.at[k, r, c], corner.at[i, k], sem.at[i, k]) for k in range(2)]
            for i, (r, c) in enumerate(spots)
        ]
        first = pltpu.make_async_copy(coup_ref, near, sem_c)
        first.start()
        for pair in copies:
            for copy in pair:
                copy.start()
        first.wait()
        c = near[...]
        ct = c.astype(f32).T.astype(bf16)
        turn_ref[...] = ct
        for k in range(2):
            copies[0][k].wait()
            maps_ref[:layer, k * layer : (k + 1) * layer] = dot(ct, corner[0, k]).astype(bf16)
        for k in range(2):
            copies[1][k].wait()
            maps_ref[layer:, k * layer : (k + 1) * layer] = dot(corner[1, k], c).astype(bf16)

    maps, coup_t = call(
        own_maps,
        [((2 * layer, 2 * layer), bf16), ((layer, layer), bf16)],
        (far_green, far_coup),
        8 * layer**3,
        {0: pltpu.HBM, 1: pltpu.HBM},
        [
            pltpu.VMEM((2, 2, layer, layer), bf16),
            pltpu.VMEM((layer, layer), bf16),
            pltpu.SemaphoreType.DMA((2, 2)),
            pltpu.SemaphoreType.DMA,
        ],
    )

    def pick(start_ref, panel_ref, *outs):
        me = lax.axis_index("energy")
        for k in range(energies - 1):
            first = pl.multiple_of(start_ref[me ^ (k + 1), me] * rows, rows)
            outs[k][...] = panel_ref[pl.ds(first, span)]

    pieces = call(
        pick, [((span, width), bf16)] * (energies - 1), (block_start, panel), 0, {0: SMEM}
    )
    received = [None] * (energies - 1)
    for mask in range(energies - 1, 0, -1):
        received[mask - 1] = swapped(pieces[mask - 1], "energy", mask)

    held = green

    def fetch(green_ref, hint_ref, held_ref, sem):
        parts = [(k, pl.ds(i * layer, layer)) for k in range(2) for i in range(norb // layer)]
        copies = [
            pltpu.make_async_copy(green_ref.at[k, r], held_ref.at[k, r], sem.at[i])
            for i, (k, r) in enumerate(parts)
        ]
        for copy in copies:
            copy.start()
        for copy in copies:
            copy.wait()

    (held,) = call(
        fetch,
        [(green.shape, bf16)],
        (far_green, coup_t),
        0,
        {0: pltpu.HBM, 1: pl.ANY},
        [pltpu.SemaphoreType.DMA((2 * norb // layer,))],
    )

    ways = (slice(0, layer), slice(layer, 2 * layer))
    wide = (2 * layer, 2 * layer)
    laters, befores = [], [None]
    own = maps
    for level in range(levels - 1):
        grow = level + 2 < levels

        def group(*refs, level=level, grow=grow):
            refs = list(refs)
            mine = refs.pop(0)
            if level == 0:
                near = refs.pop(0)
                theirs = [near[w] for w in ways]
            else:
                near, far, old = refs.pop(0), refs.pop(0), refs.pop(0)
                first = place(0)
                a, b = near[...], far[...]
                theirs = [jnp.where(first, b, a), jnp.where(first, a, b)]
            later_ref, before_ref = refs.pop(0), refs.pop(0)
            if grow:
                total_ref, send_ref = refs
            grown = []
            for way in range(2):
                after = place(level) if way == 0 else ~place(level)
                other, self = theirs[way], mine[ways[way]]
                later = jnp.where(after, self, other)
                later_ref[ways[way]] = later
                if level == 0:
                    row = lax.broadcasted_iota(jnp.int32, (layer, 2 * layer), 0)
                    col = lax.broadcasted_iota(jnp.int32, (layer, 2 * layer), 1)
                    before = (row == col).astype(f32).astype(bf16)
                    before_ref[ways[way]] = jnp.where(after, other, before)
                else:
                    before = old[ways[way]]
                    before_ref[ways[way]] = jnp.where(
                        after, mapped(before, other).astype(bf16), before
                    )
                if grow:
                    earlier = jnp.where(after, other, self)
                    grown.append(mapped(later, earlier).astype(bf16))
                    total_ref[ways[way]] = grown[way]
            if grow:
                send_ref[...] = jnp.where(place(0), grown[1], grown[0])

        if level == 0:
            args = (own, swapped(own, "slab", 1))
        else:
            near = swapped(send, "slab", 1 << level)
            args = (own, near, swapped(near, "slab", 1), befores[-1])
        outs = [(wide, bf16), (wide, bf16)]
        if grow:
            outs += [(wide, bf16), ((layer, 2 * layer), bf16)]
        res = call(group, outs, args, 32 * layer**3)
        laters.append(res[0])
        befores.append(res[1])
        if grow:
            own, send = res[2], res[3]

    def reach_step(level, way, reach_ref, before_ref, other):
        after = place(level) if way == 0 else ~place(level)
        if level == 0:
            return jnp.where(after, other, jnp.zeros_like(other))
        more = mapped(before_ref[ways[way]], other)
        return reach_ref[...] + jnp.where(after, more, jnp.zeros_like(more))

    def scan(vector, way):
        total, reach, sent = vector, None, vector
        for level in range(levels - 1):
            other = swapped(sent, "slab", 1 << level)

            final = level == levels - 2

            def step(*refs, level=level, final=final):
                refs = list(refs)
                mine, other_ref, later = refs[:3]
                sent_ref, reached = refs[-2:]
                after = place(level) if way == 0 else ~place(level)
                theirs = other_ref[...].astype(f32)
                self = mine[...]
                earlier = jnp.where(after, theirs, self)
                latest = jnp.where(after, self, theirs)
                new = mapped(later[ways[way]], earlier) + latest
                sent_ref[...] = new.astype(bf16)
                if not final:
                    refs[-3][...] = new
                before = refs[3] if level else None
                so_far = refs[4] if level else None
                reached[...] = reach_step(level, way, so_far, before, theirs)

            args = (total, other, laters[level])
            if level:
                args += (befores[level], reach)
            size = (layer, width)
            res = call(
                step,
                [(size, f32)] * (not final) + [(size, bf16), (size, f32)],
                args,
                16 * layer * layer * width,
            )
            total, sent, reach = res if not final else [None] + list(res)
        return swapped(sent, "slab", slabs // 2), reach

    def prepare(inj_ref, panel_ref, start_ref, count_ref, strength_ref, acc_ref, weight_ref):
        me = lax.axis_index("energy")
        row = lax.broadcasted_iota(jnp.int32, (span, width), 0)
        acc_ref[...] = inj_ref[...].astype(f32)
        for k in range(energies):
            s = me ^ k
            weight = jnp.where(row < count_ref[me, s] * rows, strength_ref[me, s], 0.0)
            if k:
                weight_ref[k - 1] = weight
            else:
                first = pl.multiple_of(start_ref[me, me] * rows, rows)
                part = pl.ds(first, span)
                acc_ref[part] = acc_ref[part] + panel_ref[part].astype(f32) * weight

    acc, weights = call(
        prepare,
        [((norb, width), f32), ((energies - 1, span, width), f32)],
        (injection[0, 0], panel, block_start, block_count, strength),
        0,
        {2: SMEM, 3: SMEM, 4: SMEM},
    )

    def load(start_ref, acc_ref, weight_ref, held_ref, turn_ref, *refs):
        got, (source_ref, spun_ref, low_ref, sent_ref, sum_ref) = refs[:-5], refs[-5:]
        me = lax.axis_index("energy")
        sum_ref[...] = acc_ref[...]
        for k in range(1, energies):
            first = pl.multiple_of(start_ref[me, me ^ k] * rows, rows)
            part = pl.ds(first, span)
            sum_ref[part] = sum_ref[part] + got[k - 1][...].astype(f32) * weight_ref[k - 1]
        source = sum_ref[...].astype(bf16)
        spun = turned(source.astype(f32)).astype(bf16)
        source_ref[...] = source
        spun_ref[...] = spun
        direct = dot(held_ref[0, low:], source) + dot(held_ref[1, low:], spun)
        low_ref[...] = direct
        sent_ref[...] = fine(turn_ref[...], direct)

    source, spun, direct_low, sent = call(
        load,
        [((norb, width), bf16)] * 2 + [((layer, width), f32)] * 2,
        (block_start, acc, weights, held, coup_t, *received),
        4 * layer * norb * width,
        {0: SMEM},
        [pltpu.VMEM((norb, width), f32)],
    )
    arrived, reach = scan(sent, 0)

    def direct_step(held_ref, source_ref, spun_ref, out_ref):
        out_ref[...] = dot(held_ref[0, :low], source_ref[...]) + dot(
            held_ref[1, :low], spun_ref[...]
        )

    (direct,) = call(
        direct_step, [((low, width), f32)], (held, source, spun), 4 * low * norb * width
    )

    def turn_round(other_ref, reach_ref, before_ref, held_ref, direct_ref, inc_ref, top_ref):
        incoming = reach_step(levels - 1, 0, reach_ref, before_ref, other_ref[...]).astype(bf16)
        inc_ref[...] = incoming
        top_ref[...] = direct_ref[:layer] + applied(
            held_ref[0, :layer, :layer], held_ref[1, :layer, :layer], incoming
        )

    incoming, forward_top = call(
        turn_round,
        [((layer, width), bf16), ((layer, width), f32)],
        (arrived, reach, befores[levels - 1], held, direct),
        16 * layer * layer * width,
    )
    arrived, reach = scan(forward_top, 1)

    def forward_step(held_ref, inc_ref, direct_ref, low_ref, out_ref):
        incoming = inc_ref[...]
        spun = turned(incoming.astype(f32)).astype(bf16)
        more = dot(held_ref[0, :, :layer], incoming) + dot(held_ref[1, :, :layer], spun)
        out_ref[:low] = direct_ref[...] + more[:low]
        out_ref[low:] = low_ref[...] + more[low:]

    (forward,) = call(
        forward_step,
        [((norb, width), f32)],
        (held, incoming, direct, direct_low),
        8 * norb * layer * width,
    )

    def finish(
        other_ref, reach_ref, before_ref, held_ref, coup_ref, forward_ref, out_ref, kept, sem
    ):
        back = reach_step(levels - 1, 1, reach_ref, before_ref, other_ref[...])
        outgoing = fine(coup_ref[...], back).astype(bf16)
        spun = turned(outgoing.astype(f32)).astype(bf16)
        copies = []
        for i in range(norb // layer):
            part = pl.ds(i * layer, layer)
            kept[part] = (
                forward_ref[part]
                + dot(held_ref[0, part, low:], outgoing)
                + dot(held_ref[1, part, low:], spun)
            ).astype(bf16)
            copy = pltpu.make_async_copy(kept.at[part], out_ref.at[part], sem.at[i])
            copy.start()
            copies.append(copy)
        for copy in copies:
            copy.wait()

    (out,) = call(
        finish,
        [((norb, width), bf16)],
        (arrived, reach, befores[levels - 1], held, coup, forward),
        8 * norb * layer * width,
        scratch=[pltpu.VMEM((norb, width), bf16), pltpu.SemaphoreType.DMA((norb // layer,))],
        out_space=pltpu.HBM,
    )
    return out[None, None]


def solution(mesh):
    in_specs = (
        P("energy", "slab", None, None, None),
        P("energy", "slab", None, None),
        P("energy", "slab", None, None),
        P("slab", None, None),
        P(),
        P(),
        P(),
    )
    out_specs = P("energy", "slab", None, None)
    return jax.shard_map(body, mesh=mesh, in_specs=in_specs, out_specs=out_specs, check_vma=False)
```

```python
import math

import jax
import jax.numpy as jnp
from jax import lax
from jax.experimental import pallas as pl
from jax.experimental.pallas import tpu as pltpu
from jax.sharding import PartitionSpec as P


NBLK = 16
CAP = 4
VMEM_BYTES = 67043328
bf16 = jnp.bfloat16
f32 = jnp.float32
VMEM = pltpu.VMEM


def swapped(block, axis, mask):
    count = lax.axis_size(axis)
    return lax.ppermute(block, axis, [(i, i ^ mask) for i in range(count)])


def dot(a, b):
    return jnp.dot(a, b, preferred_element_type=f32)


def turned(v):
    half = v.shape[1] // 2
    if half % 128 == 0:
        return jnp.concatenate([-v[:, half:], v[:, :half]], axis=1)
    lane = lax.broadcasted_iota(jnp.int32, v.shape, 1)
    moved = pltpu.roll(v, half, 1)
    return jnp.where(lane < half, -moved, moved)


def applied(real, imag, v):
    v = v.astype(f32)
    return dot(real, v.astype(bf16)) + dot(imag, turned(v).astype(bf16))


def mapped(wide, v):
    side = wide.shape[1] // 2
    return applied(wide[:, :side], wide[:, side:], v)


def fine(real, v):
    high = v.astype(bf16)
    return dot(real, high) + dot(real, (v - high.astype(f32)).astype(bf16))


def place(k):
    return ((lax.axis_index("slab") >> k) & 1) == 1


def call(kernel, outs, args, flops, spaces=None, scratch=(), out_space=VMEM, spare=None):
    spaces = spaces or {}
    specs = [pl.BlockSpec(memory_space=spaces.get(i, VMEM)) for i in range(len(args))]
    moved = sum(a.size * a.dtype.itemsize for a in args)
    kept = sum(math.prod(s) * jnp.dtype(t).itemsize for s, t in outs)
    kept += sum(a.size * a.dtype.itemsize for i, a in enumerate(args) if i not in spaces)
    limit = kept + (4 << 20) if spare is None else VMEM_BYTES - spare
    shapes = [jax.ShapeDtypeStruct(s, t) for s, t in outs]
    return pl.pallas_call(
        kernel,
        out_shape=shapes,
        in_specs=specs,
        out_specs=[pl.BlockSpec(memory_space=out_space)] * len(shapes),
        scratch_shapes=list(scratch),
        compiler_params=pltpu.CompilerParams(vmem_limit_bytes=limit),
        cost_estimate=pl.CostEstimate(
            flops=flops, bytes_accessed=moved, transcendentals=0
        ),
    )(*args)


def body(pivots, injection, previous, coupling, strength, block_start, block_count):
    green = pivots[0, 0]
    norb = green.shape[1]
    layer = coupling.shape[1]
    width = injection.shape[3]
    rows = norb // NBLK
    span = rows * CAP
    far_green = pltpu.with_memory_space_constraint(green, pltpu.HBM)
    coup = coupling[0]
    far_coup = pltpu.with_memory_space_constraint(coup, pltpu.HBM)
    panel = previous[0, 0]
    energies = lax.axis_size("energy")
    slabs = lax.axis_size("slab")
    levels = slabs.bit_length() - 1
    low = norb - layer
    SMEM = pltpu.SMEM

    rows_of = [slice(k * layer, (k + 1) * layer) for k in range(6)]
    triple, one_map = (3 * layer, 2 * layer), (layer, 2 * layer)

    def own_maps(green_ref, coup_ref, maps_ref, turn_ref, corner, near, sem, sem_c):
        top, end = pl.ds(0, layer), pl.ds(low, layer)
        copies = [
            [
                pltpu.make_async_copy(green_ref.at[k, r, c], corner.at[i, k], sem.at[i, k])
                for k in range(2)
            ]
            for i, (r, c) in enumerate(((end, top), (top, end), (top, top)))
        ]
        first = pltpu.make_async_copy(coup_ref, near, sem_c)
        first.start()
        for pair in copies:
            for copy in pair:
                copy.start()
        first.wait()
        c = near[...]
        ct = c.astype(f32).T.astype(bf16)
        turn_ref[...] = ct
        for i in range(3):
            for k in range(2):
                copies[i][k].wait()
                held = corner[i, k]
                if i == 0:
                    held = dot(ct, held).astype(bf16)
                elif i == 1:
                    held = dot(held, c).astype(bf16)
                maps_ref[rows_of[i], rows_of[k]] = held

    maps, coup_t = call(
        own_maps,
        [(triple, bf16), ((layer, layer), bf16)],
        (far_green, far_coup),
        8 * layer**3,
        {0: pltpu.HBM, 1: pltpu.HBM},
        [
            pltpu.VMEM((3, 2, layer, layer), bf16),
            pltpu.VMEM((layer, layer), bf16),
            pltpu.SemaphoreType.DMA((3, 2)),
            pltpu.SemaphoreType.DMA,
        ],
    )

    def pick(start_ref, panel_ref, *outs):
        me = lax.axis_index("energy")
        for k in range(energies - 1):
            first = pl.multiple_of(start_ref[me ^ (k + 1), me] * rows, rows)
            outs[k][...] = panel_ref[pl.ds(first, span)]

    pieces = call(
        pick, [((span, width), bf16)] * (energies - 1), (block_start, panel), 0, {0: SMEM}
    )
    received = [None] * (energies - 1)
    for mask in range(energies - 1, 0, -1):
        received[mask - 1] = swapped(pieces[mask - 1], "energy", mask)

    held = green

    def fetch(green_ref, hint_ref, held_ref, sem):
        parts = [(k, pl.ds(i * layer, layer)) for k in range(2) for i in range(norb // layer)]
        copies = [
            pltpu.make_async_copy(green_ref.at[k, r], held_ref.at[k, r], sem.at[i])
            for i, (k, r) in enumerate(parts)
        ]
        for copy in copies:
            copy.start()
        for copy in copies:
            copy.wait()

    (held,) = call(
        fetch,
        [(green.shape, bf16)],
        (far_green, coup_t),
        0,
        {0: pltpu.HBM, 1: pl.ANY},
        [pltpu.SemaphoreType.DMA((2 * norb // layer,))],
    )

    half = 3 * layer // 2
    final = levels - 1
    plans, members, totals = [], None, maps
    for level in range(final):
        near = swapped(totals if level == 0 else send, "slab", 1 << level)
        far = None if level == 0 else swapped(near, "slab", 1)
        closing = level == final - 1

        def group(*refs, level=level, closing=closing):
            refs = list(refs)
            mine, near_ref = refs[:2]
            plan, member, send_ref = refs[-3:]
            total = None if closing else refs[-4]
            after = place(level)
            if level == 0:
                theirs = near_ref[...]
            else:
                first = place(0)
                a, b = near_ref[...], refs[2][...]
                theirs = jnp.concatenate(
                    [jnp.where(first, b, a), jnp.where(first, a, b)], axis=0
                )
                old = refs[3]
            own_a, own_b, own_e = (mine[rows_of[k]] for k in range(3))
            its_a, its_b, its_e = (theirs[rows_of[k]] for k in range(3))
            a_left = jnp.where(after, its_a, own_a)
            a_right = jnp.where(after, own_a, its_a)
            b_left = jnp.where(after, its_b, own_b)
            b_right = jnp.where(after, own_b, its_b)
            e_left = jnp.where(after, its_e, own_e)
            e_right = jnp.where(after, own_e, its_e)
            plan[rows_of[0]] = a_right
            plan[rows_of[1]] = e_right
            if level:
                plan[rows_of[2]] = old[rows_of[0]]
                plan[rows_of[3]] = b_left
                plan[rows_of[4]] = jnp.where(after, old[rows_of[2]], old[rows_of[1]])
            else:
                plan[rows_of[2]] = b_left

            def reflected():
                bounce = mapped(e_right, a_left).astype(bf16)
                return bounce, (e_left.astype(f32) + mapped(b_left, bounce)).astype(bf16)

            def before():
                p = old[rows_of[0]]
                return jnp.where(after, mapped(p, a_left).astype(bf16), p)

            def behind():
                q = old[rows_of[1]]
                return jnp.where(after, q, mapped(q, b_right).astype(bf16))

            def turned_round(bounce):
                q, r = old[rows_of[1]], old[rows_of[2]]
                more = mapped(jnp.where(after, r, q), jnp.where(after, a_left, bounce))
                return jnp.where(after, more, more + r.astype(f32)).astype(bf16)

            if level == 0:
                bounce, e_total = reflected()
                row = lax.broadcasted_iota(jnp.int32, one_map, 0)
                col = lax.broadcasted_iota(jnp.int32, one_map, 1)
                unit = (row == col).astype(f32).astype(bf16)
                ends = (
                    jnp.where(after, a_left, unit),
                    jnp.where(after, unit, b_right),
                    jnp.where(after, jnp.zeros_like(bounce), bounce),
                )
            elif not closing:
                bounce, e_total = reflected()
                ends = (before(), behind(), turned_round(bounce))
            if not closing:
                grown = (
                    mapped(a_right, a_left).astype(bf16),
                    mapped(b_left, b_right).astype(bf16),
                    e_total,
                )
                for k in range(3):
                    total[rows_of[k]] = grown[k]
                whole = jnp.concatenate(grown, axis=0)
                send_ref[...] = jnp.where(place(0), whole[half:], whole[:half])
                for k, end in enumerate(ends):
                    member[rows_of[k]] = end
                return

            @pl.when(place(final))
            def _():
                bounce, e_total = reflected()
                member[rows_of[0]] = before()
                member[rows_of[1]] = turned_round(bounce)
                cut = layer // 2
                send_ref[...] = jnp.where(place(0), e_total[cut:], e_total[:cut])

            @pl.when(~place(final))
            def _():
                member[rows_of[0]] = jnp.zeros(one_map, bf16)
                member[rows_of[1]] = behind()
                send_ref[...] = jnp.zeros((layer // 2, 2 * layer), bf16)

        plan_size = (5 * layer if level else 3 * layer, 2 * layer)
        args = (totals, near) if level == 0 else (totals, near, far, members)
        *grown, plan, members, send = call(
            group,
            [(triple, bf16)] * (not closing)
            + [
                (plan_size, bf16),
                ((2 * layer, 2 * layer) if closing else triple, bf16),
                ((layer // 2 if closing else half, 2 * layer), bf16),
            ],
            args,
            64 * layer**3,
        )
        totals = None if closing else grown[0]
        plans.append(plan)
    e_near = swapped(send, "slab", 1 << final)
    e_far = swapped(e_near, "slab", 1)

    ways = (slice(0, layer), slice(layer, 2 * layer))
    pair = (2 * layer, width)

    def scan(vector):
        total, sent, reach = vector, vector, None
        for level in range(final):
            other = swapped(sent, "slab", 1 << level)
            closing = level == final - 1

            def step(*refs, level=level, closing=closing):
                mine, other_ref, plan = refs[:3]
                total_ref, sent_ref, reach_ref = refs[-3:]
                after = place(level)
                own = [mine[w] for w in ways]
                its = [other_ref[w].astype(f32) for w in ways]
                c_left, c_right = jnp.where(after, its[0], own[0]), jnp.where(after, own[0], its[0])
                f_left, f_right = jnp.where(after, its[1], own[1]), jnp.where(after, own[1], its[1])
                spread = mapped(plan[: (3 if level else 2) * layer], c_left)
                back = f_right + spread[ways[1]]
                c_new = c_right + spread[ways[0]]
                f_new = f_left + mapped(plan[rows_of[3 if level else 2]], back)
                if level:
                    so_far = refs[3]
                    more = mapped(plan[rows_of[4]], jnp.where(after, c_left, back))
                    z = so_far[ways[0]] + jnp.where(after, spread[rows_of[2]], 0.0)
                    u = so_far[ways[1]] + more
                else:
                    z = jnp.where(after, c_left, jnp.zeros_like(c_left))
                    u = jnp.where(after, jnp.zeros_like(back), back)
                reach_ref[ways[0]] = z
                reach_ref[ways[1]] = u
                if closing:
                    total_ref[...] = c_new
                    sent_ref[...] = jnp.where(place(final), f_new, c_new).astype(bf16)
                else:
                    total_ref[ways[0]] = c_new
                    total_ref[ways[1]] = f_new
                    sent_ref[ways[0]] = c_new.astype(bf16)
                    sent_ref[ways[1]] = f_new.astype(bf16)

            size = (layer, width) if closing else pair
            args = (total, other, plans[level]) + ((reach,) if level else ())
            total, sent, reach = call(
                step, [(size, f32), (size, bf16), (pair, f32)], args, 40 * layer * layer * width
            )
        return total, swapped(sent, "slab", 1 << final), reach

    def prepare(inj_ref, panel_ref, start_ref, count_ref, strength_ref, acc_ref, weight_ref):
        me = lax.axis_index("energy")
        row = lax.broadcasted_iota(jnp.int32, (span, width), 0)
        acc_ref[...] = inj_ref[...].astype(f32)
        for k in range(energies):
            s = me ^ k
            weight = jnp.where(row < count_ref[me, s] * rows, strength_ref[me, s], 0.0)
            if k:
                weight_ref[k - 1] = weight
            else:
                first = pl.multiple_of(start_ref[me, me] * rows, rows)
                part = pl.ds(first, span)
                acc_ref[part] = acc_ref[part] + panel_ref[part].astype(f32) * weight

    acc, weights = call(
        prepare,
        [((norb, width), f32), ((energies - 1, span, width), f32)],
        (injection[0, 0], panel, block_start, block_count, strength),
        0,
        {2: SMEM, 3: SMEM, 4: SMEM},
    )

    def load(start_ref, acc_ref, weight_ref, held_ref, turn_ref, *refs):
        got, (source_ref, spun_ref, low_ref, sent_ref, sum_ref) = refs[:-5], refs[-5:]
        me = lax.axis_index("energy")
        sum_ref[...] = acc_ref[...]
        for k in range(1, energies):
            first = pl.multiple_of(start_ref[me, me ^ k] * rows, rows)
            part = pl.ds(first, span)
            sum_ref[part] = sum_ref[part] + got[k - 1][...].astype(f32) * weight_ref[k - 1]
        source = sum_ref[...].astype(bf16)
        spun = turned(source.astype(f32)).astype(bf16)
        source_ref[...] = source
        spun_ref[...] = spun
        direct = dot(held_ref[0, low:], source) + dot(held_ref[1, low:], spun)
        low_ref[...] = direct
        sent_ref[ways[0]] = fine(turn_ref[...], direct)
        sent_ref[ways[1]] = dot(held_ref[0, :layer], source) + dot(held_ref[1, :layer], spun)

    source, spun, direct_low, sent = call(
        load,
        [((norb, width), bf16)] * 2 + [((layer, width), f32), (pair, f32)],
        (block_start, acc, weights, held, coup_t, *received),
        8 * layer * norb * width,
        {0: SMEM},
        [pltpu.VMEM((norb, width), f32)],
    )
    c_total, arrived, reach = scan(sent)

    def direct_step(held_ref, source_ref, spun_ref, ends_ref, low_ref, out_ref):
        mid = slice(layer, low)
        out_ref[:layer] = ends_ref[ways[1]]
        out_ref[mid] = dot(held_ref[0, mid], source_ref[...]) + dot(
            held_ref[1, mid], spun_ref[...]
        )
        out_ref[low:] = low_ref[...]

    (direct,) = call(
        direct_step,
        [((norb, width), f32)],
        (held, source, spun, sent, direct_low),
        4 * (low - layer) * norb * width,
    )

    def finish(
        other_ref, c_ref, near_ref, far_ref, member, reach_ref, held_ref, coup_ref, direct_ref,
        out_ref, kept, sem,
    ):
        after, first = place(final), place(0)
        other = other_ref[...].astype(f32)
        c_left = c_ref[...]
        a, b = mapped(near_ref[...], c_left), mapped(far_ref[...], c_left)
        bounce = jnp.concatenate([jnp.where(first, b, a), jnp.where(first, a, b)], axis=0)
        back = other + jnp.where(after, jnp.zeros_like(bounce), bounce)
        more = mapped(member[ways[0]], other)
        z = reach_ref[ways[0]] + jnp.where(after, more, jnp.zeros_like(more))
        incoming = z.astype(bf16)
        spun_z = turned(incoming.astype(f32)).astype(bf16)
        u = reach_ref[ways[1]] + mapped(member[ways[1]], back)
        outgoing = fine(coup_ref[...], u).astype(bf16)
        spun_u = turned(outgoing.astype(f32)).astype(bf16)
        copies = []
        for i in range(norb // layer):
            part = pl.ds(i * layer, layer)
            kept[part] = (
                direct_ref[part]
                + dot(held_ref[0, part, :layer], incoming)
                + dot(held_ref[1, part, :layer], spun_z)
                + dot(held_ref[0, part, low:], outgoing)
                + dot(held_ref[1, part, low:], spun_u)
            ).astype(bf16)
            copy = pltpu.make_async_copy(kept.at[part], out_ref.at[part], sem.at[i])
            copy.start()
            copies.append(copy)
        for copy in copies:
            copy.wait()

    (out,) = call(
        finish,
        [((norb, width), bf16)],
        (arrived, c_total, e_near, e_far, members, reach, held, coup, direct),
        16 * norb * layer * width,
        scratch=[pltpu.VMEM((norb, width), bf16), pltpu.SemaphoreType.DMA((norb // layer,))],
        out_space=pltpu.HBM,
    )
    return out[None, None]


def solution(mesh):
    in_specs = (
        P("energy", "slab", None, None, None),
        P("energy", "slab", None, None),
        P("energy", "slab", None, None),
        P("slab", None, None),
        P(),
        P(),
        P(),
    )
    out_specs = P("energy", "slab", None, None)
    return jax.shard_map(body, mesh=mesh, in_specs=in_specs, out_specs=out_specs, check_vma=False)
```

```python
import math

import jax
import jax.numpy as jnp
from jax import lax
from jax.experimental import pallas as pl
from jax.experimental.pallas import tpu as pltpu
from jax.sharding import PartitionSpec as P


NBLK = 16
CAP = 4
VMEM_BYTES = 67043328
bf16 = jnp.bfloat16
f32 = jnp.float32
VMEM = pltpu.VMEM


def swapped(block, axis, mask):
    count = lax.axis_size(axis)
    return lax.ppermute(block, axis, [(i, i ^ mask) for i in range(count)])


def dot(a, b):
    return jnp.dot(a, b, preferred_element_type=f32)


def turned(v):
    half = v.shape[1] // 2
    if half % 128 == 0:
        return jnp.concatenate([-v[:, half:], v[:, :half]], axis=1)
    lane = lax.broadcasted_iota(jnp.int32, v.shape, 1)
    moved = pltpu.roll(v, half, 1)
    return jnp.where(lane < half, -moved, moved)


def applied(real, imag, v):
    v = v.astype(f32)
    return dot(real, v.astype(bf16)) + dot(imag, turned(v).astype(bf16))


def mapped(wide, v):
    side = wide.shape[1] // 2
    return applied(wide[:, :side], wide[:, side:], v)


def fine(real, v):
    high = v.astype(bf16)
    return dot(real, high) + dot(real, (v - high.astype(f32)).astype(bf16))


def place(k):
    return ((lax.axis_index("slab") >> k) & 1) == 1


def call(kernel, outs, args, flops, spaces=None, scratch=(), out_space=VMEM, spare=None):
    spaces = spaces or {}
    specs = [pl.BlockSpec(memory_space=spaces.get(i, VMEM)) for i in range(len(args))]
    moved = sum(a.size * a.dtype.itemsize for a in args)
    kept = sum(math.prod(s) * jnp.dtype(t).itemsize for s, t in outs)
    kept += sum(a.size * a.dtype.itemsize for i, a in enumerate(args) if i not in spaces)
    limit = kept + (4 << 20) if spare is None else VMEM_BYTES - spare
    shapes = [jax.ShapeDtypeStruct(s, t) for s, t in outs]
    return pl.pallas_call(
        kernel,
        out_shape=shapes,
        in_specs=specs,
        out_specs=[pl.BlockSpec(memory_space=out_space)] * len(shapes),
        scratch_shapes=list(scratch),
        compiler_params=pltpu.CompilerParams(vmem_limit_bytes=limit),
        cost_estimate=pl.CostEstimate(
            flops=flops, bytes_accessed=moved, transcendentals=0
        ),
    )(*args)


def in_hbm(array):
    return pltpu.with_memory_space_constraint(array, pltpu.HBM)


def body(pivots, injection, previous, coupling, strength, block_start, block_count):
    green = pivots[0, 0]
    norb = green.shape[1]
    layer = coupling.shape[1]
    width = injection.shape[3]
    rows = norb // NBLK
    span = rows * CAP
    far_green = in_hbm(green)
    coup = coupling[0]
    far_coup = in_hbm(coup)
    panel = previous[0, 0]
    energies = lax.axis_size("energy")
    slabs = lax.axis_size("slab")
    levels = slabs.bit_length() - 1
    low = norb - layer
    SMEM = pltpu.SMEM

    rows_of = [slice(k * layer, (k + 1) * layer) for k in range(6)]
    triple, one_map = (3 * layer, 2 * layer), (layer, 2 * layer)

    def own_maps(green_ref, coup_ref, start_ref, panel_ref, *refs):
        maps_ref, turn_ref = refs[:2]
        pieces = refs[2 : energies + 1]
        corner, near, table, sem, sem_c, sem_t, sem_p = refs[energies + 1 :]
        ask = pltpu.make_async_copy(start_ref, table, sem_t)
        ask.start()
        top, end = pl.ds(0, layer), pl.ds(low, layer)
        copies = [
            [
                pltpu.make_async_copy(green_ref.at[k, r, c], corner.at[i, k], sem.at[i, k])
                for k in range(2)
            ]
            for i, (r, c) in enumerate(((end, top), (top, end), (top, top)))
        ]
        first = pltpu.make_async_copy(coup_ref, near, sem_c)
        first.start()
        for pair in copies:
            for copy in pair:
                copy.start()
        me = lax.axis_index("energy")
        ask.wait()
        picks = []
        for k in range(energies - 1):
            begin = pl.multiple_of(table[me ^ (k + 1), me] * rows, rows)
            picks.append(
                pltpu.make_async_copy(panel_ref.at[pl.ds(begin, span)], pieces[k], sem_p.at[k])
            )
            picks[k].start()
        first.wait()
        c = near[...]
        ct = c.astype(f32).T.astype(bf16)
        turn_ref[...] = ct
        for i in range(3):
            for k in range(2):
                copies[i][k].wait()
                held = corner[i, k]
                if i == 0:
                    held = dot(ct, held).astype(bf16)
                elif i == 1:
                    held = dot(held, c).astype(bf16)
                maps_ref[rows_of[i], rows_of[k]] = held
        for pick in picks:
            pick.wait()

    maps, coup_t, *pieces = call(
        own_maps,
        [(triple, bf16), ((layer, layer), bf16)] + [((span, width), bf16)] * (energies - 1),
        (far_green, far_coup, in_hbm(block_start), in_hbm(panel)),
        8 * layer**3,
        {k: pltpu.HBM for k in range(4)},
        [
            pltpu.VMEM((3, 2, layer, layer), bf16),
            pltpu.VMEM((layer, layer), bf16),
            pltpu.SMEM(block_start.shape, block_start.dtype),
            pltpu.SemaphoreType.DMA((3, 2)),
            pltpu.SemaphoreType.DMA,
            pltpu.SemaphoreType.DMA,
            pltpu.SemaphoreType.DMA((energies - 1,)),
        ],
    )
    received = [None] * (energies - 1)
    for mask in range(energies - 1, 0, -1):
        received[mask - 1] = swapped(pieces[mask - 1], "energy", mask)

    half = 3 * layer // 2
    final = levels - 1
    plans, members, totals = [], None, maps
    for level in range(final):
        near = swapped(totals if level == 0 else send, "slab", 1 << level)
        far = None if level == 0 else swapped(near, "slab", 1)
        closing = level == final - 1

        def group(*refs, level=level, closing=closing):
            refs = list(refs)
            mine, near_ref = refs[:2]
            plan, member, send_ref = refs[-3:]
            total = None if closing else refs[-4]
            after = place(level)
            if level == 0:
                theirs = near_ref[...]
            else:
                first = place(0)
                a, b = near_ref[...], refs[2][...]
                theirs = jnp.concatenate(
                    [jnp.where(first, b, a), jnp.where(first, a, b)], axis=0
                )
                old = refs[3]
            own_a, own_b, own_e = (mine[rows_of[k]] for k in range(3))
            its_a, its_b, its_e = (theirs[rows_of[k]] for k in range(3))
            a_left = jnp.where(after, its_a, own_a)
            a_right = jnp.where(after, own_a, its_a)
            b_left = jnp.where(after, its_b, own_b)
            b_right = jnp.where(after, own_b, its_b)
            e_left = jnp.where(after, its_e, own_e)
            e_right = jnp.where(after, own_e, its_e)
            plan[rows_of[0]] = a_right
            plan[rows_of[1]] = e_right
            if level:
                plan[rows_of[2]] = old[rows_of[0]]
                plan[rows_of[3]] = b_left
                plan[rows_of[4]] = jnp.where(after, old[rows_of[2]], old[rows_of[1]])
            else:
                plan[rows_of[2]] = b_left

            def reflected():
                bounce = mapped(e_right, a_left).astype(bf16)
                return bounce, (e_left.astype(f32) + mapped(b_left, bounce)).astype(bf16)

            def before():
                p = old[rows_of[0]]
                return jnp.where(after, mapped(p, a_left).astype(bf16), p)

            def behind():
                q = old[rows_of[1]]
                return jnp.where(after, q, mapped(q, b_right).astype(bf16))

            def turned_round(bounce):
                q, r = old[rows_of[1]], old[rows_of[2]]
                more = mapped(jnp.where(after, r, q), jnp.where(after, a_left, bounce))
                return jnp.where(after, more, more + r.astype(f32)).astype(bf16)

            if level == 0:
                bounce, e_total = reflected()
                row = lax.broadcasted_iota(jnp.int32, one_map, 0)
                col = lax.broadcasted_iota(jnp.int32, one_map, 1)
                unit = (row == col).astype(f32).astype(bf16)
                ends = (
                    jnp.where(after, a_left, unit),
                    jnp.where(after, unit, b_right),
                    jnp.where(after, jnp.zeros_like(bounce), bounce),
                )
            elif not closing:
                bounce, e_total = reflected()
                ends = (before(), behind(), turned_round(bounce))
            if not closing:
                grown = (
                    mapped(a_right, a_left).astype(bf16),
                    mapped(b_left, b_right).astype(bf16),
                    e_total,
                )
                for k in range(3):
                    total[rows_of[k]] = grown[k]
                whole = jnp.concatenate(grown, axis=0)
                send_ref[...] = jnp.where(place(0), whole[half:], whole[:half])
                for k, end in enumerate(ends):
                    member[rows_of[k]] = end
                return

            @pl.when(place(final))
            def _():
                bounce, e_total = reflected()
                member[rows_of[0]] = before()
                member[rows_of[1]] = turned_round(bounce)
                cut = layer // 2
                send_ref[...] = jnp.where(place(0), e_total[cut:], e_total[:cut])

            @pl.when(~place(final))
            def _():
                member[rows_of[0]] = jnp.zeros(one_map, bf16)
                member[rows_of[1]] = behind()
                send_ref[...] = jnp.zeros((layer // 2, 2 * layer), bf16)

        plan_size = (5 * layer if level else 3 * layer, 2 * layer)
        args = (totals, near) if level == 0 else (totals, near, far, members)
        *grown, plan, members, send = call(
            group,
            [(triple, bf16)] * (not closing)
            + [
                (plan_size, bf16),
                ((2 * layer, 2 * layer) if closing else triple, bf16),
                ((layer // 2 if closing else half, 2 * layer), bf16),
            ],
            args,
            64 * layer**3,
        )
        totals = None if closing else grown[0]
        plans.append(plan)
    e_near = swapped(send, "slab", 1 << final)
    e_far = swapped(e_near, "slab", 1)

    ways = (slice(0, layer), slice(layer, 2 * layer))
    pair = (2 * layer, width)

    def scan(vector):
        total, sent, reach = vector, vector, None
        for level in range(final):
            other = swapped(sent, "slab", 1 << level)
            closing = level == final - 1

            def step(*refs, level=level, closing=closing):
                mine, other_ref, plan = refs[:3]
                total_ref, sent_ref, reach_ref = refs[-3:]
                after = place(level)
                own = [mine[w] for w in ways]
                its = [other_ref[w].astype(f32) for w in ways]
                c_left, c_right = jnp.where(after, its[0], own[0]), jnp.where(after, own[0], its[0])
                f_left, f_right = jnp.where(after, its[1], own[1]), jnp.where(after, own[1], its[1])
                spread = mapped(plan[: (3 if level else 2) * layer], c_left)
                back = f_right + spread[ways[1]]
                c_new = c_right + spread[ways[0]]
                f_new = f_left + mapped(plan[rows_of[3 if level else 2]], back)
                if level:
                    so_far = refs[3]
                    more = mapped(plan[rows_of[4]], jnp.where(after, c_left, back))
                    z = so_far[ways[0]] + jnp.where(after, spread[rows_of[2]], 0.0)
                    u = so_far[ways[1]] + more
                else:
                    z = jnp.where(after, c_left, jnp.zeros_like(c_left))
                    u = jnp.where(after, jnp.zeros_like(back), back)
                reach_ref[ways[0]] = z
                reach_ref[ways[1]] = u
                if closing:
                    total_ref[...] = c_new
                    sent_ref[...] = jnp.where(place(final), f_new, c_new).astype(bf16)
                else:
                    total_ref[ways[0]] = c_new
                    total_ref[ways[1]] = f_new
                    sent_ref[ways[0]] = c_new.astype(bf16)
                    sent_ref[ways[1]] = f_new.astype(bf16)

            size = (layer, width) if closing else pair
            args = (total, other, plans[level]) + ((reach,) if level else ())
            total, sent, reach = call(
                step, [(size, f32), (size, bf16), (pair, f32)], args, 40 * layer * layer * width
            )
        return total, swapped(sent, "slab", 1 << final), reach

    def fetch(green_ref, held_ref, sem, spots):
        copies = [
            pltpu.make_async_copy(green_ref.at[k, r], held_ref.at[k, i], sem.at[i, k])
            for i, r in enumerate(spots)
            for k in range(2)
        ]
        for copy in copies:
            copy.start()
        return copies

    def prepare(
        green_ref, inj_ref, panel_ref, start_ref, count_ref, strength_ref,
        ends_ref, acc_ref, weight_ref, sem,
    ):
        copies = fetch(green_ref, ends_ref, sem, (pl.ds(0, layer), pl.ds(low, layer)))
        me = lax.axis_index("energy")
        row = lax.broadcasted_iota(jnp.int32, (span, width), 0)
        acc_ref[...] = inj_ref[...].astype(f32)
        for k in range(energies):
            s = me ^ k
            weight = jnp.where(row < count_ref[me, s] * rows, strength_ref[me, s], 0.0)
            if k:
                weight_ref[k - 1] = weight
            else:
                first = pl.multiple_of(start_ref[me, me] * rows, rows)
                part = pl.ds(first, span)
                acc_ref[part] = acc_ref[part] + panel_ref[part].astype(f32) * weight
        for copy in copies:
            copy.wait()

    ends, acc, weights = call(
        prepare,
        [
            ((2, 2, layer, norb), bf16),
            ((norb, width), f32),
            ((energies - 1, span, width), f32),
        ],
        (far_green, injection[0, 0], panel, block_start, block_count, strength),
        0,
        {0: pltpu.HBM, 3: SMEM, 4: SMEM, 5: SMEM},
        [pltpu.SemaphoreType.DMA((2, 2))],
    )

    def load(start_ref, acc_ref, weight_ref, ends_ref, turn_ref, *refs):
        got, (source_ref, spun_ref, low_ref, sent_ref, sum_ref) = refs[:-5], refs[-5:]
        me = lax.axis_index("energy")
        sum_ref[...] = acc_ref[...]
        for k in range(1, energies):
            first = pl.multiple_of(start_ref[me, me ^ k] * rows, rows)
            part = pl.ds(first, span)
            sum_ref[part] = sum_ref[part] + got[k - 1][...].astype(f32) * weight_ref[k - 1]
        source = sum_ref[...].astype(bf16)
        spun = turned(source.astype(f32)).astype(bf16)
        source_ref[...] = source
        spun_ref[...] = spun
        direct = dot(ends_ref[0, 1], source) + dot(ends_ref[1, 1], spun)
        low_ref[...] = direct
        sent_ref[ways[0]] = fine(turn_ref[...], direct)
        sent_ref[ways[1]] = dot(ends_ref[0, 0], source) + dot(ends_ref[1, 0], spun)

    source, spun, direct_low, sent = call(
        load,
        [((norb, width), bf16)] * 2 + [((layer, width), f32), (pair, f32)],
        (block_start, acc, weights, ends, coup_t, *received),
        8 * layer * norb * width,
        {0: SMEM},
        [pltpu.VMEM((norb, width), f32)],
    )
    c_total, arrived, reach = scan(sent)

    blocks = (low - layer) // layer

    def fetch_mid(green_ref, hint_ref, mid_ref, sem):
        spots = [pl.ds((i + 1) * layer, layer) for i in range(blocks)]
        for copy in fetch(green_ref, mid_ref, sem, spots):
            copy.wait()

    (mid,) = call(
        fetch_mid,
        [((2, blocks, layer, norb), bf16)],
        (far_green, direct_low),
        0,
        {0: pltpu.HBM, 1: pl.ANY},
        [pltpu.SemaphoreType.DMA((blocks, 2))],
    )

    def direct_step(mid_ref, source_ref, spun_ref, out_ref):
        for i in range(blocks):
            out_ref[i] = dot(mid_ref[0, i], source_ref[...]) + dot(mid_ref[1, i], spun_ref[...])

    (direct_mid,) = call(
        direct_step,
        [((blocks, layer, width), f32)],
        (mid, source, spun),
        4 * (low - layer) * norb * width,
    )

    def finish(
        other_ref, c_ref, near_ref, far_ref, member, reach_ref, ends_ref, mid_ref, coup_ref,
        sent_ref, low_ref, direct_ref, out_ref, kept, sem,
    ):
        after, first = place(final), place(0)
        other = other_ref[...].astype(f32)
        c_left = c_ref[...]
        a, b = mapped(near_ref[...], c_left), mapped(far_ref[...], c_left)
        bounce = jnp.concatenate([jnp.where(first, b, a), jnp.where(first, a, b)], axis=0)
        back = other + jnp.where(after, jnp.zeros_like(bounce), bounce)
        more = mapped(member[ways[0]], other)
        z = reach_ref[ways[0]] + jnp.where(after, more, jnp.zeros_like(more))
        incoming = z.astype(bf16)
        spun_z = turned(incoming.astype(f32)).astype(bf16)
        u = reach_ref[ways[1]] + mapped(member[ways[1]], back)
        outgoing = fine(coup_ref[...], u).astype(bf16)
        spun_u = turned(outgoing.astype(f32)).astype(bf16)
        copies = []
        tail = slice(low, norb)
        for i in range(blocks + 2):
            if i == 0:
                direct, held = sent_ref[ways[1]], [ends_ref.at[k, 0] for k in range(2)]
            elif i > blocks:
                direct, held = low_ref[...], [ends_ref.at[k, 1] for k in range(2)]
            else:
                direct, held = direct_ref[i - 1], [mid_ref.at[k, i - 1] for k in range(2)]
            part = pl.ds(i * layer, layer)
            kept[part] = (
                direct
                + dot(held[0][:, :layer], incoming)
                + dot(held[1][:, :layer], spun_z)
                + dot(held[0][:, tail], outgoing)
                + dot(held[1][:, tail], spun_u)
            ).astype(bf16)
            copy = pltpu.make_async_copy(kept.at[part], out_ref.at[part], sem.at[i])
            copy.start()
            copies.append(copy)
        for copy in copies:
            copy.wait()

    (out,) = call(
        finish,
        [((norb, width), bf16)],
        (
            arrived, c_total, e_near, e_far, members, reach, ends, mid, coup,
            sent, direct_low, direct_mid,
        ),
        16 * norb * layer * width,
        scratch=[pltpu.VMEM((norb, width), bf16), pltpu.SemaphoreType.DMA((norb // layer,))],
        out_space=pltpu.HBM,
    )
    return out[None, None]


def solution(mesh):
    in_specs = (
        P("energy", "slab", None, None, None),
        P("energy", "slab", None, None),
        P("energy", "slab", None, None),
        P("slab", None, None),
        P(),
        P(),
        P(),
    )
    out_specs = P("energy", "slab", None, None)
    return jax.shard_map(body, mesh=mesh, in_specs=in_specs, out_specs=out_specs, check_vma=False)
```

```python
import math

import jax
import jax.numpy as jnp
from jax import lax
from jax.experimental import pallas as pl
from jax.experimental.pallas import tpu as pltpu
from jax.sharding import PartitionSpec as P


NBLK = 16
CAP = 4
VMEM_BYTES = 67043328
bf16 = jnp.bfloat16
f32 = jnp.float32
VMEM = pltpu.VMEM


def swapped(block, axis, mask):
    count = lax.axis_size(axis)
    return lax.ppermute(block, axis, [(i, i ^ mask) for i in range(count)])


def dot(a, b):
    return jnp.dot(a, b, preferred_element_type=f32)


def turned(v):
    half = v.shape[1] // 2
    if half % 128 == 0:
        return jnp.concatenate([-v[:, half:], v[:, :half]], axis=1)
    lane = lax.broadcasted_iota(jnp.int32, v.shape, 1)
    moved = pltpu.roll(v, half, 1)
    return jnp.where(lane < half, -moved, moved)


def applied(real, imag, v):
    v = v.astype(f32)
    return dot(real, v.astype(bf16)) + dot(imag, turned(v).astype(bf16))


def mapped(wide, v):
    side = wide.shape[1] // 2
    return applied(wide[:, :side], wide[:, side:], v)


def fine(real, v):
    high = v.astype(bf16)
    return dot(real, high) + dot(real, (v - high.astype(f32)).astype(bf16))


def member_before(after, p, a_left):
    return jnp.where(after, mapped(p, a_left).astype(bf16), p)


def member_behind(after, q, b_right):
    return jnp.where(after, q, mapped(q, b_right).astype(bf16))


def member_turned(after, q, r, a_left, bounce):
    more = mapped(jnp.where(after, r, q), jnp.where(after, a_left, bounce))
    return jnp.where(after, more, more + r.astype(f32)).astype(bf16)


def place(k):
    return ((lax.axis_index("slab") >> k) & 1) == 1


def call(kernel, outs, args, flops, spaces=None, scratch=(), out_space=VMEM, spare=None):
    spaces = spaces or {}
    specs = [pl.BlockSpec(memory_space=spaces.get(i, VMEM)) for i in range(len(args))]
    moved = sum(a.size * a.dtype.itemsize for a in args)
    kept = sum(math.prod(s) * jnp.dtype(t).itemsize for s, t in outs)
    kept += sum(a.size * a.dtype.itemsize for i, a in enumerate(args) if i not in spaces)
    limit = kept + (4 << 20) if spare is None else VMEM_BYTES - spare
    shapes = [jax.ShapeDtypeStruct(s, t) for s, t in outs]
    return pl.pallas_call(
        kernel,
        out_shape=shapes,
        in_specs=specs,
        out_specs=[pl.BlockSpec(memory_space=out_space)] * len(shapes),
        scratch_shapes=list(scratch),
        compiler_params=pltpu.CompilerParams(vmem_limit_bytes=limit),
        cost_estimate=pl.CostEstimate(
            flops=flops, bytes_accessed=moved, transcendentals=0
        ),
    )(*args)


def in_hbm(array):
    return pltpu.with_memory_space_constraint(array, pltpu.HBM)


def body(pivots, injection, previous, coupling, strength, block_start, block_count):
    green = pivots[0, 0]
    norb = green.shape[1]
    layer = coupling.shape[1]
    width = injection.shape[3]
    rows = norb // NBLK
    span = rows * CAP
    far_green = in_hbm(green)
    coup = coupling[0]
    far_coup = in_hbm(coup)
    panel = previous[0, 0]
    energies = lax.axis_size("energy")
    slabs = lax.axis_size("slab")
    levels = slabs.bit_length() - 1
    low = norb - layer
    SMEM = pltpu.SMEM

    rows_of = [slice(k * layer, (k + 1) * layer) for k in range(6)]
    triple, one_map = (3 * layer, 2 * layer), (layer, 2 * layer)

    def own_maps(green_ref, coup_ref, start_ref, panel_ref, *refs):
        maps_ref, turn_ref = refs[:2]
        pieces = refs[2 : energies + 1]
        corner, near, whole, table, sem, sem_c, sem_t, sem_p = refs[energies + 1 :]
        ask = pltpu.make_async_copy(start_ref, table, sem_t)
        panel_copy = pltpu.make_async_copy(panel_ref, whole, sem_p)
        first = pltpu.make_async_copy(coup_ref, near, sem_c)
        top, end = pl.ds(0, layer), pl.ds(low, layer)
        copies = [
            [
                pltpu.make_async_copy(green_ref.at[k, r, c], corner.at[i, k], sem.at[i, k])
                for k in range(2)
            ]
            for i, (r, c) in enumerate(((end, top), (top, end), (top, top)))
        ]
        ask.start()
        first.start()
        panel_copy.start()
        for pair in copies:
            for copy in pair:
                copy.start()
        me = lax.axis_index("energy")
        first.wait()
        c = near[...]
        ct = c.astype(f32).T.astype(bf16)
        turn_ref[...] = ct
        panel_copy.wait()
        ask.wait()
        for k in range(energies - 1):
            begin = pl.multiple_of(table[me ^ (k + 1), me] * rows, rows)
            pieces[k][...] = whole[pl.ds(begin, span)]
        for i in range(3):
            for k in range(2):
                copies[i][k].wait()
                held = corner[i, k]
                if i == 0:
                    held = dot(ct, held).astype(bf16)
                elif i == 1:
                    held = dot(held, c).astype(bf16)
                maps_ref[rows_of[i], rows_of[k]] = held

    maps, coup_t, *pieces = call(
        own_maps,
        [(triple, bf16), ((layer, layer), bf16)] + [((span, width), bf16)] * (energies - 1),
        (far_green, far_coup, in_hbm(block_start), in_hbm(panel)),
        8 * layer**3,
        {k: pltpu.HBM for k in range(4)},
        [
            pltpu.VMEM((3, 2, layer, layer), bf16),
            pltpu.VMEM((layer, layer), bf16),
            pltpu.VMEM(panel.shape, bf16),
            pltpu.SMEM(block_start.shape, block_start.dtype),
            pltpu.SemaphoreType.DMA((3, 2)),
            pltpu.SemaphoreType.DMA,
            pltpu.SemaphoreType.DMA,
            pltpu.SemaphoreType.DMA,
        ],
    )
    received = [None] * (energies - 1)
    for mask in range(energies - 1, 0, -1):
        received[mask - 1] = swapped(pieces[mask - 1], "energy", mask)

    half = 3 * layer // 2
    final = levels - 1
    plans, members, totals = [], None, maps
    for level in range(final):
        near = swapped(totals if level == 0 else send, "slab", 1 << level)
        far = None if level == 0 else swapped(near, "slab", 1)
        closing = level == final - 1

        def group(*refs, level=level, closing=closing):
            refs = list(refs)
            mine, near_ref = refs[:2]
            plan, member, send_ref = refs[-3:]
            total = None if closing else refs[-4]
            after = place(level)
            if level == 0:
                theirs = near_ref[...]
            else:
                first = place(0)
                a, b = near_ref[...], refs[2][...]
                theirs = jnp.concatenate(
                    [jnp.where(first, b, a), jnp.where(first, a, b)], axis=0
                )
                old = refs[3]
            own_a, own_b, own_e = (mine[rows_of[k]] for k in range(3))
            its_a, its_b, its_e = (theirs[rows_of[k]] for k in range(3))
            a_left = jnp.where(after, its_a, own_a)
            a_right = jnp.where(after, own_a, its_a)
            b_left = jnp.where(after, its_b, own_b)
            b_right = jnp.where(after, own_b, its_b)
            e_left = jnp.where(after, its_e, own_e)
            e_right = jnp.where(after, own_e, its_e)
            plan[rows_of[0]] = a_right
            plan[rows_of[1]] = e_right
            if level:
                plan[rows_of[2]] = old[rows_of[0]]
                plan[rows_of[3]] = b_left
                plan[rows_of[4]] = jnp.where(after, old[rows_of[2]], old[rows_of[1]])
            else:
                plan[rows_of[2]] = b_left

            def reflected():
                bounce = mapped(e_right, a_left).astype(bf16)
                return bounce, (e_left.astype(f32) + mapped(b_left, bounce)).astype(bf16)

            if level == 0:
                bounce, e_total = reflected()
                row = lax.broadcasted_iota(jnp.int32, one_map, 0)
                col = lax.broadcasted_iota(jnp.int32, one_map, 1)
                unit = (row == col).astype(f32).astype(bf16)
                ends = (
                    jnp.where(after, a_left, unit),
                    jnp.where(after, unit, b_right),
                    jnp.where(after, jnp.zeros_like(bounce), bounce),
                )
            elif not closing:
                bounce, e_total = reflected()
                q, r = old[rows_of[1]], old[rows_of[2]]
                ends = (
                    member_before(after, old[rows_of[0]], a_left),
                    member_behind(after, q, b_right),
                    member_turned(after, q, r, a_left, bounce),
                )
            if not closing:
                grown = (
                    mapped(a_right, a_left).astype(bf16),
                    mapped(b_left, b_right).astype(bf16),
                    e_total,
                )
                for k in range(3):
                    total[rows_of[k]] = grown[k]
                whole = jnp.concatenate(grown, axis=0)
                send_ref[...] = jnp.where(place(0), whole[half:], whole[:half])
                for k, end in enumerate(ends):
                    member[rows_of[k]] = end
                return

            @pl.when(place(final))
            def _():
                bounce, e_total = reflected()
                member[...] = bounce
                cut = layer // 2
                send_ref[...] = jnp.where(place(0), e_total[cut:], e_total[:cut])

            @pl.when(~place(final))
            def _():
                member[...] = jnp.zeros(one_map, bf16)
                send_ref[...] = jnp.zeros((layer // 2, 2 * layer), bf16)

        plan_size = (5 * layer if level else 3 * layer, 2 * layer)
        args = (totals, near) if level == 0 else (totals, near, far, members)
        *grown, plan, member, send = call(
            group,
            [(triple, bf16)] * (not closing)
            + [
                (plan_size, bf16),
                (one_map if closing else triple, bf16),
                ((layer // 2 if closing else half, 2 * layer), bf16),
            ],
            args,
            64 * layer**3,
        )
        plans.append(plan)
        if not closing:
            totals, members = grown[0], member

    def last_ends(mine, near_ref, far_ref, old, bounce_ref, hint_ref, out_ref):
        after, first = place(final - 1), place(0)

        @pl.when(place(final))
        def _():
            its_a = jnp.where(first, far_ref[:layer], near_ref[:layer])
            a_left = jnp.where(after, its_a, mine[rows_of[0]])
            out_ref[rows_of[0]] = member_before(after, old[rows_of[0]], a_left)
            out_ref[rows_of[1]] = member_turned(
                after, old[rows_of[1]], old[rows_of[2]], a_left, bounce_ref[...]
            )

        @pl.when(~place(final))
        def _():
            a, b = near_ref[...], far_ref[...]
            theirs = jnp.concatenate([jnp.where(first, b, a), jnp.where(first, a, b)], axis=0)
            b_right = jnp.where(after, mine[rows_of[1]], theirs[rows_of[1]])
            out_ref[rows_of[0]] = jnp.zeros(one_map, bf16)
            out_ref[rows_of[1]] = member_behind(after, old[rows_of[1]], b_right)

    e_near = swapped(send, "slab", 1 << final)
    e_far = swapped(e_near, "slab", 1)

    (ends_last,) = call(
        last_ends,
        [((2 * layer, 2 * layer), bf16)],
        (totals, near, far, members, member, send),
        64 * layer**3,
        {5: pl.ANY},
    )

    ways = (slice(0, layer), slice(layer, 2 * layer))
    pair = (2 * layer, width)

    def scan(vector):
        total, sent, reach = vector, vector, None
        for level in range(final):
            other = swapped(sent, "slab", 1 << level)
            closing = level == final - 1

            def step(*refs, level=level, closing=closing):
                mine, other_ref, plan = refs[:3]
                total_ref, sent_ref, reach_ref = refs[-3:]
                after = place(level)
                own = [mine[w] for w in ways]
                its = [other_ref[w].astype(f32) for w in ways]
                c_left, c_right = jnp.where(after, its[0], own[0]), jnp.where(after, own[0], its[0])
                f_left, f_right = jnp.where(after, its[1], own[1]), jnp.where(after, own[1], its[1])
                spread = mapped(plan[: (3 if level else 2) * layer], c_left)
                back = f_right + spread[ways[1]]
                c_new = c_right + spread[ways[0]]
                f_new = f_left + mapped(plan[rows_of[3 if level else 2]], back)
                if level:
                    so_far = refs[3]
                    more = mapped(plan[rows_of[4]], jnp.where(after, c_left, back))
                    z = so_far[ways[0]] + jnp.where(after, spread[rows_of[2]], 0.0)
                    u = so_far[ways[1]] + more
                else:
                    z = jnp.where(after, c_left, jnp.zeros_like(c_left))
                    u = jnp.where(after, jnp.zeros_like(back), back)
                reach_ref[ways[0]] = z
                reach_ref[ways[1]] = u
                if closing:
                    total_ref[...] = c_new
                    sent_ref[...] = jnp.where(place(final), f_new, c_new).astype(bf16)
                else:
                    total_ref[ways[0]] = c_new
                    total_ref[ways[1]] = f_new
                    sent_ref[ways[0]] = c_new.astype(bf16)
                    sent_ref[ways[1]] = f_new.astype(bf16)

            size = (layer, width) if closing else pair
            args = (total, other, plans[level]) + ((reach,) if level else ())
            total, sent, reach = call(
                step, [(size, f32), (size, bf16), (pair, f32)], args, 40 * layer * layer * width
            )
        return total, swapped(sent, "slab", 1 << final), reach

    def fetch(green_ref, held_ref, sem, spots):
        copies = [
            pltpu.make_async_copy(green_ref.at[k, r], held_ref.at[k, i], sem.at[i, k])
            for i, r in enumerate(spots)
            for k in range(2)
        ]
        for copy in copies:
            copy.start()
        return copies

    def prepare(
        green_ref, inj_ref, panel_ref, start_ref, count_ref, strength_ref,
        ends_ref, acc_ref, weight_ref, sem,
    ):
        copies = fetch(green_ref, ends_ref, sem, (pl.ds(0, layer), pl.ds(low, layer)))
        me = lax.axis_index("energy")
        row = lax.broadcasted_iota(jnp.int32, (span, width), 0)
        acc_ref[...] = inj_ref[...].astype(f32)
        for k in range(energies):
            s = me ^ k
            weight = jnp.where(row < count_ref[me, s] * rows, strength_ref[me, s], 0.0)
            if k:
                weight_ref[k - 1] = weight
            else:
                first = pl.multiple_of(start_ref[me, me] * rows, rows)
                part = pl.ds(first, span)
                acc_ref[part] = acc_ref[part] + panel_ref[part].astype(f32) * weight
        for copy in copies:
            copy.wait()

    ends, acc, weights = call(
        prepare,
        [
            ((2, 2, layer, norb), bf16),
            ((norb, width), f32),
            ((energies - 1, span, width), f32),
        ],
        (far_green, injection[0, 0], panel, block_start, block_count, strength),
        0,
        {0: pltpu.HBM, 3: SMEM, 4: SMEM, 5: SMEM},
        [pltpu.SemaphoreType.DMA((2, 2))],
    )

    def load(start_ref, acc_ref, weight_ref, ends_ref, turn_ref, *refs):
        got, (source_ref, spun_ref, low_ref, sent_ref, sum_ref) = refs[:-5], refs[-5:]
        me = lax.axis_index("energy")
        sum_ref[...] = acc_ref[...]
        for k in range(1, energies):
            first = pl.multiple_of(start_ref[me, me ^ k] * rows, rows)
            part = pl.ds(first, span)
            sum_ref[part] = sum_ref[part] + got[k - 1][...].astype(f32) * weight_ref[k - 1]
        source = sum_ref[...].astype(bf16)
        spun = turned(source.astype(f32)).astype(bf16)
        source_ref[...] = source
        spun_ref[...] = spun
        direct = dot(ends_ref[0, 1], source) + dot(ends_ref[1, 1], spun)
        low_ref[...] = direct
        sent_ref[ways[0]] = fine(turn_ref[...], direct)
        sent_ref[ways[1]] = dot(ends_ref[0, 0], source) + dot(ends_ref[1, 0], spun)

    source, spun, direct_low, sent = call(
        load,
        [((norb, width), bf16)] * 2 + [((layer, width), f32), (pair, f32)],
        (block_start, acc, weights, ends, coup_t, *received),
        8 * layer * norb * width,
        {0: SMEM},
        [pltpu.VMEM((norb, width), f32)],
    )
    c_total, arrived, reach = scan(sent)

    blocks = (low - layer) // layer

    def fetch_mid(green_ref, hint_ref, mid_ref, sem):
        spots = [pl.ds((i + 1) * layer, layer) for i in range(blocks)]
        for copy in fetch(green_ref, mid_ref, sem, spots):
            copy.wait()

    (mid,) = call(
        fetch_mid,
        [((2, blocks, layer, norb), bf16)],
        (far_green, direct_low),
        0,
        {0: pltpu.HBM, 1: pl.ANY},
        [pltpu.SemaphoreType.DMA((blocks, 2))],
    )

    def direct_step(mid_ref, source_ref, spun_ref, out_ref):
        for i in range(blocks):
            out_ref[i] = dot(mid_ref[0, i], source_ref[...]) + dot(mid_ref[1, i], spun_ref[...])

    (direct_mid,) = call(
        direct_step,
        [((blocks, layer, width), f32)],
        (mid, source, spun),
        4 * (low - layer) * norb * width,
    )

    def finish(
        other_ref, c_ref, near_ref, far_ref, member, reach_ref, ends_ref, mid_ref, coup_ref,
        sent_ref, low_ref, direct_ref, out_ref, kept, sem,
    ):
        after, first = place(final), place(0)
        other = other_ref[...].astype(f32)
        c_left = c_ref[...]
        a, b = mapped(near_ref[...], c_left), mapped(far_ref[...], c_left)
        bounce = jnp.concatenate([jnp.where(first, b, a), jnp.where(first, a, b)], axis=0)
        back = other + jnp.where(after, jnp.zeros_like(bounce), bounce)
        more = mapped(member[ways[0]], other)
        z = reach_ref[ways[0]] + jnp.where(after, more, jnp.zeros_like(more))
        incoming = z.astype(bf16)
        spun_z = turned(incoming.astype(f32)).astype(bf16)
        u = reach_ref[ways[1]] + mapped(member[ways[1]], back)
        outgoing = fine(coup_ref[...], u).astype(bf16)
        spun_u = turned(outgoing.astype(f32)).astype(bf16)
        copies = []
        tail = slice(low, norb)
        for i in range(blocks + 2):
            if i == 0:
                direct, held = sent_ref[ways[1]], [ends_ref.at[k, 0] for k in range(2)]
            elif i > blocks:
                direct, held = low_ref[...], [ends_ref.at[k, 1] for k in range(2)]
            else:
                direct, held = direct_ref[i - 1], [mid_ref.at[k, i - 1] for k in range(2)]
            part = pl.ds(i * layer, layer)
            kept[part] = (
                direct
                + dot(held[0][:, :layer], incoming)
                + dot(held[1][:, :layer], spun_z)
                + dot(held[0][:, tail], outgoing)
                + dot(held[1][:, tail], spun_u)
            ).astype(bf16)
            copy = pltpu.make_async_copy(kept.at[part], out_ref.at[part], sem.at[i])
            copy.start()
            copies.append(copy)
        for copy in copies:
            copy.wait()

    (out,) = call(
        finish,
        [((norb, width), bf16)],
        (
            arrived, c_total, e_near, e_far, ends_last, reach, ends, mid, coup,
            sent, direct_low, direct_mid,
        ),
        16 * norb * layer * width,
        scratch=[pltpu.VMEM((norb, width), bf16), pltpu.SemaphoreType.DMA((norb // layer,))],
        out_space=pltpu.HBM,
    )
    return out[None, None]


def solution(mesh):
    in_specs = (
        P("energy", "slab", None, None, None),
        P("energy", "slab", None, None),
        P("energy", "slab", None, None),
        P("slab", None, None),
        P(),
        P(),
        P(),
    )
    out_specs = P("energy", "slab", None, None)
    return jax.shard_map(body, mesh=mesh, in_specs=in_specs, out_specs=out_specs, check_vma=False)
```

```python
import math

import jax
import jax.numpy as jnp
from jax import lax
from jax.experimental import pallas as pl
from jax.experimental.pallas import tpu as pltpu
from jax.sharding import PartitionSpec as P


NBLK = 16
CAP = 4
VMEM_BYTES = 67043328
bf16 = jnp.bfloat16
f32 = jnp.float32
VMEM = pltpu.VMEM


def swapped(block, axis, mask):
    count = lax.axis_size(axis)
    return lax.ppermute(block, axis, [(i, i ^ mask) for i in range(count)])


def dot(a, b):
    return jnp.dot(a, b, preferred_element_type=f32)


def turned(v):
    half = v.shape[1] // 2
    if half % 128 == 0:
        return jnp.concatenate([-v[:, half:], v[:, :half]], axis=1)
    lane = lax.broadcasted_iota(jnp.int32, v.shape, 1)
    moved = pltpu.roll(v, half, 1)
    return jnp.where(lane < half, -moved, moved)


def applied(real, imag, v):
    v = v.astype(f32)
    return dot(real, v.astype(bf16)) + dot(imag, turned(v).astype(bf16))


def mapped(wide, v):
    side = wide.shape[1] // 2
    return applied(wide[:, :side], wide[:, side:], v)


def fine(real, v):
    high = v.astype(bf16)
    return dot(real, high) + dot(real, (v - high.astype(f32)).astype(bf16))


def member_before(after, p, a_left):
    return jnp.where(after, mapped(p, a_left).astype(bf16), p)


def member_behind(after, q, b_right):
    return jnp.where(after, q, mapped(q, b_right).astype(bf16))


def member_turned(after, q, r, a_left, bounce):
    more = mapped(jnp.where(after, r, q), jnp.where(after, a_left, bounce))
    return jnp.where(after, more, more + r.astype(f32)).astype(bf16)


def place(k):
    return ((lax.axis_index("slab") >> k) & 1) == 1


def call(kernel, outs, args, flops, spaces=None, scratch=(), out_space=VMEM, spare=None):
    spaces = spaces or {}
    specs = [pl.BlockSpec(memory_space=spaces.get(i, VMEM)) for i in range(len(args))]
    moved = sum(a.size * a.dtype.itemsize for a in args)
    kept = sum(math.prod(s) * jnp.dtype(t).itemsize for s, t in outs)
    kept += sum(a.size * a.dtype.itemsize for i, a in enumerate(args) if i not in spaces)
    limit = kept + (4 << 20) if spare is None else VMEM_BYTES - spare
    shapes = [jax.ShapeDtypeStruct(s, t) for s, t in outs]
    return pl.pallas_call(
        kernel,
        out_shape=shapes,
        in_specs=specs,
        out_specs=[pl.BlockSpec(memory_space=out_space)] * len(shapes),
        scratch_shapes=list(scratch),
        compiler_params=pltpu.CompilerParams(vmem_limit_bytes=limit),
        cost_estimate=pl.CostEstimate(
            flops=flops, bytes_accessed=moved, transcendentals=0
        ),
    )(*args)


def in_hbm(array):
    return pltpu.with_memory_space_constraint(array, pltpu.HBM)


def body(pivots, injection, previous, coupling, strength, block_start, block_count):
    green = pivots[0, 0]
    norb = green.shape[1]
    layer = coupling.shape[1]
    width = injection.shape[3]
    rows = norb // NBLK
    span = rows * CAP
    far_green = in_hbm(green)
    coup = coupling[0]
    far_coup = in_hbm(coup)
    panel = previous[0, 0]
    energies = lax.axis_size("energy")
    slabs = lax.axis_size("slab")
    levels = slabs.bit_length() - 1
    low = norb - layer
    SMEM = pltpu.SMEM

    rows_of = [slice(k * layer, (k + 1) * layer) for k in range(6)]
    triple, one_map = (3 * layer, 2 * layer), (layer, 2 * layer)

    def own_maps(green_ref, coup_ref, start_ref, panel_ref, *refs):
        maps_ref, turn_ref = refs[:2]
        pieces = refs[2 : energies + 1]
        corner, near, whole, table, sem, sem_c, sem_t, sem_p = refs[energies + 1 :]
        ask = pltpu.make_async_copy(start_ref, table, sem_t)
        panel_copy = pltpu.make_async_copy(panel_ref, whole, sem_p)
        first = pltpu.make_async_copy(coup_ref, near, sem_c)
        top, end = pl.ds(0, layer), pl.ds(low, layer)
        copies = [
            [
                pltpu.make_async_copy(green_ref.at[k, r, c], corner.at[i, k], sem.at[i, k])
                for k in range(2)
            ]
            for i, (r, c) in enumerate(((end, top), (top, end), (top, top)))
        ]
        ask.start()
        first.start()
        panel_copy.start()
        for pair in copies:
            for copy in pair:
                copy.start()
        me = lax.axis_index("energy")
        first.wait()
        c = near[...]
        ct = c.astype(f32).T.astype(bf16)
        turn_ref[...] = ct
        panel_copy.wait()
        ask.wait()
        for k in range(energies - 1):
            begin = pl.multiple_of(table[me ^ (k + 1), me] * rows, rows)
            pieces[k][...] = whole[pl.ds(begin, span)]
        for i in range(3):
            for k in range(2):
                copies[i][k].wait()
                held = corner[i, k]
                if i == 0:
                    held = dot(ct, held).astype(bf16)
                elif i == 1:
                    held = dot(held, c).astype(bf16)
                maps_ref[rows_of[i], rows_of[k]] = held

    maps, coup_t, *pieces = call(
        own_maps,
        [(triple, bf16), ((layer, layer), bf16)] + [((span, width), bf16)] * (energies - 1),
        (far_green, far_coup, in_hbm(block_start), in_hbm(panel)),
        8 * layer**3,
        {k: pltpu.HBM for k in range(4)},
        [
            pltpu.VMEM((3, 2, layer, layer), bf16),
            pltpu.VMEM((layer, layer), bf16),
            pltpu.VMEM(panel.shape, bf16),
            pltpu.SMEM(block_start.shape, block_start.dtype),
            pltpu.SemaphoreType.DMA((3, 2)),
            pltpu.SemaphoreType.DMA,
            pltpu.SemaphoreType.DMA,
            pltpu.SemaphoreType.DMA,
        ],
    )
    received = [None] * (energies - 1)
    for mask in range(energies - 1, 0, -1):
        received[mask - 1] = swapped(pieces[mask - 1], "energy", mask)

    half = 3 * layer // 2
    final = levels - 1
    plans, members, totals = [], None, maps
    for level in range(final):
        near = swapped(totals if level == 0 else send, "slab", 1 << level)
        far = None if level == 0 else swapped(near, "slab", 1)
        closing = level == final - 1

        def group(*refs, level=level, closing=closing):
            refs = list(refs)
            mine, near_ref = refs[:2]
            plan, member, send_ref = refs[-3:]
            total = None if closing else refs[-4]
            after = place(level)
            if level == 0:
                theirs = near_ref[...]
            else:
                first = place(0)
                a, b = near_ref[...], refs[2][...]
                theirs = jnp.concatenate(
                    [jnp.where(first, b, a), jnp.where(first, a, b)], axis=0
                )
                old = refs[3]
            own_a, own_b, own_e = (mine[rows_of[k]] for k in range(3))
            its_a, its_b, its_e = (theirs[rows_of[k]] for k in range(3))
            a_left = jnp.where(after, its_a, own_a)
            a_right = jnp.where(after, own_a, its_a)
            b_left = jnp.where(after, its_b, own_b)
            b_right = jnp.where(after, own_b, its_b)
            e_left = jnp.where(after, its_e, own_e)
            e_right = jnp.where(after, own_e, its_e)
            plan[rows_of[0]] = a_right
            plan[rows_of[1]] = e_right
            if level:
                plan[rows_of[2]] = old[rows_of[0]]
                plan[rows_of[3]] = b_left
                plan[rows_of[4]] = jnp.where(after, old[rows_of[2]], old[rows_of[1]])
            else:
                plan[rows_of[2]] = b_left

            def reflected():
                bounce = mapped(e_right, a_left).astype(bf16)
                return bounce, (e_left.astype(f32) + mapped(b_left, bounce)).astype(bf16)

            if level == 0:
                bounce, e_total = reflected()
                row = lax.broadcasted_iota(jnp.int32, one_map, 0)
                col = lax.broadcasted_iota(jnp.int32, one_map, 1)
                unit = (row == col).astype(f32).astype(bf16)
                ends = (
                    jnp.where(after, a_left, unit),
                    jnp.where(after, unit, b_right),
                    jnp.where(after, jnp.zeros_like(bounce), bounce),
                )
            elif not closing:
                bounce, e_total = reflected()
                q, r = old[rows_of[1]], old[rows_of[2]]
                ends = (
                    member_before(after, old[rows_of[0]], a_left),
                    member_behind(after, q, b_right),
                    member_turned(after, q, r, a_left, bounce),
                )
            if not closing:
                grown = (
                    mapped(a_right, a_left).astype(bf16),
                    mapped(b_left, b_right).astype(bf16),
                    e_total,
                )
                for k in range(3):
                    total[rows_of[k]] = grown[k]
                whole = jnp.concatenate(grown, axis=0)
                send_ref[...] = jnp.where(place(0), whole[half:], whole[:half])
                for k, end in enumerate(ends):
                    member[rows_of[k]] = end
                return

            @pl.when(place(final))
            def _():
                bounce, e_total = reflected()
                member[...] = bounce
                cut = layer // 2
                send_ref[...] = jnp.where(place(0), e_total[cut:], e_total[:cut])

            @pl.when(~place(final))
            def _():
                member[...] = jnp.zeros(one_map, bf16)
                send_ref[...] = jnp.zeros((layer // 2, 2 * layer), bf16)

        plan_size = (5 * layer if level else 3 * layer, 2 * layer)
        args = (totals, near) if level == 0 else (totals, near, far, members)
        *grown, plan, member, send = call(
            group,
            [(triple, bf16)] * (not closing)
            + [
                (plan_size, bf16),
                (one_map if closing else triple, bf16),
                ((layer // 2 if closing else half, 2 * layer), bf16),
            ],
            args,
            64 * layer**3,
        )
        plans.append(plan)
        if not closing:
            totals, members = grown[0], member

    e_near = swapped(send, "slab", 1 << final)
    e_far = swapped(e_near, "slab", 1)

    ways = (slice(0, layer), slice(layer, 2 * layer))
    pair = (2 * layer, width)

    def scan(vector):
        total, sent, reach = vector, vector, None
        for level in range(final):
            other = swapped(sent, "slab", 1 << level)
            closing = level == final - 1

            def step(*refs, level=level, closing=closing):
                mine, other_ref, plan = refs[:3]
                total_ref, sent_ref, reach_ref = refs[-3:]
                after = place(level)
                own = [mine[w] for w in ways]
                its = [other_ref[w].astype(f32) for w in ways]
                c_left, c_right = jnp.where(after, its[0], own[0]), jnp.where(after, own[0], its[0])
                f_left, f_right = jnp.where(after, its[1], own[1]), jnp.where(after, own[1], its[1])
                spread = mapped(plan[: (3 if level else 2) * layer], c_left)
                back = f_right + spread[ways[1]]
                c_new = c_right + spread[ways[0]]
                f_new = f_left + mapped(plan[rows_of[3 if level else 2]], back)
                if level:
                    so_far = refs[3]
                    more = mapped(plan[rows_of[4]], jnp.where(after, c_left, back))
                    z = so_far[ways[0]] + jnp.where(after, spread[rows_of[2]], 0.0)
                    u = so_far[ways[1]] + more
                else:
                    z = jnp.where(after, c_left, jnp.zeros_like(c_left))
                    u = jnp.where(after, jnp.zeros_like(back), back)
                reach_ref[ways[0]] = z
                reach_ref[ways[1]] = u
                if closing:
                    total_ref[...] = c_new
                    sent_ref[...] = jnp.where(place(final), f_new, c_new).astype(bf16)
                else:
                    total_ref[ways[0]] = c_new
                    total_ref[ways[1]] = f_new
                    sent_ref[ways[0]] = c_new.astype(bf16)
                    sent_ref[ways[1]] = f_new.astype(bf16)

            size = (layer, width) if closing else pair
            args = (total, other, plans[level]) + ((reach,) if level else ())
            total, sent, reach = call(
                step, [(size, f32), (size, bf16), (pair, f32)], args, 40 * layer * layer * width
            )
        return total, swapped(sent, "slab", 1 << final), reach

    def fetch(green_ref, held_ref, sem, spots):
        copies = [
            pltpu.make_async_copy(green_ref.at[k, r], held_ref.at[k, i], sem.at[i, k])
            for i, r in enumerate(spots)
            for k in range(2)
        ]
        for copy in copies:
            copy.start()
        return copies

    def prepare(
        green_ref, inj_ref, panel_ref, start_ref, count_ref, strength_ref,
        ends_ref, acc_ref, weight_ref, sem,
    ):
        copies = fetch(green_ref, ends_ref, sem, (pl.ds(0, layer), pl.ds(low, layer)))
        me = lax.axis_index("energy")
        row = lax.broadcasted_iota(jnp.int32, (span, width), 0)
        acc_ref[...] = inj_ref[...].astype(f32)
        for k in range(energies):
            s = me ^ k
            weight = jnp.where(row < count_ref[me, s] * rows, strength_ref[me, s], 0.0)
            if k:
                weight_ref[k - 1] = weight
            else:
                first = pl.multiple_of(start_ref[me, me] * rows, rows)
                part = pl.ds(first, span)
                acc_ref[part] = acc_ref[part] + panel_ref[part].astype(f32) * weight
        for copy in copies:
            copy.wait()

    ends, acc, weights = call(
        prepare,
        [
            ((2, 2, layer, norb), bf16),
            ((norb, width), f32),
            ((energies - 1, span, width), f32),
        ],
        (far_green, injection[0, 0], panel, block_start, block_count, strength),
        0,
        {0: pltpu.HBM, 3: SMEM, 4: SMEM, 5: SMEM},
        [pltpu.SemaphoreType.DMA((2, 2))],
    )

    def load(start_ref, acc_ref, weight_ref, ends_ref, turn_ref, *refs):
        got, (source_ref, spun_ref, low_ref, sent_ref, sum_ref) = refs[:-5], refs[-5:]
        me = lax.axis_index("energy")
        sum_ref[...] = acc_ref[...]
        for k in range(1, energies):
            first = pl.multiple_of(start_ref[me, me ^ k] * rows, rows)
            part = pl.ds(first, span)
            sum_ref[part] = sum_ref[part] + got[k - 1][...].astype(f32) * weight_ref[k - 1]
        source = sum_ref[...].astype(bf16)
        spun = turned(source.astype(f32)).astype(bf16)
        source_ref[...] = source
        spun_ref[...] = spun
        direct = dot(ends_ref[0, 1], source) + dot(ends_ref[1, 1], spun)
        low_ref[...] = direct
        sent_ref[ways[0]] = fine(turn_ref[...], direct)
        sent_ref[ways[1]] = dot(ends_ref[0, 0], source) + dot(ends_ref[1, 0], spun)

    source, spun, direct_low, sent = call(
        load,
        [((norb, width), bf16)] * 2 + [((layer, width), f32), (pair, f32)],
        (block_start, acc, weights, ends, coup_t, *received),
        8 * layer * norb * width,
        {0: SMEM},
        [pltpu.VMEM((norb, width), f32)],
    )
    c_total, arrived, reach = scan(sent)

    blocks = (low - layer) // layer

    def fetch_mid(green_ref, hint_ref, mid_ref, sem):
        spots = [pl.ds((i + 1) * layer, layer) for i in range(blocks)]
        for copy in fetch(green_ref, mid_ref, sem, spots):
            copy.wait()

    (mid,) = call(
        fetch_mid,
        [((2, blocks, layer, norb), bf16)],
        (far_green, direct_low),
        0,
        {0: pltpu.HBM, 1: pl.ANY},
        [pltpu.SemaphoreType.DMA((blocks, 2))],
    )

    def direct_step(mid_ref, source_ref, spun_ref, out_ref):
        for i in range(blocks):
            out_ref[i] = dot(mid_ref[0, i], source_ref[...]) + dot(mid_ref[1, i], spun_ref[...])

    (direct_mid,) = call(
        direct_step,
        [((blocks, layer, width), f32)],
        (mid, source, spun),
        4 * (low - layer) * norb * width,
    )

    def weights(
        mine, near_ref, far_ref, old, bounce_ref, reach_ref, ends_ref, mid_ref, coup_ref,
        sent_ref, low_ref, direct_ref, base_ref, wide_ref,
    ):
        after, first, right = place(final - 1), place(0), place(final)
        c = coup_ref[...]
        incoming = reach_ref[ways[0]].astype(bf16)
        spun_z = turned(incoming.astype(f32)).astype(bf16)
        outgoing = fine(c, reach_ref[ways[1]]).astype(bf16)
        spun_u = turned(outgoing.astype(f32)).astype(bf16)
        tail = slice(low, norb)

        def held_rows(i):
            if i == 0:
                return [ends_ref.at[k, 0] for k in range(2)]
            if i > blocks:
                return [ends_ref.at[k, 1] for k in range(2)]
            return [mid_ref.at[k, i - 1] for k in range(2)]

        def twice(wide):
            return wide, turned(wide.astype(f32)).astype(bf16)

        @pl.when(right)
        def _():
            its_a = jnp.where(first, far_ref[:layer], near_ref[:layer])
            a_left = jnp.where(after, its_a, mine[rows_of[0]])
            p, spun_p = twice(member_before(after, old[rows_of[0]], a_left))
            r = member_turned(after, old[rows_of[1]], old[rows_of[2]], a_left, bounce_ref[...])
            s, spun_s = twice(dot(c, r).astype(bf16))
            for i in range(blocks + 2):
                real, imag = held_rows(i)
                wide_ref[i * layer : (i + 1) * layer] = (
                    dot(real[:, :layer], p)
                    + dot(imag[:, :layer], spun_p)
                    + dot(real[:, tail], s)
                    + dot(imag[:, tail], spun_s)
                ).astype(bf16)

        @pl.when(~right)
        def _():
            a, b = near_ref[...], far_ref[...]
            theirs = jnp.concatenate([jnp.where(first, b, a), jnp.where(first, a, b)], axis=0)
            b_right = jnp.where(after, mine[rows_of[1]], theirs[rows_of[1]])
            q = member_behind(after, old[rows_of[1]], b_right)
            s, spun_s = twice(dot(c, q).astype(bf16))
            for i in range(blocks + 2):
                real, imag = held_rows(i)
                wide_ref[i * layer : (i + 1) * layer] = (
                    dot(real[:, tail], s) + dot(imag[:, tail], spun_s)
                ).astype(bf16)

        for i in range(blocks + 2):
            real, imag = held_rows(i)
            if i == 0:
                direct = sent_ref[ways[1]]
            elif i > blocks:
                direct = low_ref[...]
            else:
                direct = direct_ref[i - 1]
            base_ref[i * layer : (i + 1) * layer] = (
                direct
                + dot(real[:, :layer], incoming)
                + dot(imag[:, :layer], spun_z)
                + dot(real[:, tail], outgoing)
                + dot(imag[:, tail], spun_u)
            )

    base, last_map = call(
        weights,
        [((norb, width), f32), ((norb, 2 * layer), bf16)],
        (
            totals, near, far, members, member, reach, ends, mid, coup,
            sent, direct_low, direct_mid,
        ),
        16 * norb * layer * (width + 2 * layer),
    )

    def finish(other_ref, c_ref, near_ref, far_ref, base_ref, wide_ref, out_ref, kept, sem):
        first = place(0)
        other = other_ref[...].astype(f32)
        c_left = c_ref[...]
        a, b = mapped(near_ref[...], c_left), mapped(far_ref[...], c_left)
        bounce = jnp.concatenate([jnp.where(first, b, a), jnp.where(first, a, b)], axis=0)
        last = other + jnp.where(place(final), jnp.zeros_like(bounce), bounce)
        copies = []
        v, spun = last.astype(bf16), turned(last).astype(bf16)
        for i in range(norb // layer):
            part = pl.ds(i * layer, layer)
            kept[part] = (
                base_ref[part] + dot(wide_ref[part, :layer], v) + dot(wide_ref[part, layer:], spun)
            ).astype(bf16)
            copy = pltpu.make_async_copy(kept.at[part], out_ref.at[part], sem.at[i])
            copy.start()
            copies.append(copy)
        for copy in copies:
            copy.wait()

    (out,) = call(
        finish,
        [((norb, width), bf16)],
        (arrived, c_total, e_near, e_far, base, last_map),
        8 * norb * layer * width,
        scratch=[pltpu.VMEM((norb, width), bf16), pltpu.SemaphoreType.DMA((norb // layer,))],
        out_space=pltpu.HBM,
    )
    return out[None, None]


def solution(mesh):
    in_specs = (
        P("energy", "slab", None, None, None),
        P("energy", "slab", None, None),
        P("energy", "slab", None, None),
        P("slab", None, None),
        P(),
        P(),
        P(),
    )
    out_specs = P("energy", "slab", None, None)
    return jax.shard_map(body, mesh=mesh, in_specs=in_specs, out_specs=out_specs, check_vma=False)
```

```python
import math

import jax
import jax.numpy as jnp
from jax import lax
from jax.experimental import pallas as pl
from jax.experimental.pallas import tpu as pltpu
from jax.sharding import PartitionSpec as P


NBLK = 16
CAP = 4
VMEM_BYTES = 67043328
bf16 = jnp.bfloat16
f32 = jnp.float32
VMEM = pltpu.VMEM


def swapped(block, axis, mask):
    count = lax.axis_size(axis)
    return lax.ppermute(block, axis, [(i, i ^ mask) for i in range(count)])


def dot(a, b):
    return jnp.dot(a, b, preferred_element_type=f32)


def turned(v):
    half = v.shape[1] // 2
    if half % 128 == 0:
        return jnp.concatenate([-v[:, half:], v[:, :half]], axis=1)
    lane = lax.broadcasted_iota(jnp.int32, v.shape, 1)
    moved = pltpu.roll(v, half, 1)
    return jnp.where(lane < half, -moved, moved)


def applied(real, imag, v):
    v = v.astype(f32)
    return dot(real, v.astype(bf16)) + dot(imag, turned(v).astype(bf16))


def mapped(wide, v):
    side = wide.shape[1] // 2
    return applied(wide[:, :side], wide[:, side:], v)


def fine(real, v):
    high = v.astype(bf16)
    return dot(real, high) + dot(real, (v - high.astype(f32)).astype(bf16))


def member_before(after, p, a_left):
    return jnp.where(after, mapped(p, a_left).astype(bf16), p)


def member_behind(after, q, b_right):
    return jnp.where(after, q, mapped(q, b_right).astype(bf16))


def member_turned(after, q, r, a_left, bounce):
    more = mapped(jnp.where(after, r, q), jnp.where(after, a_left, bounce))
    return jnp.where(after, more, more + r.astype(f32)).astype(bf16)


def place(k):
    return ((lax.axis_index("slab") >> k) & 1) == 1


def call(kernel, outs, args, flops, spaces=None, scratch=(), out_space=VMEM, spare=None):
    spaces = spaces or {}
    specs = [pl.BlockSpec(memory_space=spaces.get(i, VMEM)) for i in range(len(args))]
    moved = sum(a.size * a.dtype.itemsize for a in args)
    kept = sum(math.prod(s) * jnp.dtype(t).itemsize for s, t in outs)
    kept += sum(a.size * a.dtype.itemsize for i, a in enumerate(args) if i not in spaces)
    limit = kept + (4 << 20) if spare is None else VMEM_BYTES - spare
    shapes = [jax.ShapeDtypeStruct(s, t) for s, t in outs]
    return pl.pallas_call(
        kernel,
        out_shape=shapes,
        in_specs=specs,
        out_specs=[pl.BlockSpec(memory_space=out_space)] * len(shapes),
        scratch_shapes=list(scratch),
        compiler_params=pltpu.CompilerParams(vmem_limit_bytes=limit),
        cost_estimate=pl.CostEstimate(
            flops=flops, bytes_accessed=moved, transcendentals=0
        ),
    )(*args)


def in_hbm(array):
    return pltpu.with_memory_space_constraint(array, pltpu.HBM)


def body(pivots, injection, previous, coupling, strength, block_start, block_count):
    green = pivots[0, 0]
    norb = green.shape[1]
    layer = coupling.shape[1]
    width = injection.shape[3]
    rows = norb // NBLK
    span = rows * CAP
    far_green = in_hbm(green)
    coup = coupling[0]
    far_coup = in_hbm(coup)
    panel = previous[0, 0]
    energies = lax.axis_size("energy")
    slabs = lax.axis_size("slab")
    levels = slabs.bit_length() - 1
    low = norb - layer
    SMEM = pltpu.SMEM

    rows_of = [slice(k * layer, (k + 1) * layer) for k in range(6)]
    triple, one_map = (3 * layer, 2 * layer), (layer, 2 * layer)

    def own_maps(green_ref, coup_ref, start_ref, panel_ref, *refs):
        maps_ref, turn_ref = refs[:2]
        pieces = refs[2 : energies + 1]
        corner, near, whole, table, sem, sem_c, sem_t, sem_p = refs[energies + 1 :]
        ask = pltpu.make_async_copy(start_ref, table, sem_t)
        panel_copy = pltpu.make_async_copy(panel_ref, whole, sem_p)
        first = pltpu.make_async_copy(coup_ref, near, sem_c)
        top, end = pl.ds(0, layer), pl.ds(low, layer)
        copies = [
            [
                pltpu.make_async_copy(green_ref.at[k, r, c], corner.at[i, k], sem.at[i, k])
                for k in range(2)
            ]
            for i, (r, c) in enumerate(((end, top), (top, end), (top, top)))
        ]
        ask.start()
        first.start()
        panel_copy.start()
        for pair in copies:
            for copy in pair:
                copy.start()
        me = lax.axis_index("energy")
        first.wait()
        c = near[...]
        ct = c.astype(f32).T.astype(bf16)
        turn_ref[...] = ct
        panel_copy.wait()
        ask.wait()
        for k in range(energies - 1):
            begin = pl.multiple_of(table[me ^ (k + 1), me] * rows, rows)
            pieces[k][...] = whole[pl.ds(begin, span)]
        for i in range(3):
            for k in range(2):
                copies[i][k].wait()
                held = corner[i, k]
                if i == 0:
                    held = dot(ct, held).astype(bf16)
                elif i == 1:
                    held = dot(held, c).astype(bf16)
                maps_ref[rows_of[i], rows_of[k]] = held

    maps, coup_t, *pieces = call(
        own_maps,
        [(triple, bf16), ((layer, layer), bf16)] + [((span, width), bf16)] * (energies - 1),
        (far_green, far_coup, in_hbm(block_start), in_hbm(panel)),
        8 * layer**3,
        {k: pltpu.HBM for k in range(4)},
        [
            pltpu.VMEM((3, 2, layer, layer), bf16),
            pltpu.VMEM((layer, layer), bf16),
            pltpu.VMEM(panel.shape, bf16),
            pltpu.SMEM(block_start.shape, block_start.dtype),
            pltpu.SemaphoreType.DMA((3, 2)),
            pltpu.SemaphoreType.DMA,
            pltpu.SemaphoreType.DMA,
            pltpu.SemaphoreType.DMA,
        ],
    )
    received = [None] * (energies - 1)
    for mask in range(energies - 1, 0, -1):
        received[mask - 1] = swapped(pieces[mask - 1], "energy", mask)

    half = 3 * layer // 2
    final = levels - 1
    plans = []

    def sides(mine, theirs, after):
        own = [mine[rows_of[k]] for k in range(3)]
        its = [theirs[rows_of[k]] for k in range(3)]
        left = [jnp.where(after, b, a) for a, b in zip(own, its)]
        right = [jnp.where(after, a, b) for a, b in zip(own, its)]
        return left, right

    def joined(near_ref, far_ref):
        first, a, b = place(0), near_ref[...], far_ref[...]
        return jnp.concatenate([jnp.where(first, b, a), jnp.where(first, a, b)], axis=0)

    def reflected(left, right):
        bounce = mapped(right[2], left[0]).astype(bf16)
        return bounce, (left[2].astype(f32) + mapped(left[1], bounce)).astype(bf16)

    cut = layer // 2
    parts = [((2 * cut, 2 * layer), bf16), ((cut, 2 * layer), bf16)]
    direct_close = final == 2

    def pack(grown, x_ref, y_ref):
        later = place(final - 1)
        x_ref[:cut] = grown[0]
        x_ref[cut:] = jnp.where(later, grown[2], grown[1])
        y_ref[...] = jnp.where(later, grown[1], grown[2])

    def halved(block):
        return jnp.where(place(0), block[cut:], block[:cut])

    def group0(mine, near_ref, plan, *sends):
        def fill(left, right, begin):
            rows_in = [slice(k * layer + begin, k * layer + begin + cut) for k in range(3)]
            plan[rows_of[0]], plan[rows_of[1]] = right[rows_of[0]], right[rows_of[2]]
            plan[rows_of[2]] = left[rows_of[1]]
            bounce = mapped(right[rows_of[2]], left[rows_of[0]]).astype(bf16)
            if direct_close:
                b_rows = left[rows_in[1]]
                grown = (
                    mapped(right[rows_in[0]], left[rows_of[0]]).astype(bf16),
                    mapped(b_rows, right[rows_of[1]]).astype(bf16),
                    (left[rows_in[2]].astype(f32) + mapped(b_rows, bounce)).astype(bf16),
                )
                pack(grown, *sends)
                return
            whole = jnp.concatenate(
                [
                    mapped(right[rows_of[0]], left[rows_of[0]]).astype(bf16),
                    mapped(left[rows_of[1]], right[rows_of[1]]).astype(bf16),
                    (
                        left[rows_of[2]].astype(f32) + mapped(left[rows_of[1]], bounce)
                    ).astype(bf16),
                ],
                axis=0,
            )
            sends[0][...] = whole[half:] if begin else whole[:half]

        pl.when(place(0))(lambda: fill(near_ref, mine, cut))
        pl.when(~place(0))(lambda: fill(mine, near_ref, 0))

    def grow0(mine, near_ref, total, member):
        after = place(0)
        left, right = sides(mine, near_ref, after)
        bounce, e_total = reflected(left, right)
        total[rows_of[0]] = mapped(right[0], left[0]).astype(bf16)
        total[rows_of[1]] = mapped(left[1], right[1]).astype(bf16)
        total[rows_of[2]] = e_total
        row = lax.broadcasted_iota(jnp.int32, one_map, 0)
        col = lax.broadcasted_iota(jnp.int32, one_map, 1)
        unit = (row == col).astype(f32).astype(bf16)
        member[rows_of[0]] = jnp.where(after, left[0], unit)
        member[rows_of[1]] = jnp.where(after, unit, right[1])
        member[rows_of[2]] = jnp.where(after, jnp.zeros_like(bounce), bounce)

    near = swapped(maps, "slab", 1)
    sent_half = [((half, 2 * layer), bf16)]
    plan, *sends = call(
        group0, [(triple, bf16)] + (parts if direct_close else sent_half), (maps, near),
        32 * layer**3,
    )
    totals, members = call(grow0, [(triple, bf16)] * 2, (maps, near), 64 * layer**3)
    plans.append(plan)

    for level in range(1, final - 1):
        near = swapped(sends[0], "slab", 1 << level)
        far = swapped(near, "slab", 1)
        to_close = level == final - 2

        def group(
            mine, near_ref, far_ref, old, total, plan, member, *refs, level=level, to_close=to_close
        ):
            after = place(level)
            left, right = sides(mine, joined(near_ref, far_ref), after)
            p, q, r = (old[rows_of[k]] for k in range(3))
            plan_rows = (right[0], right[2], p, left[1], jnp.where(after, r, q))
            for k, part in enumerate(plan_rows):
                plan[rows_of[k]] = part
            bounce, e_total = reflected(left, right)
            member[rows_of[0]] = member_before(after, p, left[0])
            member[rows_of[1]] = member_behind(after, q, right[1])
            member[rows_of[2]] = member_turned(after, q, r, left[0], bounce)
            grown = (
                mapped(right[0], left[0]).astype(bf16),
                mapped(left[1], right[1]).astype(bf16),
                e_total,
            )
            whole = jnp.concatenate(grown, axis=0)
            total[...] = whole
            if to_close:
                pack([halved(g) for g in grown], *refs)
            else:
                refs[0][...] = jnp.where(place(0), whole[half:], whole[:half])

        totals, plan, members, *sends = call(
            group,
            [
                (triple, bf16),
                ((5 * layer, 2 * layer), bf16),
                (triple, bf16),
            ]
            + (parts if to_close else sent_half),
            (totals, near, far, members),
            64 * layer**3,
        )
        plans.append(plan)

    near_x = swapped(sends[0], "slab", 1 << (final - 1))
    near_y = swapped(sends[1], "slab", 1 << (final - 1))
    far_x = swapped(near_x, "slab", 1)
    far_y = swapped(near_y, "slab", 1)

    def theirs(near_ref, far_ref, begin):
        first, a, b = place(0), near_ref[begin : begin + cut], far_ref[begin : begin + cut]
        return jnp.concatenate([jnp.where(first, b, a), jnp.where(first, a, b)], axis=0)

    def reflect(mine, near_ref, far_ref, ny_ref, bounce_ref, send_ref):
        after, right = place(final - 1), place(final)

        @pl.when(right & after)
        def _():
            bounce = mapped(mine[rows_of[2]], theirs(near_ref, far_ref, 0)).astype(bf16)
            bounce_ref[...] = bounce
            send_ref[...] = (
                ny_ref[...].astype(f32) + mapped(near_ref[cut:], bounce)
            ).astype(bf16)

        @pl.when(right & ~after)
        def _():
            bounce = mapped(theirs(near_ref, far_ref, cut), mine[rows_of[0]]).astype(bf16)
            bounce_ref[...] = bounce
            send_ref[...] = (
                halved(mine[rows_of[2]]).astype(f32) + mapped(halved(mine[rows_of[1]]), bounce)
            ).astype(bf16)

        @pl.when(~right)
        def _():
            bounce_ref[...] = jnp.zeros(bounce_ref.shape, bf16)
            send_ref[...] = jnp.zeros(send_ref.shape, bf16)

    bounced, send = call(
        reflect,
        [(one_map, bf16), ((cut, 2 * layer), bf16)],
        (totals, near_x, far_x, near_y),
        24 * layer**3,
    )
    e_near = swapped(send, "slab", 1 << final)
    e_far = swapped(e_near, "slab", 1)

    ways = (slice(0, layer), slice(layer, 2 * layer))
    pair = (2 * layer, width)

    def scan(vector):
        total, sent, reach = vector, vector, None
        for level in range(final):
            other = swapped(sent, "slab", 1 << level)
            closing = level == final - 1

            def step(mine, other_ref, *refs, level=level, closing=closing):
                total_ref, sent_ref, reach_ref = refs[-3:]
                after = place(level)
                own = [mine[w] for w in ways]
                its = [other_ref[w].astype(f32) for w in ways]
                c_left, c_right = jnp.where(after, its[0], own[0]), jnp.where(after, own[0], its[0])
                f_left, f_right = jnp.where(after, its[1], own[1]), jnp.where(after, own[1], its[1])
                if closing:
                    mine_ref, near_ref, far_ref, old, so_far = refs[:5]
                    right = place(final)

                    @pl.when(~after)
                    def _():
                        e_right = theirs(near_ref, far_ref, cut)
                        back = f_right + mapped(e_right, c_left)
                        reach_ref[ways[0]] = so_far[ways[0]]
                        reach_ref[ways[1]] = so_far[ways[1]] + mapped(old[rows_of[1]], back)

                        @pl.when(right)
                        def _():
                            f_new = f_left + mapped(mine_ref[rows_of[1]], back)
                            total_ref[...] = f_new
                            sent_ref[...] = f_new.astype(bf16)

                        @pl.when(~right)
                        def _():
                            c_new = c_right + mapped(theirs(near_ref, far_ref, 0), c_left)
                            total_ref[...] = c_new
                            sent_ref[...] = c_new.astype(bf16)

                    @pl.when(after)
                    def _():
                        reach_ref[ways[0]] = so_far[ways[0]] + mapped(old[rows_of[0]], c_left)
                        reach_ref[ways[1]] = so_far[ways[1]] + mapped(old[rows_of[2]], c_left)

                        @pl.when(right)
                        def _():
                            back = f_right + mapped(mine_ref[rows_of[2]], c_left)
                            b_left = theirs(near_ref, far_ref, cut)
                            f_new = f_left + mapped(b_left, back)
                            total_ref[...] = f_new
                            sent_ref[...] = f_new.astype(bf16)

                        @pl.when(~right)
                        def _():
                            c_new = c_right + mapped(mine_ref[rows_of[0]], c_left)
                            total_ref[...] = c_new
                            sent_ref[...] = c_new.astype(bf16)

                    return
                plan = refs[0]
                spread = mapped(plan[: (3 if level else 2) * layer], c_left)
                back = f_right + spread[ways[1]]
                c_new = c_right + spread[ways[0]]
                f_new = f_left + mapped(plan[rows_of[3 if level else 2]], back)
                if level:
                    so_far = refs[1]
                    more = mapped(plan[rows_of[4]], jnp.where(after, c_left, back))
                    z = so_far[ways[0]] + jnp.where(after, spread[rows_of[2]], 0.0)
                    u = so_far[ways[1]] + more
                else:
                    z = jnp.where(after, c_left, jnp.zeros_like(c_left))
                    u = jnp.where(after, jnp.zeros_like(back), back)
                reach_ref[ways[0]] = z
                reach_ref[ways[1]] = u
                total_ref[ways[0]] = c_new
                total_ref[ways[1]] = f_new
                sent_ref[ways[0]] = c_new.astype(bf16)
                sent_ref[ways[1]] = f_new.astype(bf16)

            size = (layer, width) if closing else pair
            if closing:
                args = (total, other, totals, near_x, far_x, members, reach)
            else:
                args = (total, other, plans[level]) + ((reach,) if level else ())
            total, sent, reach = call(
                step, [(size, f32), (size, bf16), (pair, f32)], args, 40 * layer * layer * width
            )
        return total, swapped(sent, "slab", 1 << final), reach

    blocks = (low - layer) // layer

    def fetch(green_ref, held_ref, sem, spots):
        copies = [
            pltpu.make_async_copy(green_ref.at[k, r], held_ref.at[k, i], sem.at[i, k])
            for i, r in enumerate(spots)
            for k in range(2)
        ]
        for copy in copies:
            copy.start()
        return copies

    def prepare(
        green_ref, inj_ref, panel_ref, start_ref, count_ref, strength_ref,
        ends_ref, mid_ref, acc_ref, weight_ref, sem, sem_mid,
    ):
        copies = fetch(green_ref, ends_ref, sem, (pl.ds(0, layer), pl.ds(low, layer)))
        spots = [pl.ds((i + 1) * layer, layer) for i in range(blocks)]
        copies += fetch(green_ref, mid_ref, sem_mid, spots)
        me = lax.axis_index("energy")
        row = lax.broadcasted_iota(jnp.int32, (span, width), 0)
        acc_ref[...] = inj_ref[...].astype(f32)
        for k in range(energies):
            s = me ^ k
            weight = jnp.where(row < count_ref[me, s] * rows, strength_ref[me, s], 0.0)
            if k:
                weight_ref[k - 1] = weight
            else:
                first = pl.multiple_of(start_ref[me, me] * rows, rows)
                part = pl.ds(first, span)
                acc_ref[part] = acc_ref[part] + panel_ref[part].astype(f32) * weight
        for copy in copies:
            copy.wait()

    ends, mid, acc, weights = call(
        prepare,
        [
            ((2, 2, layer, norb), bf16),
            ((2, blocks, layer, norb), bf16),
            ((norb, width), f32),
            ((energies - 1, span, width), f32),
        ],
        (far_green, injection[0, 0], panel, block_start, block_count, strength),
        0,
        {0: pltpu.HBM, 3: SMEM, 4: SMEM, 5: SMEM},
        [pltpu.SemaphoreType.DMA((2, 2)), pltpu.SemaphoreType.DMA((blocks, 2))],
    )

    def load(start_ref, acc_ref, weight_ref, ends_ref, turn_ref, *refs):
        got, (source_ref, spun_ref, low_ref, sent_ref, sum_ref) = refs[:-5], refs[-5:]
        me = lax.axis_index("energy")
        sum_ref[...] = acc_ref[...]
        for k in range(1, energies):
            first = pl.multiple_of(start_ref[me, me ^ k] * rows, rows)
            part = pl.ds(first, span)
            sum_ref[part] = sum_ref[part] + got[k - 1][...].astype(f32) * weight_ref[k - 1]
        source = sum_ref[...].astype(bf16)
        spun = turned(source.astype(f32)).astype(bf16)
        source_ref[...] = source
        spun_ref[...] = spun
        direct = dot(ends_ref[0, 1], source) + dot(ends_ref[1, 1], spun)
        low_ref[...] = direct
        sent_ref[ways[0]] = fine(turn_ref[...], direct)
        sent_ref[ways[1]] = dot(ends_ref[0, 0], source) + dot(ends_ref[1, 0], spun)

    source, spun, direct_low, sent = call(
        load,
        [((norb, width), bf16)] * 2 + [((layer, width), f32), (pair, f32)],
        (block_start, acc, weights, ends, coup_t, *received),
        8 * layer * norb * width,
        {0: SMEM},
        [pltpu.VMEM((norb, width), f32)],
    )
    c_total, arrived, reach = scan(sent)

    def direct_step(mid_ref, source_ref, spun_ref, out_ref):
        for i in range(blocks):
            out_ref[i] = dot(mid_ref[0, i], source_ref[...]) + dot(mid_ref[1, i], spun_ref[...])

    (direct_mid,) = call(
        direct_step,
        [((blocks, layer, width), f32)],
        (mid, source, spun),
        4 * (low - layer) * norb * width,
    )

    def weights(
        mine, near_ref, far_ref, ny_ref, fy_ref, old, bounce_ref, hint_ref, ends_ref, mid_ref,
        coup_ref, wide_ref,
    ):
        after, right = place(final - 1), place(final)
        c = coup_ref[...]
        tail = slice(low, norb)

        def held_rows(i):
            if i == 0:
                return [ends_ref.at[k, 0] for k in range(2)]
            if i > blocks:
                return [ends_ref.at[k, 1] for k in range(2)]
            return [mid_ref.at[k, i - 1] for k in range(2)]

        def twice(wide):
            return wide, turned(wide.astype(f32)).astype(bf16)

        @pl.when(right)
        def _():
            a_left = jnp.where(after, theirs(near_ref, far_ref, 0), mine[rows_of[0]])
            p, spun_p = twice(member_before(after, old[rows_of[0]], a_left))
            r = member_turned(after, old[rows_of[1]], old[rows_of[2]], a_left, bounce_ref[...])
            s, spun_s = twice(dot(c, r).astype(bf16))
            for i in range(blocks + 2):
                real, imag = held_rows(i)
                wide_ref[i * layer : (i + 1) * layer] = (
                    dot(real[:, :layer], p)
                    + dot(imag[:, :layer], spun_p)
                    + dot(real[:, tail], s)
                    + dot(imag[:, tail], spun_s)
                ).astype(bf16)

        @pl.when(~right)
        def _():
            b_right = jnp.where(after, mine[rows_of[1]], theirs(ny_ref, fy_ref, 0))
            q = member_behind(after, old[rows_of[1]], b_right)
            s, spun_s = twice(dot(c, q).astype(bf16))
            for i in range(blocks + 2):
                real, imag = held_rows(i)
                wide_ref[i * layer : (i + 1) * layer] = (
                    dot(real[:, tail], s) + dot(imag[:, tail], spun_s)
                ).astype(bf16)

    (last_map,) = call(
        weights,
        [((norb, 2 * layer), bf16)],
        (totals, near_x, far_x, near_y, far_y, members, bounced, reach, ends, mid, coup),
        32 * norb * layer * layer,
    )

    def based(reach_ref, ends_ref, mid_ref, coup_ref, sent_ref, low_ref, direct_ref, base_ref):
        incoming = reach_ref[ways[0]].astype(bf16)
        spun_z = turned(incoming.astype(f32)).astype(bf16)
        outgoing = fine(coup_ref[...], reach_ref[ways[1]]).astype(bf16)
        spun_u = turned(outgoing.astype(f32)).astype(bf16)
        tail = slice(low, norb)
        for i in range(blocks + 2):
            if i == 0:
                direct, held = sent_ref[ways[1]], [ends_ref.at[k, 0] for k in range(2)]
            elif i > blocks:
                direct, held = low_ref[...], [ends_ref.at[k, 1] for k in range(2)]
            else:
                direct, held = direct_ref[i - 1], [mid_ref.at[k, i - 1] for k in range(2)]
            base_ref[i * layer : (i + 1) * layer] = (
                direct
                + dot(held[0][:, :layer], incoming)
                + dot(held[1][:, :layer], spun_z)
                + dot(held[0][:, tail], outgoing)
                + dot(held[1][:, tail], spun_u)
            )

    (base,) = call(
        based,
        [((norb, width), f32)],
        (reach, ends, mid, coup, sent, direct_low, direct_mid),
        16 * norb * layer * width,
    )

    def finish(other_ref, c_ref, near_ref, far_ref, base_ref, wide_ref, out_ref, kept, sem):
        first = place(0)
        other = other_ref[...].astype(f32)
        c_left = c_ref[...]
        a, b = mapped(near_ref[...], c_left), mapped(far_ref[...], c_left)
        bounce = jnp.concatenate([jnp.where(first, b, a), jnp.where(first, a, b)], axis=0)
        last = other + jnp.where(place(final), jnp.zeros_like(bounce), bounce)
        copies = []
        v, spun = last.astype(bf16), turned(last).astype(bf16)
        for i in range(norb // layer):
            part = pl.ds(i * layer, layer)
            kept[part] = (
                base_ref[part] + dot(wide_ref[part, :layer], v) + dot(wide_ref[part, layer:], spun)
            ).astype(bf16)
            copy = pltpu.make_async_copy(kept.at[part], out_ref.at[part], sem.at[i])
            copy.start()
            copies.append(copy)
        for copy in copies:
            copy.wait()

    (out,) = call(
        finish,
        [((norb, width), bf16)],
        (arrived, c_total, e_near, e_far, base, last_map),
        8 * norb * layer * width,
        scratch=[pltpu.VMEM((norb, width), bf16), pltpu.SemaphoreType.DMA((norb // layer,))],
        out_space=pltpu.HBM,
    )
    return out[None, None]


def solution(mesh):
    in_specs = (
        P("energy", "slab", None, None, None),
        P("energy", "slab", None, None),
        P("energy", "slab", None, None),
        P("slab", None, None),
        P(),
        P(),
        P(),
    )
    out_specs = P("energy", "slab", None, None)
    return jax.shard_map(body, mesh=mesh, in_specs=in_specs, out_specs=out_specs, check_vma=False)
```

```python
import math

import jax
import jax.numpy as jnp
from jax import lax
from jax.experimental import pallas as pl
from jax.experimental.pallas import tpu as pltpu
from jax.sharding import PartitionSpec as P


NBLK = 16
CAP = 4
VMEM_BYTES = 67043328
bf16 = jnp.bfloat16
f32 = jnp.float32
VMEM = pltpu.VMEM


def swapped(block, axis, mask):
    count = lax.axis_size(axis)
    return lax.ppermute(block, axis, [(i, i ^ mask) for i in range(count)])


def dot(a, b):
    return jnp.dot(a, b, preferred_element_type=f32)


def turned(v):
    half = v.shape[1] // 2
    if half % 128 == 0:
        return jnp.concatenate([-v[:, half:], v[:, :half]], axis=1)
    lane = lax.broadcasted_iota(jnp.int32, v.shape, 1)
    moved = pltpu.roll(v, half, 1)
    return jnp.where(lane < half, -moved, moved)


def applied(real, imag, v):
    v = v.astype(f32)
    return dot(real, v.astype(bf16)) + dot(imag, turned(v).astype(bf16))


def mapped(wide, v):
    side = wide.shape[1] // 2
    return applied(wide[:, :side], wide[:, side:], v)


def fine(real, v):
    high = v.astype(bf16)
    return dot(real, high) + dot(real, (v - high.astype(f32)).astype(bf16))


def member_before(after, p, a_left):
    return jnp.where(after, mapped(p, a_left).astype(bf16), p)


def member_behind(after, q, b_right):
    return jnp.where(after, q, mapped(q, b_right).astype(bf16))


def member_turned(after, q, r, a_left, bounce):
    more = mapped(jnp.where(after, r, q), jnp.where(after, a_left, bounce))
    return jnp.where(after, more, more + r.astype(f32)).astype(bf16)


def place(k):
    return ((lax.axis_index("slab") >> k) & 1) == 1


def call(kernel, outs, args, flops, spaces=None, scratch=(), out_space=VMEM, spare=None):
    spaces = spaces or {}
    specs = [pl.BlockSpec(memory_space=spaces.get(i, VMEM)) for i in range(len(args))]
    moved = sum(a.size * a.dtype.itemsize for a in args)
    kept = sum(math.prod(s) * jnp.dtype(t).itemsize for s, t in outs)
    kept += sum(a.size * a.dtype.itemsize for i, a in enumerate(args) if i not in spaces)
    limit = kept + (4 << 20) if spare is None else VMEM_BYTES - spare
    shapes = [jax.ShapeDtypeStruct(s, t) for s, t in outs]
    return pl.pallas_call(
        kernel,
        out_shape=shapes,
        in_specs=specs,
        out_specs=[pl.BlockSpec(memory_space=out_space)] * len(shapes),
        scratch_shapes=list(scratch),
        compiler_params=pltpu.CompilerParams(vmem_limit_bytes=limit),
        cost_estimate=pl.CostEstimate(
            flops=flops, bytes_accessed=moved, transcendentals=0
        ),
    )(*args)


def in_hbm(array):
    return pltpu.with_memory_space_constraint(array, pltpu.HBM)


def body(pivots, injection, previous, coupling, strength, block_start, block_count):
    green = pivots[0, 0]
    norb = green.shape[1]
    layer = coupling.shape[1]
    width = injection.shape[3]
    rows = norb // NBLK
    span = rows * CAP
    far_green = in_hbm(green)
    coup = coupling[0]
    far_coup = in_hbm(coup)
    panel = previous[0, 0]
    energies = lax.axis_size("energy")
    slabs = lax.axis_size("slab")
    levels = slabs.bit_length() - 1
    low = norb - layer
    SMEM = pltpu.SMEM

    rows_of = [slice(k * layer, (k + 1) * layer) for k in range(6)]
    triple, one_map = (3 * layer, 2 * layer), (layer, 2 * layer)

    def own_maps(green_ref, coup_ref, start_ref, panel_ref, *refs):
        maps_ref, turn_ref, ends_ref = refs[:3]
        pieces = refs[3 : energies + 2]
        near, whole, table, sem, sem_c, sem_t, sem_p = refs[energies + 2 :]
        ask = pltpu.make_async_copy(start_ref, table, sem_t)
        panel_copy = pltpu.make_async_copy(panel_ref, whole, sem_p)
        first = pltpu.make_async_copy(coup_ref, near, sem_c)
        copies = [
            [
                pltpu.make_async_copy(
                    green_ref.at[k, pl.ds(i * low, layer)], ends_ref.at[k, i], sem.at[i, k]
                )
                for k in range(2)
            ]
            for i in range(2)
        ]
        ask.start()
        first.start()
        panel_copy.start()
        for pair in copies:
            for copy in pair:
                copy.start()
        me = lax.axis_index("energy")
        first.wait()
        c = near[...]
        panel_copy.wait()
        ask.wait()
        for k in range(energies - 1):
            begin = pl.multiple_of(table[me ^ (k + 1), me] * rows, rows)
            pieces[k][...] = whole[pl.ds(begin, span)]
        ct = c.astype(f32).T.astype(bf16)
        turn_ref[...] = ct
        for pair in copies:
            for copy in pair:
                copy.wait()
        for k in range(2):
            maps_ref[rows_of[1], rows_of[k]] = dot(ends_ref[k, 0, :, low:], c).astype(bf16)
            maps_ref[rows_of[0], rows_of[k]] = dot(ct, ends_ref[k, 1, :, :layer]).astype(bf16)
            maps_ref[rows_of[2], rows_of[k]] = ends_ref[k, 0, :, :layer]

    maps, coup_t, ends, *pieces = call(
        own_maps,
        [(triple, bf16), ((layer, layer), bf16), ((2, 2, layer, norb), bf16)]
        + [((span, width), bf16)] * (energies - 1),
        (far_green, far_coup, in_hbm(block_start), in_hbm(panel)),
        8 * layer**3,
        {k: pltpu.HBM for k in range(4)},
        [
            pltpu.VMEM((layer, layer), bf16),
            pltpu.VMEM(panel.shape, bf16),
            pltpu.SMEM(block_start.shape, block_start.dtype),
            pltpu.SemaphoreType.DMA((2, 2)),
            pltpu.SemaphoreType.DMA,
            pltpu.SemaphoreType.DMA,
            pltpu.SemaphoreType.DMA,
        ],
    )
    received = [None] * (energies - 1)
    for mask in range(energies - 1, 0, -1):
        received[mask - 1] = swapped(pieces[mask - 1], "energy", mask)

    half = 3 * layer // 2
    final = levels - 1
    plans = []

    def sides(mine, theirs, after):
        own = [mine[rows_of[k]] for k in range(3)]
        its = [theirs[rows_of[k]] for k in range(3)]
        left = [jnp.where(after, b, a) for a, b in zip(own, its)]
        right = [jnp.where(after, a, b) for a, b in zip(own, its)]
        return left, right

    def joined(near_ref, far_ref):
        first, a, b = place(0), near_ref[...], far_ref[...]
        return jnp.concatenate([jnp.where(first, b, a), jnp.where(first, a, b)], axis=0)

    def reflected(left, right):
        bounce = mapped(right[2], left[0]).astype(bf16)
        return bounce, (left[2].astype(f32) + mapped(left[1], bounce)).astype(bf16)

    cut = layer // 2
    parts = [((2 * cut, 2 * layer), bf16), ((cut, 2 * layer), bf16)]
    direct_close = final == 2

    def pack(grown, x_ref, y_ref):
        later = place(final - 1)
        x_ref[:cut] = grown[0]
        x_ref[cut:] = jnp.where(later, grown[2], grown[1])
        y_ref[...] = jnp.where(later, grown[1], grown[2])

    def halved(block):
        return jnp.where(place(0), block[cut:], block[:cut])

    def group0(mine, near_ref, plan, *sends):
        def fill(left, right, begin):
            rows_in = [slice(k * layer + begin, k * layer + begin + cut) for k in range(3)]
            plan[rows_of[0]], plan[rows_of[1]] = right[rows_of[0]], right[rows_of[2]]
            plan[rows_of[2]] = left[rows_of[1]]
            bounce = mapped(right[rows_of[2]], left[rows_of[0]]).astype(bf16)
            if direct_close:
                b_rows = left[rows_in[1]]
                grown = (
                    mapped(right[rows_in[0]], left[rows_of[0]]).astype(bf16),
                    mapped(b_rows, right[rows_of[1]]).astype(bf16),
                    (left[rows_in[2]].astype(f32) + mapped(b_rows, bounce)).astype(bf16),
                )
                pack(grown, *sends)
                return
            whole = jnp.concatenate(
                [
                    mapped(right[rows_of[0]], left[rows_of[0]]).astype(bf16),
                    mapped(left[rows_of[1]], right[rows_of[1]]).astype(bf16),
                    (
                        left[rows_of[2]].astype(f32) + mapped(left[rows_of[1]], bounce)
                    ).astype(bf16),
                ],
                axis=0,
            )
            sends[0][...] = whole[half:] if begin else whole[:half]

        pl.when(place(0))(lambda: fill(near_ref, mine, cut))
        pl.when(~place(0))(lambda: fill(mine, near_ref, 0))

    def grow0(mine, near_ref, total, member):
        after = place(0)
        left, right = sides(mine, near_ref, after)
        bounce, e_total = reflected(left, right)
        total[rows_of[0]] = mapped(right[0], left[0]).astype(bf16)
        total[rows_of[1]] = mapped(left[1], right[1]).astype(bf16)
        total[rows_of[2]] = e_total
        row = lax.broadcasted_iota(jnp.int32, one_map, 0)
        col = lax.broadcasted_iota(jnp.int32, one_map, 1)
        unit = (row == col).astype(f32).astype(bf16)
        member[rows_of[0]] = jnp.where(after, left[0], unit)
        member[rows_of[1]] = jnp.where(after, unit, right[1])
        member[rows_of[2]] = jnp.where(after, jnp.zeros_like(bounce), bounce)

    near = swapped(maps, "slab", 1)
    sent_half = [((half, 2 * layer), bf16)]
    plan, *sends = call(
        group0, [(triple, bf16)] + (parts if direct_close else sent_half), (maps, near),
        32 * layer**3,
    )
    totals, members = call(grow0, [(triple, bf16)] * 2, (maps, near), 64 * layer**3)
    plans.append(plan)

    for level in range(1, final - 1):
        near = swapped(sends[0], "slab", 1 << level)
        far = swapped(near, "slab", 1)
        to_close = level == final - 2

        def group(
            mine, near_ref, far_ref, old, total, plan, member, *refs, level=level, to_close=to_close
        ):
            after = place(level)
            left, right = sides(mine, joined(near_ref, far_ref), after)
            p, q, r = (old[rows_of[k]] for k in range(3))
            plan_rows = (right[0], right[2], p, left[1], jnp.where(after, r, q))
            for k, part in enumerate(plan_rows):
                plan[rows_of[k]] = part
            bounce, e_total = reflected(left, right)
            member[rows_of[0]] = member_before(after, p, left[0])
            member[rows_of[1]] = member_behind(after, q, right[1])
            member[rows_of[2]] = member_turned(after, q, r, left[0], bounce)
            grown = (
                mapped(right[0], left[0]).astype(bf16),
                mapped(left[1], right[1]).astype(bf16),
                e_total,
            )
            whole = jnp.concatenate(grown, axis=0)
            total[...] = whole
            if to_close:
                pack([halved(g) for g in grown], *refs)
            else:
                refs[0][...] = jnp.where(place(0), whole[half:], whole[:half])

        totals, plan, members, *sends = call(
            group,
            [
                (triple, bf16),
                ((5 * layer, 2 * layer), bf16),
                (triple, bf16),
            ]
            + (parts if to_close else sent_half),
            (totals, near, far, members),
            64 * layer**3,
        )
        plans.append(plan)

    near_x = swapped(sends[0], "slab", 1 << (final - 1))
    near_y = swapped(sends[1], "slab", 1 << (final - 1))
    far_x = swapped(near_x, "slab", 1)
    far_y = swapped(near_y, "slab", 1)

    def theirs(near_ref, far_ref, begin):
        first, a, b = place(0), near_ref[begin : begin + cut], far_ref[begin : begin + cut]
        return jnp.concatenate([jnp.where(first, b, a), jnp.where(first, a, b)], axis=0)

    def reflect(mine, near_ref, far_ref, ny_ref, bounce_ref, send_ref):
        after, right = place(final - 1), place(final)

        @pl.when(right & after)
        def _():
            bounce = mapped(mine[rows_of[2]], theirs(near_ref, far_ref, 0)).astype(bf16)
            bounce_ref[...] = bounce
            send_ref[...] = (
                ny_ref[...].astype(f32) + mapped(near_ref[cut:], bounce)
            ).astype(bf16)

        @pl.when(right & ~after)
        def _():
            bounce = mapped(theirs(near_ref, far_ref, cut), mine[rows_of[0]]).astype(bf16)
            bounce_ref[...] = bounce
            send_ref[...] = (
                halved(mine[rows_of[2]]).astype(f32) + mapped(halved(mine[rows_of[1]]), bounce)
            ).astype(bf16)

        @pl.when(~right)
        def _():
            bounce_ref[...] = jnp.zeros(bounce_ref.shape, bf16)
            send_ref[...] = jnp.zeros(send_ref.shape, bf16)

    bounced, send = call(
        reflect,
        [(one_map, bf16), ((cut, 2 * layer), bf16)],
        (totals, near_x, far_x, near_y),
        24 * layer**3,
    )
    e_near = swapped(send, "slab", 1 << final)
    e_far = swapped(e_near, "slab", 1)

    ways = (slice(0, layer), slice(layer, 2 * layer))
    pair = (2 * layer, width)

    def scan(vector):
        total, sent, reach = vector, vector, None
        for level in range(final):
            other = swapped(sent, "slab", 1 << level)
            closing = level == final - 1

            def step(mine, other_ref, *refs, level=level, closing=closing):
                total_ref, sent_ref, reach_ref = refs[-3:]
                after = place(level)
                own = [mine[w] for w in ways]
                its = [other_ref[w].astype(f32) for w in ways]
                c_left, c_right = jnp.where(after, its[0], own[0]), jnp.where(after, own[0], its[0])
                f_left, f_right = jnp.where(after, its[1], own[1]), jnp.where(after, own[1], its[1])
                if closing:
                    mine_ref, near_ref, far_ref, old, so_far = refs[:5]
                    right = place(final)

                    @pl.when(~after)
                    def _():
                        e_right = theirs(near_ref, far_ref, cut)
                        back = f_right + mapped(e_right, c_left)
                        reach_ref[ways[0]] = so_far[ways[0]]
                        reach_ref[ways[1]] = so_far[ways[1]] + mapped(old[rows_of[1]], back)

                        @pl.when(right)
                        def _():
                            f_new = f_left + mapped(mine_ref[rows_of[1]], back)
                            total_ref[...] = f_new
                            sent_ref[...] = f_new.astype(bf16)

                        @pl.when(~right)
                        def _():
                            c_new = c_right + mapped(theirs(near_ref, far_ref, 0), c_left)
                            total_ref[...] = c_new
                            sent_ref[...] = c_new.astype(bf16)

                    @pl.when(after)
                    def _():
                        reach_ref[ways[0]] = so_far[ways[0]] + mapped(old[rows_of[0]], c_left)
                        reach_ref[ways[1]] = so_far[ways[1]] + mapped(old[rows_of[2]], c_left)

                        @pl.when(right)
                        def _():
                            back = f_right + mapped(mine_ref[rows_of[2]], c_left)
                            b_left = theirs(near_ref, far_ref, cut)
                            f_new = f_left + mapped(b_left, back)
                            total_ref[...] = f_new
                            sent_ref[...] = f_new.astype(bf16)

                        @pl.when(~right)
                        def _():
                            c_new = c_right + mapped(mine_ref[rows_of[0]], c_left)
                            total_ref[...] = c_new
                            sent_ref[...] = c_new.astype(bf16)

                    return
                plan = refs[0]
                spread = mapped(plan[: (3 if level else 2) * layer], c_left)
                back = f_right + spread[ways[1]]
                c_new = c_right + spread[ways[0]]
                f_new = f_left + mapped(plan[rows_of[3 if level else 2]], back)
                if level:
                    so_far = refs[1]
                    more = mapped(plan[rows_of[4]], jnp.where(after, c_left, back))
                    z = so_far[ways[0]] + jnp.where(after, spread[rows_of[2]], 0.0)
                    u = so_far[ways[1]] + more
                else:
                    z = jnp.where(after, c_left, jnp.zeros_like(c_left))
                    u = jnp.where(after, jnp.zeros_like(back), back)
                reach_ref[ways[0]] = z
                reach_ref[ways[1]] = u
                total_ref[ways[0]] = c_new
                total_ref[ways[1]] = f_new
                sent_ref[ways[0]] = c_new.astype(bf16)
                sent_ref[ways[1]] = f_new.astype(bf16)

            size = (layer, width) if closing else pair
            if closing:
                args = (total, other, totals, near_x, far_x, members, reach)
            else:
                args = (total, other, plans[level]) + ((reach,) if level else ())
            total, sent, reach = call(
                step, [(size, f32), (size, bf16), (pair, f32)], args, 40 * layer * layer * width
            )
        return total, swapped(sent, "slab", 1 << final), reach

    blocks = (low - layer) // layer

    def fetch(green_ref, held_ref, sem, spots):
        copies = [
            pltpu.make_async_copy(green_ref.at[k, r], held_ref.at[k, i], sem.at[i, k])
            for i, r in enumerate(spots)
            for k in range(2)
        ]
        for copy in copies:
            copy.start()
        return copies

    def prepare(
        green_ref, inj_ref, panel_ref, start_ref, count_ref, strength_ref,
        mid_ref, acc_ref, weight_ref, sem,
    ):
        spots = [pl.ds((i + 1) * layer, layer) for i in range(blocks)]
        copies = fetch(green_ref, mid_ref, sem, spots)
        me = lax.axis_index("energy")
        row = lax.broadcasted_iota(jnp.int32, (span, width), 0)
        acc_ref[...] = inj_ref[...].astype(f32)
        for k in range(energies):
            s = me ^ k
            weight = jnp.where(row < count_ref[me, s] * rows, strength_ref[me, s], 0.0)
            if k:
                weight_ref[k - 1] = weight
            else:
                first = pl.multiple_of(start_ref[me, me] * rows, rows)
                part = pl.ds(first, span)
                acc_ref[part] = acc_ref[part] + panel_ref[part].astype(f32) * weight
        for copy in copies:
            copy.wait()

    mid, acc, weights = call(
        prepare,
        [
            ((2, blocks, layer, norb), bf16),
            ((norb, width), f32),
            ((energies - 1, span, width), f32),
        ],
        (far_green, injection[0, 0], panel, block_start, block_count, strength),
        0,
        {0: pltpu.HBM, 3: SMEM, 4: SMEM, 5: SMEM},
        [pltpu.SemaphoreType.DMA((blocks, 2))],
    )

    def load(start_ref, acc_ref, weight_ref, ends_ref, turn_ref, *refs):
        got, (source_ref, spun_ref, low_ref, sent_ref, sum_ref) = refs[:-5], refs[-5:]
        me = lax.axis_index("energy")
        sum_ref[...] = acc_ref[...]
        for k in range(1, energies):
            first = pl.multiple_of(start_ref[me, me ^ k] * rows, rows)
            part = pl.ds(first, span)
            sum_ref[part] = sum_ref[part] + got[k - 1][...].astype(f32) * weight_ref[k - 1]
        source = sum_ref[...].astype(bf16)
        spun = turned(source.astype(f32)).astype(bf16)
        source_ref[...] = source
        spun_ref[...] = spun
        direct = dot(ends_ref[0, 1], source) + dot(ends_ref[1, 1], spun)
        low_ref[...] = direct
        sent_ref[ways[1]] = dot(ends_ref[0, 0], source) + dot(ends_ref[1, 0], spun)
        sent_ref[ways[0]] = fine(turn_ref[...], direct)

    source, spun, direct_low, sent = call(
        load,
        [((norb, width), bf16)] * 2 + [((layer, width), f32), (pair, f32)],
        (block_start, acc, weights, ends, coup_t, *received),
        8 * layer * norb * width,
        {0: SMEM},
        [pltpu.VMEM((norb, width), f32)],
    )
    c_total, arrived, reach = scan(sent)

    def direct_step(mid_ref, source_ref, spun_ref, out_ref):
        for i in range(blocks):
            out_ref[i] = dot(mid_ref[0, i], source_ref[...]) + dot(mid_ref[1, i], spun_ref[...])

    (direct_mid,) = call(
        direct_step,
        [((blocks, layer, width), f32)],
        (mid, source, spun),
        4 * (low - layer) * norb * width,
    )

    def weights(
        mine, near_ref, far_ref, ny_ref, fy_ref, old, bounce_ref, hint_ref, ends_ref, mid_ref,
        coup_ref, wide_ref,
    ):
        after, right = place(final - 1), place(final)
        c = coup_ref[...]
        tail = slice(low, norb)

        def held_rows(i):
            if i == 0:
                return [ends_ref.at[k, 0] for k in range(2)]
            if i > blocks:
                return [ends_ref.at[k, 1] for k in range(2)]
            return [mid_ref.at[k, i - 1] for k in range(2)]

        def twice(wide):
            return wide, turned(wide.astype(f32)).astype(bf16)

        @pl.when(right)
        def _():
            a_left = jnp.where(after, theirs(near_ref, far_ref, 0), mine[rows_of[0]])
            p, spun_p = twice(member_before(after, old[rows_of[0]], a_left))
            r = member_turned(after, old[rows_of[1]], old[rows_of[2]], a_left, bounce_ref[...])
            s, spun_s = twice(dot(c, r).astype(bf16))
            for i in range(blocks + 2):
                real, imag = held_rows(i)
                wide_ref[i * layer : (i + 1) * layer] = (
                    dot(real[:, :layer], p)
                    + dot(imag[:, :layer], spun_p)
                    + dot(real[:, tail], s)
                    + dot(imag[:, tail], spun_s)
                ).astype(bf16)

        @pl.when(~right)
        def _():
            b_right = jnp.where(after, mine[rows_of[1]], theirs(ny_ref, fy_ref, 0))
            q = member_behind(after, old[rows_of[1]], b_right)
            s, spun_s = twice(dot(c, q).astype(bf16))
            for i in range(blocks + 2):
                real, imag = held_rows(i)
                wide_ref[i * layer : (i + 1) * layer] = (
                    dot(real[:, tail], s) + dot(imag[:, tail], spun_s)
                ).astype(bf16)

    (last_map,) = call(
        weights,
        [((norb, 2 * layer), bf16)],
        (totals, near_x, far_x, near_y, far_y, members, bounced, reach, ends, mid, coup),
        32 * norb * layer * layer,
    )

    def based(reach_ref, ends_ref, mid_ref, coup_ref, sent_ref, low_ref, direct_ref, base_ref):
        incoming = reach_ref[ways[0]].astype(bf16)
        spun_z = turned(incoming.astype(f32)).astype(bf16)
        outgoing = fine(coup_ref[...], reach_ref[ways[1]]).astype(bf16)
        spun_u = turned(outgoing.astype(f32)).astype(bf16)
        tail = slice(low, norb)
        for i in range(blocks + 2):
            if i == 0:
                direct, held = sent_ref[ways[1]], [ends_ref.at[k, 0] for k in range(2)]
            elif i > blocks:
                direct, held = low_ref[...], [ends_ref.at[k, 1] for k in range(2)]
            else:
                direct, held = direct_ref[i - 1], [mid_ref.at[k, i - 1] for k in range(2)]
            base_ref[i * layer : (i + 1) * layer] = (
                direct
                + dot(held[0][:, :layer], incoming)
                + dot(held[1][:, :layer], spun_z)
                + dot(held[0][:, tail], outgoing)
                + dot(held[1][:, tail], spun_u)
            )

    (base,) = call(
        based,
        [((norb, width), f32)],
        (reach, ends, mid, coup, sent, direct_low, direct_mid),
        16 * norb * layer * width,
    )

    def rebound(c_ref, near_ref, far_ref, out_ref):
        @pl.when(place(final))
        def _():
            out_ref[...] = jnp.zeros(out_ref.shape, f32)

        @pl.when(~place(final))
        def _():
            out_ref[...] = mapped(theirs(near_ref, far_ref, 0), c_ref[...])

    (bounce,) = call(
        rebound, [((layer, width), f32)], (c_total, e_near, e_far), 8 * layer * layer * width
    )

    def finish(other_ref, bounce_ref, base_ref, wide_ref, out_ref, kept, sem):
        last = other_ref[...].astype(f32) + bounce_ref[...]
        copies = []
        v, spun = last.astype(bf16), turned(last).astype(bf16)
        for i in range(norb // layer):
            part = pl.ds(i * layer, layer)
            kept[part] = (
                base_ref[part] + dot(wide_ref[part, :layer], v) + dot(wide_ref[part, layer:], spun)
            ).astype(bf16)
            copy = pltpu.make_async_copy(kept.at[part], out_ref.at[part], sem.at[i])
            copy.start()
            copies.append(copy)
        for copy in copies:
            copy.wait()

    (out,) = call(
        finish,
        [((norb, width), bf16)],
        (arrived, bounce, base, last_map),
        8 * norb * layer * width,
        scratch=[pltpu.VMEM((norb, width), bf16), pltpu.SemaphoreType.DMA((norb // layer,))],
        out_space=pltpu.HBM,
    )
    return out[None, None]


def solution(mesh):
    in_specs = (
        P("energy", "slab", None, None, None),
        P("energy", "slab", None, None),
        P("energy", "slab", None, None),
        P("slab", None, None),
        P(),
        P(),
        P(),
    )
    out_specs = P("energy", "slab", None, None)
    return jax.shard_map(body, mesh=mesh, in_specs=in_specs, out_specs=out_specs, check_vma=False)
```

```python
import math

import jax
import jax.numpy as jnp
from jax import lax
from jax.experimental import pallas as pl
from jax.experimental.pallas import tpu as pltpu
from jax.sharding import PartitionSpec as P


NBLK = 16
CAP = 4
VMEM_BYTES = 67043328
bf16 = jnp.bfloat16
f32 = jnp.float32
VMEM = pltpu.VMEM


def swapped(block, axis, mask):
    count = lax.axis_size(axis)
    return lax.ppermute(block, axis, [(i, i ^ mask) for i in range(count)])


def dot(a, b):
    return jnp.dot(a, b, preferred_element_type=f32)


def turned(v):
    half = v.shape[1] // 2
    if half % 128 == 0:
        return jnp.concatenate([-v[:, half:], v[:, :half]], axis=1)
    lane = lax.broadcasted_iota(jnp.int32, v.shape, 1)
    moved = pltpu.roll(v, half, 1)
    return jnp.where(lane < half, -moved, moved)


def applied(real, imag, v):
    v = v.astype(f32)
    return dot(real, v.astype(bf16)) + dot(imag, turned(v).astype(bf16))


def mapped(wide, v):
    side = wide.shape[1] // 2
    return applied(wide[:, :side], wide[:, side:], v)


def fine(real, v):
    high = v.astype(bf16)
    return dot(real, high) + dot(real, (v - high.astype(f32)).astype(bf16))


def member_before(after, p, a_left):
    return jnp.where(after, mapped(p, a_left).astype(bf16), p)


def member_behind(after, q, b_right):
    return jnp.where(after, q, mapped(q, b_right).astype(bf16))


def member_turned(after, q, r, a_left, bounce):
    more = mapped(jnp.where(after, r, q), jnp.where(after, a_left, bounce))
    return jnp.where(after, more, more + r.astype(f32)).astype(bf16)


def place(k):
    return ((lax.axis_index("slab") >> k) & 1) == 1


def call(kernel, outs, args, flops, spaces=None, scratch=(), out_space=VMEM, spare=None):
    spaces = spaces or {}
    specs = [pl.BlockSpec(memory_space=spaces.get(i, VMEM)) for i in range(len(args))]
    moved = sum(a.size * a.dtype.itemsize for a in args)
    kept = sum(math.prod(s) * jnp.dtype(t).itemsize for s, t in outs)
    kept += sum(a.size * a.dtype.itemsize for i, a in enumerate(args) if i not in spaces)
    limit = kept + (4 << 20) if spare is None else VMEM_BYTES - spare
    shapes = [jax.ShapeDtypeStruct(s, t) for s, t in outs]
    return pl.pallas_call(
        kernel,
        out_shape=shapes,
        in_specs=specs,
        out_specs=[pl.BlockSpec(memory_space=out_space)] * len(shapes),
        scratch_shapes=list(scratch),
        compiler_params=pltpu.CompilerParams(vmem_limit_bytes=limit),
        cost_estimate=pl.CostEstimate(
            flops=flops, bytes_accessed=moved, transcendentals=0
        ),
    )(*args)


def in_hbm(array):
    return pltpu.with_memory_space_constraint(array, pltpu.HBM)


def body(pivots, injection, previous, coupling, strength, block_start, block_count):
    green = pivots[0, 0]
    norb = green.shape[1]
    layer = coupling.shape[1]
    width = injection.shape[3]
    rows = norb // NBLK
    span = rows * CAP
    far_green = in_hbm(green)
    coup = coupling[0]
    far_coup = in_hbm(coup)
    panel = previous[0, 0]
    energies = lax.axis_size("energy")
    slabs = lax.axis_size("slab")
    levels = slabs.bit_length() - 1
    low = norb - layer
    SMEM = pltpu.SMEM

    rows_of = [slice(k * layer, (k + 1) * layer) for k in range(6)]
    triple, one_map = (3 * layer, 2 * layer), (layer, 2 * layer)

    def own_maps(green_ref, coup_ref, start_ref, panel_ref, *refs):
        maps_ref, turn_ref, ends_ref = refs[:3]
        pieces = refs[3 : energies + 2]
        near, whole, table, sem, sem_c, sem_t, sem_p = refs[energies + 2 :]
        ask = pltpu.make_async_copy(start_ref, table, sem_t)
        panel_copy = pltpu.make_async_copy(panel_ref, whole, sem_p)
        first = pltpu.make_async_copy(coup_ref, near, sem_c)
        copies = [
            [
                pltpu.make_async_copy(
                    green_ref.at[k, pl.ds(i * low, layer)], ends_ref.at[k, i], sem.at[i, k]
                )
                for k in range(2)
            ]
            for i in range(2)
        ]
        ask.start()
        first.start()
        panel_copy.start()
        for pair in copies:
            for copy in pair:
                copy.start()
        me = lax.axis_index("energy")
        first.wait()
        c = near[...]
        panel_copy.wait()
        ask.wait()
        for k in range(energies - 1):
            begin = pl.multiple_of(table[me ^ (k + 1), me] * rows, rows)
            pieces[k][...] = whole[pl.ds(begin, span)]
        ct = c.astype(f32).T.astype(bf16)
        turn_ref[...] = ct
        for pair in copies:
            for copy in pair:
                copy.wait()
        for k in range(2):
            maps_ref[rows_of[1], rows_of[k]] = dot(ends_ref[k, 0, :, low:], c).astype(bf16)
            maps_ref[rows_of[0], rows_of[k]] = dot(ct, ends_ref[k, 1, :, :layer]).astype(bf16)
            maps_ref[rows_of[2], rows_of[k]] = ends_ref[k, 0, :, :layer]

    maps, coup_t, ends, *pieces = call(
        own_maps,
        [(triple, bf16), ((layer, layer), bf16), ((2, 2, layer, norb), bf16)]
        + [((span, width), bf16)] * (energies - 1),
        (far_green, far_coup, in_hbm(block_start), in_hbm(panel)),
        8 * layer**3,
        {k: pltpu.HBM for k in range(4)},
        [
            pltpu.VMEM((layer, layer), bf16),
            pltpu.VMEM(panel.shape, bf16),
            pltpu.SMEM(block_start.shape, block_start.dtype),
            pltpu.SemaphoreType.DMA((2, 2)),
            pltpu.SemaphoreType.DMA,
            pltpu.SemaphoreType.DMA,
            pltpu.SemaphoreType.DMA,
        ],
    )
    received = [None] * (energies - 1)
    for mask in range(energies - 1, 0, -1):
        received[mask - 1] = swapped(pieces[mask - 1], "energy", mask)

    half = 3 * layer // 2
    final = levels - 1
    plans = []

    def sides(mine, theirs, after):
        own = [mine[rows_of[k]] for k in range(3)]
        its = [theirs[rows_of[k]] for k in range(3)]
        left = [jnp.where(after, b, a) for a, b in zip(own, its)]
        right = [jnp.where(after, a, b) for a, b in zip(own, its)]
        return left, right

    def joined(near_ref, far_ref):
        first, a, b = place(0), near_ref[...], far_ref[...]
        return jnp.concatenate([jnp.where(first, b, a), jnp.where(first, a, b)], axis=0)

    def reflected(left, right):
        bounce = mapped(right[2], left[0]).astype(bf16)
        return bounce, (left[2].astype(f32) + mapped(left[1], bounce)).astype(bf16)

    cut = layer // 2
    parts = [((2 * cut, 2 * layer), bf16), ((cut, 2 * layer), bf16)]
    direct_close = final == 2

    def pack(grown, x_ref, y_ref):
        later = place(final - 1)
        x_ref[:cut] = grown[0]
        x_ref[cut:] = jnp.where(later, grown[2], grown[1])
        y_ref[...] = jnp.where(later, grown[1], grown[2])

    def halved(block):
        return jnp.where(place(0), block[cut:], block[:cut])

    def group0(mine, near_ref, plan, *sends):
        def fill(left, right, begin):
            rows_in = [slice(k * layer + begin, k * layer + begin + cut) for k in range(3)]
            plan[rows_of[0]], plan[rows_of[1]] = right[rows_of[0]], right[rows_of[2]]
            plan[rows_of[2]] = left[rows_of[1]]
            bounce = mapped(right[rows_of[2]], left[rows_of[0]]).astype(bf16)
            if direct_close:
                b_rows = left[rows_in[1]]
                grown = (
                    mapped(right[rows_in[0]], left[rows_of[0]]).astype(bf16),
                    mapped(b_rows, right[rows_of[1]]).astype(bf16),
                    (left[rows_in[2]].astype(f32) + mapped(b_rows, bounce)).astype(bf16),
                )
                pack(grown, *sends)
                return
            whole = jnp.concatenate(
                [
                    mapped(right[rows_of[0]], left[rows_of[0]]).astype(bf16),
                    mapped(left[rows_of[1]], right[rows_of[1]]).astype(bf16),
                    (
                        left[rows_of[2]].astype(f32) + mapped(left[rows_of[1]], bounce)
                    ).astype(bf16),
                ],
                axis=0,
            )
            sends[0][...] = whole[half:] if begin else whole[:half]

        pl.when(place(0))(lambda: fill(near_ref, mine, cut))
        pl.when(~place(0))(lambda: fill(mine, near_ref, 0))

    def grow0(mine, near_ref, total, member):
        after = place(0)
        left, right = sides(mine, near_ref, after)
        bounce, e_total = reflected(left, right)
        total[rows_of[0]] = mapped(right[0], left[0]).astype(bf16)
        total[rows_of[1]] = mapped(left[1], right[1]).astype(bf16)
        total[rows_of[2]] = e_total
        row = lax.broadcasted_iota(jnp.int32, one_map, 0)
        col = lax.broadcasted_iota(jnp.int32, one_map, 1)
        unit = (row == col).astype(f32).astype(bf16)
        member[rows_of[0]] = jnp.where(after, left[0], unit)
        member[rows_of[1]] = jnp.where(after, unit, right[1])
        member[rows_of[2]] = jnp.where(after, jnp.zeros_like(bounce), bounce)

    near = swapped(maps, "slab", 1)
    sent_half = [((half, 2 * layer), bf16)]
    plan, *sends = call(
        group0, [(triple, bf16)] + (parts if direct_close else sent_half), (maps, near),
        32 * layer**3,
    )
    totals, members = call(grow0, [(triple, bf16)] * 2, (maps, near), 64 * layer**3)
    plans.append(plan)

    for level in range(1, final - 1):
        near = swapped(sends[0], "slab", 1 << level)
        far = swapped(near, "slab", 1)
        to_close = level == final - 2

        def group(
            mine, near_ref, far_ref, old, total, plan, member, *refs, level=level, to_close=to_close
        ):
            after = place(level)
            left, right = sides(mine, joined(near_ref, far_ref), after)
            p, q, r = (old[rows_of[k]] for k in range(3))
            plan_rows = (right[0], right[2], p, left[1], jnp.where(after, r, q))
            for k, part in enumerate(plan_rows):
                plan[rows_of[k]] = part
            bounce, e_total = reflected(left, right)
            member[rows_of[0]] = member_before(after, p, left[0])
            member[rows_of[1]] = member_behind(after, q, right[1])
            member[rows_of[2]] = member_turned(after, q, r, left[0], bounce)
            grown = (
                mapped(right[0], left[0]).astype(bf16),
                mapped(left[1], right[1]).astype(bf16),
                e_total,
            )
            whole = jnp.concatenate(grown, axis=0)
            total[...] = whole
            if to_close:
                pack([halved(g) for g in grown], *refs)
            else:
                refs[0][...] = jnp.where(place(0), whole[half:], whole[:half])

        totals, plan, members, *sends = call(
            group,
            [
                (triple, bf16),
                ((5 * layer, 2 * layer), bf16),
                (triple, bf16),
            ]
            + (parts if to_close else sent_half),
            (totals, near, far, members),
            64 * layer**3,
        )
        plans.append(plan)

    near_x = swapped(sends[0], "slab", 1 << (final - 1))
    near_y = swapped(sends[1], "slab", 1 << (final - 1))
    far_x = swapped(near_x, "slab", 1)
    far_y = swapped(near_y, "slab", 1)

    def theirs(near_ref, far_ref, begin):
        first, a, b = place(0), near_ref[begin : begin + cut], far_ref[begin : begin + cut]
        return jnp.concatenate([jnp.where(first, b, a), jnp.where(first, a, b)], axis=0)

    def reflect(mine, near_ref, far_ref, ny_ref, bounce_ref, send_ref):
        after, right = place(final - 1), place(final)

        @pl.when(right & after)
        def _():
            bounce = mapped(mine[rows_of[2]], theirs(near_ref, far_ref, 0)).astype(bf16)
            bounce_ref[...] = bounce
            send_ref[...] = (
                ny_ref[...].astype(f32) + mapped(near_ref[cut:], bounce)
            ).astype(bf16)

        @pl.when(right & ~after)
        def _():
            bounce = mapped(theirs(near_ref, far_ref, cut), mine[rows_of[0]]).astype(bf16)
            bounce_ref[...] = bounce
            send_ref[...] = (
                halved(mine[rows_of[2]]).astype(f32) + mapped(halved(mine[rows_of[1]]), bounce)
            ).astype(bf16)

        @pl.when(~right)
        def _():
            bounce_ref[...] = jnp.zeros(bounce_ref.shape, bf16)
            send_ref[...] = jnp.zeros(send_ref.shape, bf16)

    bounced, send = call(
        reflect,
        [(one_map, bf16), ((cut, 2 * layer), bf16)],
        (totals, near_x, far_x, near_y),
        24 * layer**3,
    )
    e_near = swapped(send, "slab", 1 << final)
    e_far = swapped(e_near, "slab", 1)

    ways = (slice(0, layer), slice(layer, 2 * layer))
    pair = (2 * layer, width)

    def scan(vector):
        total, sent, reach = vector, vector, None
        for level in range(final):
            other = swapped(sent, "slab", 1 << level)
            closing = level == final - 1

            def step(mine, other_ref, *refs, level=level, closing=closing):
                total_ref, sent_ref, reach_ref = refs[-3:]
                after = place(level)
                own = [mine[w] for w in ways]
                its = [other_ref[w].astype(f32) for w in ways]
                c_left, c_right = jnp.where(after, its[0], own[0]), jnp.where(after, own[0], its[0])
                f_left, f_right = jnp.where(after, its[1], own[1]), jnp.where(after, own[1], its[1])
                if closing:
                    mine_ref, near_ref, far_ref, old, so_far = refs[:5]
                    right = place(final)

                    @pl.when(~after)
                    def _():
                        e_right = theirs(near_ref, far_ref, cut)
                        back = f_right + mapped(e_right, c_left)
                        reach_ref[ways[0]] = so_far[ways[0]]
                        reach_ref[ways[1]] = so_far[ways[1]] + mapped(old[rows_of[1]], back)

                        @pl.when(right)
                        def _():
                            f_new = f_left + mapped(mine_ref[rows_of[1]], back)
                            total_ref[...] = f_new
                            sent_ref[...] = f_new.astype(bf16)

                        @pl.when(~right)
                        def _():
                            c_new = c_right + mapped(theirs(near_ref, far_ref, 0), c_left)
                            total_ref[...] = c_new
                            sent_ref[...] = c_new.astype(bf16)

                    @pl.when(after)
                    def _():
                        reach_ref[ways[0]] = so_far[ways[0]] + mapped(old[rows_of[0]], c_left)
                        reach_ref[ways[1]] = so_far[ways[1]] + mapped(old[rows_of[2]], c_left)

                        @pl.when(right)
                        def _():
                            back = f_right + mapped(mine_ref[rows_of[2]], c_left)
                            b_left = theirs(near_ref, far_ref, cut)
                            f_new = f_left + mapped(b_left, back)
                            total_ref[...] = f_new
                            sent_ref[...] = f_new.astype(bf16)

                        @pl.when(~right)
                        def _():
                            c_new = c_right + mapped(mine_ref[rows_of[0]], c_left)
                            total_ref[...] = c_new
                            sent_ref[...] = c_new.astype(bf16)

                    return
                plan = refs[0]
                spread = mapped(plan[: (3 if level else 2) * layer], c_left)
                back = f_right + spread[ways[1]]
                c_new = c_right + spread[ways[0]]
                f_new = f_left + mapped(plan[rows_of[3 if level else 2]], back)
                if level:
                    so_far = refs[1]
                    more = mapped(plan[rows_of[4]], jnp.where(after, c_left, back))
                    z = so_far[ways[0]] + jnp.where(after, spread[rows_of[2]], 0.0)
                    u = so_far[ways[1]] + more
                else:
                    z = jnp.where(after, c_left, jnp.zeros_like(c_left))
                    u = jnp.where(after, jnp.zeros_like(back), back)
                reach_ref[ways[0]] = z
                reach_ref[ways[1]] = u
                total_ref[ways[0]] = c_new
                total_ref[ways[1]] = f_new
                sent_ref[ways[0]] = c_new.astype(bf16)
                sent_ref[ways[1]] = f_new.astype(bf16)

            size = (layer, width) if closing else pair
            if closing:
                args = (total, other, totals, near_x, far_x, members, reach)
            else:
                args = (total, other, plans[level]) + ((reach,) if level else ())
            total, sent, reach = call(
                step, [(size, f32), (size, bf16), (pair, f32)], args, 40 * layer * layer * width
            )
        return total, swapped(sent, "slab", 1 << final), reach

    blocks = (low - layer) // layer

    def fetch(green_ref, held_ref, sem, spots):
        copies = [
            pltpu.make_async_copy(green_ref.at[k, r], held_ref.at[k, i], sem.at[i, k])
            for i, r in enumerate(spots)
            for k in range(2)
        ]
        for copy in copies:
            copy.start()
        return copies

    def prepare(
        green_ref, inj_ref, panel_ref, start_ref, count_ref, strength_ref,
        mid_ref, acc_ref, weight_ref, sem,
    ):
        spots = [pl.ds((i + 1) * layer, layer) for i in range(blocks)]
        copies = fetch(green_ref, mid_ref, sem, spots)
        me = lax.axis_index("energy")
        row = lax.broadcasted_iota(jnp.int32, (span, width), 0)
        acc_ref[...] = inj_ref[...].astype(f32)
        for k in range(energies):
            s = me ^ k
            weight = jnp.where(row < count_ref[me, s] * rows, strength_ref[me, s], 0.0)
            if k:
                weight_ref[k - 1] = weight
            else:
                first = pl.multiple_of(start_ref[me, me] * rows, rows)
                part = pl.ds(first, span)
                acc_ref[part] = acc_ref[part] + panel_ref[part].astype(f32) * weight
        for copy in copies:
            copy.wait()

    mid, acc, weights = call(
        prepare,
        [
            ((2, blocks, layer, norb), bf16),
            ((norb, width), f32),
            ((energies - 1, span, width), f32),
        ],
        (far_green, injection[0, 0], panel, block_start, block_count, strength),
        0,
        {0: pltpu.HBM, 3: SMEM, 4: SMEM, 5: SMEM},
        [pltpu.SemaphoreType.DMA((blocks, 2))],
    )

    def load(start_ref, acc_ref, weight_ref, ends_ref, turn_ref, *refs):
        got, (source_ref, spun_ref, low_ref, sent_ref, sum_ref) = refs[:-5], refs[-5:]
        me = lax.axis_index("energy")
        sum_ref[...] = acc_ref[...]
        for k in range(1, energies):
            first = pl.multiple_of(start_ref[me, me ^ k] * rows, rows)
            part = pl.ds(first, span)
            sum_ref[part] = sum_ref[part] + got[k - 1][...].astype(f32) * weight_ref[k - 1]
        source = sum_ref[...].astype(bf16)
        spun = turned(source.astype(f32)).astype(bf16)
        source_ref[...] = source
        spun_ref[...] = spun
        direct = dot(ends_ref[0, 1], source) + dot(ends_ref[1, 1], spun)
        low_ref[...] = direct
        sent_ref[ways[1]] = dot(ends_ref[0, 0], source) + dot(ends_ref[1, 0], spun)
        sent_ref[ways[0]] = fine(turn_ref[...], direct)

    source, spun, direct_low, sent = call(
        load,
        [((norb, width), bf16)] * 2 + [((layer, width), f32), (pair, f32)],
        (block_start, acc, weights, ends, coup_t, *received),
        8 * layer * norb * width,
        {0: SMEM},
        [pltpu.VMEM((norb, width), f32)],
    )
    c_total, arrived, reach = scan(sent)

    def direct_step(mid_ref, source_ref, spun_ref, out_ref):
        for i in range(blocks):
            out_ref[i] = dot(mid_ref[0, i], source_ref[...]) + dot(mid_ref[1, i], spun_ref[...])

    (direct_mid,) = call(
        direct_step,
        [((blocks, layer, width), f32)],
        (mid, source, spun),
        4 * (low - layer) * norb * width,
    )

    def weights(
        mine, near_ref, far_ref, ny_ref, fy_ref, old, bounce_ref, hint_ref, ends_ref, mid_ref,
        coup_ref, wide_ref,
    ):
        after, right = place(final - 1), place(final)
        c = coup_ref[...]
        tail = slice(low, norb)

        def held_rows(i):
            if i == 0:
                return [ends_ref.at[k, 0] for k in range(2)]
            if i > blocks:
                return [ends_ref.at[k, 1] for k in range(2)]
            return [mid_ref.at[k, i - 1] for k in range(2)]

        def twice(wide):
            return wide, turned(wide.astype(f32)).astype(bf16)

        @pl.when(right)
        def _():
            a_left = jnp.where(after, theirs(near_ref, far_ref, 0), mine[rows_of[0]])
            p, spun_p = twice(member_before(after, old[rows_of[0]], a_left))
            r = member_turned(after, old[rows_of[1]], old[rows_of[2]], a_left, bounce_ref[...])
            s, spun_s = twice(dot(c, r).astype(bf16))
            for i in range(blocks + 2):
                real, imag = held_rows(i)
                wide_ref[i * layer : (i + 1) * layer] = (
                    dot(real[:, :layer], p)
                    + dot(imag[:, :layer], spun_p)
                    + dot(real[:, tail], s)
                    + dot(imag[:, tail], spun_s)
                ).astype(bf16)

        @pl.when(~right)
        def _():
            b_right = jnp.where(after, mine[rows_of[1]], theirs(ny_ref, fy_ref, 0))
            q = member_behind(after, old[rows_of[1]], b_right)
            s, spun_s = twice(dot(c, q).astype(bf16))
            for i in range(blocks + 2):
                real, imag = held_rows(i)
                wide_ref[i * layer : (i + 1) * layer] = (
                    dot(real[:, tail], s) + dot(imag[:, tail], spun_s)
                ).astype(bf16)

    (last_map,) = call(
        weights,
        [((norb, 2 * layer), bf16)],
        (totals, near_x, far_x, near_y, far_y, members, bounced, reach, ends, mid, coup),
        32 * norb * layer * layer,
    )

    def based(reach_ref, ends_ref, mid_ref, coup_ref, sent_ref, low_ref, direct_ref, base_ref):
        incoming = reach_ref[ways[0]].astype(bf16)
        spun_z = turned(incoming.astype(f32)).astype(bf16)
        outgoing = fine(coup_ref[...], reach_ref[ways[1]]).astype(bf16)
        spun_u = turned(outgoing.astype(f32)).astype(bf16)
        tail = slice(low, norb)
        for i in range(blocks + 2):
            if i == 0:
                direct, held = sent_ref[ways[1]], [ends_ref.at[k, 0] for k in range(2)]
            elif i > blocks:
                direct, held = low_ref[...], [ends_ref.at[k, 1] for k in range(2)]
            else:
                direct, held = direct_ref[i - 1], [mid_ref.at[k, i - 1] for k in range(2)]
            base_ref[i * layer : (i + 1) * layer] = (
                direct
                + dot(held[0][:, :layer], incoming)
                + dot(held[1][:, :layer], spun_z)
                + dot(held[0][:, tail], outgoing)
                + dot(held[1][:, tail], spun_u)
            )

    (base,) = call(
        based,
        [((norb, width), f32)],
        (reach, ends, mid, coup, sent, direct_low, direct_mid),
        16 * norb * layer * width,
    )

    def rebound(c_ref, near_ref, far_ref, out_ref):
        @pl.when(place(final))
        def _():
            out_ref[...] = jnp.zeros(out_ref.shape, f32)

        @pl.when(~place(final))
        def _():
            out_ref[...] = mapped(theirs(near_ref, far_ref, 0), c_ref[...])

    (bounce,) = call(
        rebound, [((layer, width), f32)], (c_total, e_near, e_far), 8 * layer * layer * width
    )

    def finish(other_ref, bounce_ref, base_ref, wide_ref, out_ref, kept, sem):
        last = other_ref[...].astype(f32) + bounce_ref[...]
        copies = []
        v, spun = last.astype(bf16), turned(last).astype(bf16)
        for i in range(norb // cut):
            part = pl.ds(i * cut, cut)
            kept[part] = (
                base_ref[part] + dot(wide_ref[part, :layer], v) + dot(wide_ref[part, layer:], spun)
            ).astype(bf16)
            copy = pltpu.make_async_copy(kept.at[part], out_ref.at[part], sem.at[i])
            copy.start()
            copies.append(copy)
        for copy in copies:
            copy.wait()

    (out,) = call(
        finish,
        [((norb, width), bf16)],
        (arrived, bounce, base, last_map),
        8 * norb * layer * width,
        scratch=[pltpu.VMEM((norb, width), bf16), pltpu.SemaphoreType.DMA((norb // cut,))],
        out_space=pltpu.HBM,
    )
    return out[None, None]


def solution(mesh):
    in_specs = (
        P("energy", "slab", None, None, None),
        P("energy", "slab", None, None),
        P("energy", "slab", None, None),
        P("slab", None, None),
        P(),
        P(),
        P(),
    )
    out_specs = P("energy", "slab", None, None)
    return jax.shard_map(body, mesh=mesh, in_specs=in_specs, out_specs=out_specs, check_vma=False)
```
